512 devices in a mesh: blk: 16 (over y_hi, x, core), dom: 32 (over y_lo, z).
Axes of the slice: x: 4, y: 4 (y_hi: 2, y_lo: 2; y = y_hi * 2 + y_lo), z: 16, core: 2. Of those that a mesh axis runs over, the one named last changes fastest.
Arguments:
- nodes: bfloat16 [65536, 512], P(('blk', 'dom')), may hold values from -6 to 6
- experts_list: int32 [512, 4], P(('blk', 'dom')), may hold values from 0 to 15, all different within a row
- w_query: bfloat16 [512, 512], replicated
- w_key: bfloat16 [512, 512], replicated
- w_value: bfloat16 [512, 512], replicated, may hold values from -0.25 to 0.25
- w_out: bfloat16 [512, 512], replicated, may hold values from -0.25 to 0.25
- w_up: bfloat16 [512, 1024], replicated, may hold values from -0.25 to 0.25
- w_down: bfloat16 [1024, 512], replicated, may hold values from -0.1875 to 0.1875
- cotangent: bfloat16 [65536, 512], P(('blk', 'dom')), may hold values from -6 to 6
Outputs:
- layer_out: bfloat16 [65536, 512], P(('blk', 'dom'))
- grad_nodes: bfloat16 [65536, 512], P(('blk', 'dom'))
The draws below stay inside these ranges and needn't reach their ends.
Inputs may be any that keep to these rules, and one draw needn't show every extreme that they name: `experts_list`: row g names 4 different values; value c stands for the block held at blk index c and the same dom index as block g. Every value is named by some row.
All inputs are finite; a program needn't handle non-finite values.
Results may differ from the reference program's by a relative error of at most 0.0057.
Values may be sent and summed in bfloat16 or wider, within the bound.
A program may use at most 128 MiB of HBM per device.

```python
import jax
import jax.numpy as jnp
from jax import lax

D = 512
H = 8
HEAD = 64
FF = 1024
BLOCK = 128
EXP = 4
NODES = 65536
N_BLK = 16
N_DOM = 32
DEVICES = 512


def projection_pair(key):
    first = jax.random.normal(jax.random.fold_in(key, 11), (D, D), jnp.float32) * D ** (-0.5)
    second = jax.random.normal(jax.random.fold_in(key, 12), (D, D), jnp.float32) * D ** (-0.5)
    return (first, second)


def draw_w_query(key, part):
    first, second = projection_pair(key)
    return first.astype(jnp.bfloat16)


def draw_w_key(key, part):
    first, second = projection_pair(key)
    result = second
    return result.astype(jnp.bfloat16)


def steps_of(stream_key, shape, split, smallest, high):
    def one(position, parts):
        heights = jax.random.uniform(jax.random.fold_in(jax.random.fold_in(stream_key, 6), position), (parts,), jnp.float32, smallest / len(split), high / len(split))
        return jnp.repeat(jnp.exp(heights), shape[position] // parts).reshape((-1,) + (1,) * (len(shape) - position - 1))

    gain = one(*split[0])
    for cut in split[1:]:
        gain = gain * one(*cut)
    return gain


def different_ones(stream_key, rows, count, top, lift):
    ranking = jax.random.permutation(jax.random.fold_in(stream_key, 1), count)
    pull = ranking
    for power in range(3):
        pull = pull * pull // count
    pull = pull * lift // count
    tickets = jax.random.randint(jax.random.fold_in(stream_key, 2), (rows, count), 0, 4096) + pull
    sure = jax.random.permutation(jax.random.fold_in(stream_key, 3), rows)[jnp.arange(count) % rows]
    tickets = jnp.where(jnp.arange(rows)[:, None] == sure[None, :], 1 << 14, tickets)
    merit = tickets * count + jnp.arange(count)
    return lax.top_k(merit.astype(jnp.int32), top)[1].astype(jnp.int32)


def centred(stream_key, dims, scale, limit, cuts=(), held_as=jnp.bfloat16):
    values = jax.random.normal(stream_key, dims, jnp.float32) * scale
    if len(cuts) > 0:
        values = steps_of(stream_key, dims, cuts, -0.22, 0.18) * values
    return jnp.clip(values, min=-limit, max=limit).astype(held_as)


def setup_inputs(seed: int = 0) -> dict:
    key_of = jax.random.split(jax.random.key(seed), 10)
    nodes = centred(key_of[0], (NODES, D), 1.0, 6.0, ((0, 512),))
    experts_list = different_ones(key_of[1], DEVICES, N_BLK, EXP, 4096)
    w_query = draw_w_query(jax.random.fold_in(key_of[9], 71), 0)
    w_key = draw_w_key(jax.random.fold_in(key_of[9], 71), 0)
    w_value = centred(key_of[4], (D, D), D ** -0.5, 0.25)
    w_out = centred(key_of[5], (D, D), D ** -0.5, 0.25)
    w_up = centred(key_of[6], (D, FF), D ** -0.5, 0.25)
    w_down = centred(key_of[7], (FF, D), FF ** -0.5, 0.1875)
    cotangent = centred(key_of[8], (NODES, D), 1.0, 6.0, ((0, 512),))
    return {"nodes": nodes, "experts_list": experts_list, "w_query": w_query, "w_key": w_key, "w_value": w_value, "w_out": w_out, "w_up": w_up, "w_down": w_down, "cotangent": cotangent}


EPS = 1e-05
NEG = -1e+30

def normalize(values):
    mean_v = lax.optimization_barrier(jnp.mean(values, axis=-1, keepdims=True))
    centered = values - mean_v
    inv_std = lax.rsqrt(lax.optimization_barrier(jnp.mean(centered * centered, axis=-1, keepdims=True)) + EPS)
    return (centered * inv_std, inv_std)

def normalize_back(values, upstream):
    unit, inv_std = normalize(values)
    return inv_std * (upstream - lax.optimization_barrier(jnp.mean(upstream, axis=-1, keepdims=True)) - unit * lax.optimization_barrier(jnp.mean(upstream * unit, axis=-1, keepdims=True)))

def heads_of(rows):
    return rows.reshape(rows.shape[0], H, HEAD).astype(jnp.float32)

def rounded(values):
    return lax.optimization_barrier(values.astype(jnp.bfloat16)).astype(jnp.float32)

def attend(queries, keyvals):
    qh = heads_of(queries)
    kh = heads_of(keyvals[:, :D])
    vh = heads_of(keyvals[:, D:])
    scores = jnp.einsum('qhd,khd->hqk', qh, kh) * HEAD ** (-0.5)
    top = lax.optimization_barrier(jnp.max(scores, axis=-1, keepdims=True))
    weights = jnp.exp(scores - top)
    total = lax.optimization_barrier(jnp.sum(weights, axis=-1, keepdims=True))
    mixed = jnp.einsum('hqk,khd->qhd', rounded(weights), vh)
    mixed = mixed / jnp.transpose(total, (1, 0, 2))
    lse = (top + jnp.log(total))[..., 0]
    return (mixed.reshape(queries.shape[0], D).astype(jnp.bfloat16), lse)

def attend_back(queries, keyvals, grad_out, lse, delta):
    qh = heads_of(queries)
    kh = heads_of(keyvals[:, :D])
    vh = heads_of(keyvals[:, D:])
    gh = heads_of(grad_out)
    scores = jnp.einsum('qhd,khd->hqk', qh, kh) * HEAD ** (-0.5)
    probs = jnp.exp(scores - lse[..., None])
    grad_v = jnp.einsum('hqk,qhd->khd', rounded(probs), gh)
    dprob = jnp.einsum('qhd,khd->hqk', gh, vh)
    dscore = rounded(probs * (dprob - delta[..., None]) * HEAD ** (-0.5))
    grad_q = jnp.einsum('hqk,khd->qhd', dscore, kh)
    grad_k = jnp.einsum('hqk,qhd->khd', dscore, qh)
    count = keyvals.shape[0]
    return (grad_q.reshape(queries.shape[0], D), jnp.concatenate([grad_k.reshape(count, D), grad_v.reshape(count, D)], 1))

def reference(nodes, experts_list, w_query, w_key, w_value, w_out, w_up, w_down, cotangent):
    f32 = jnp.float32
    bf16 = jnp.bfloat16
    x_full = nodes.astype(f32)
    unit, _ = normalize(x_full)
    normed = unit.astype(bf16)
    queries = jnp.dot(normed, w_query, preferred_element_type=f32).astype(bf16)
    keys = jnp.dot(normed, w_key, preferred_element_type=f32).astype(bf16)
    values = jnp.dot(normed, w_value, preferred_element_type=f32).astype(bf16)
    keyvals = jnp.concatenate([keys, values], 1).reshape(N_BLK, N_DOM, BLOCK, 2 * D)
    before = jnp.roll(keyvals, 1, axis=1)
    after = jnp.roll(keyvals, -1, axis=1)
    qblocks = queries.reshape(DEVICES, BLOCK, D)

    def gather_keys(index):
        brow = index // N_DOM
        dcol = index % N_DOM
        local = jnp.concatenate([before[brow, dcol], keyvals[brow, dcol], after[brow, dcol]], 0)
        far = keyvals[experts_list[index], dcol].reshape(EXP * BLOCK, 2 * D)
        return jnp.concatenate([local, far], 0)

    def forward_block(index):
        return attend(qblocks[index], gather_keys(index))
    order = jnp.arange(DEVICES, dtype=jnp.int32)
    mixed, lse = lax.map(forward_block, order)
    mixed_rows = mixed.reshape(NODES, D)
    resid = x_full + jnp.dot(mixed_rows, w_out, preferred_element_type=f32)
    unit2, _ = normalize(resid)
    normed2 = unit2.astype(bf16)
    pre = jnp.dot(normed2, w_up, preferred_element_type=f32)
    act, gelu_back = jax.vjp(jax.nn.gelu, pre)
    layer_out = (resid + jnp.dot(act.astype(bf16), w_down, preferred_element_type=f32)).astype(bf16)
    grad_act = jnp.dot(cotangent, w_down.T, preferred_element_type=f32)
    grad_pre = gelu_back(grad_act)[0].astype(bf16)
    grad_norm2 = jnp.dot(grad_pre, w_up.T, preferred_element_type=f32)
    grad_resid = cotangent.astype(f32) + normalize_back(resid, grad_norm2)
    grad_mixed = jnp.dot(grad_resid.astype(bf16), w_out.T, preferred_element_type=f32).astype(bf16)
    gblocks = grad_mixed.reshape(DEVICES, BLOCK, D)
    delta = lax.optimization_barrier(jnp.sum(grad_mixed.reshape(DEVICES, BLOCK, H, HEAD).astype(f32) * mixed.reshape(DEVICES, BLOCK, H, HEAD).astype(f32), axis=-1))
    delta = jnp.transpose(delta, (0, 2, 1))

    def back_step(sums, index):
        brow = index // N_DOM
        dcol = index % N_DOM
        grad_q, grad_kv = attend_back(qblocks[index], gather_keys(index), gblocks[index], lse[index], delta[index])
        sums = sums.at[brow, (dcol - 1) % N_DOM].add(grad_kv[:BLOCK])
        sums = sums.at[brow, dcol].add(grad_kv[BLOCK:2 * BLOCK])
        sums = sums.at[brow, (dcol + 1) % N_DOM].add(grad_kv[2 * BLOCK:3 * BLOCK])
        sums = sums.at[experts_list[index], dcol].add(grad_kv[3 * BLOCK:].reshape(EXP, BLOCK, 2 * D))
        return (sums, grad_q)
    sums, grad_q_all = lax.scan(back_step, jnp.zeros((N_BLK, N_DOM, BLOCK, 2 * D), f32), order)
    grad_kv = sums.reshape(NODES, 2 * D)
    grad_in = jnp.dot(grad_q_all.reshape(NODES, D).astype(bf16), w_query.T, preferred_element_type=f32) + jnp.dot(grad_kv[:, :D].astype(bf16), w_key.T, preferred_element_type=f32) + jnp.dot(grad_kv[:, D:].astype(bf16), w_value.T, preferred_element_type=f32)
    grad_nodes = (grad_resid + normalize_back(x_full, grad_in)).astype(bf16)
    return (layer_out, grad_nodes)
```

```python
import functools

import jax
import jax.numpy as jnp
from jax import lax
from jax.experimental import pallas as pl
from jax.experimental.pallas import tpu as pltpu
from jax.sharding import PartitionSpec as P

EPS = 1e-05
MESH = pl.DeviceIdType.MESH
D = 512
FF = 1024
ROWS = 128
HALF = 64
DHALF = 256
PAIRS = 4
F32 = jnp.float32
BF16 = jnp.bfloat16


def normalize(values):
    mean_v = jnp.mean(values, axis=-1, keepdims=True)
    centered = values - mean_v
    inv_std = lax.rsqrt(jnp.mean(centered * centered, axis=-1, keepdims=True) + EPS)
    return (centered * inv_std, inv_std)


def normalize_back(unit, inv_std, upstream):
    return inv_std * (
        upstream
        - jnp.mean(upstream, axis=-1, keepdims=True)
        - unit * jnp.mean(upstream * unit, axis=-1, keepdims=True)
    )


def dot(a, b):
    return jnp.dot(a, b, preferred_element_type=F32)


def dot_t(a, b):
    return lax.dot_general(a, b, (((1,), (1,)), ((), ())), preferred_element_type=F32)


def head_stack(tile):
    low = lax.broadcasted_iota(jnp.int32, tile.shape, 1) < 64
    zero = jnp.zeros_like(tile)
    return jnp.concatenate([jnp.where(low, tile, zero), jnp.where(low, zero, tile)], 0)


def head_join(stacked):
    low = lax.broadcasted_iota(jnp.int32, (ROWS, 128), 1) < 64
    return jnp.where(low, stacked[:ROWS], stacked[ROWS:])


def kernel(
    listed,
    nodes_hbm,
    list_hbm,
    wq_hbm,
    wk_hbm,
    wv_hbm,
    wo_hbm,
    wu_hbm,
    wd_hbm,
    cot_hbm,
    out_hbm,
    gout_hbm,
    xv,
    cotv,
    wq,
    wkv,
    wo,
    wu,
    wd,
    gath,
    halo,
    kv,
    q2,
    q2t,
    g2,
    g2t,
    wexp,
    mstat,
    lstat,
    oacc,
    fstat,
    mixv,
    delt,
    dq,
    dt,
    part,
    psib,
    lsib,
    hsend,
    hrecv,
    xo,
    yl,
    yr,
    sbuf,
    tbuf,
    ybuf,
    outv,
    goutv,
    lsem,
    gsend,
    grecv,
    rsend,
    rrecv,
):
    blk = lax.axis_index("blk")
    dom = lax.axis_index("dom")
    ndom = lax.axis_size("dom")
    core = blk % 2
    x = (blk // 2) % 4
    h = blk // 8

    def at(xx, hh, cc):
        return hh * 8 + (xx % 4) * 2 + cc

    right = {"blk": at(x + 1, h, core), "dom": dom}
    left = {"blk": at(x + 3, h, core), "dom": dom}
    across = {"blk": at(x, 1 - h, core), "dom": dom}
    twin = {"blk": at(x, h, 1 - core), "dom": dom}
    up = {"blk": blk, "dom": (dom + 1) % ndom}
    down = {"blk": blk, "dom": (dom + ndom - 1) % ndom}

    loads = []

    def load(src, dst):
        copy = pltpu.make_async_copy(src, dst, lsem.at[len(loads)])
        copy.start()
        loads.append(copy)
        return copy

    ld_x = load(nodes_hbm, xv)
    ld_wk = load(wk_hbm, wkv.at[:, pl.ds(0, D)])
    ld_wv = load(wv_hbm, wkv.at[:, pl.ds(D, D)])
    ld_wq = load(wq_hbm, wq)
    ld_wo = load(wo_hbm, wo)
    ld_wu = load(wu_hbm, wu)
    ld_wd = load(wd_hbm, wd)
    ld_cot = load(cot_hbm, cotv)

    barrier = pltpu.get_barrier_semaphore()
    for peer in (right, left, across, twin, up, down):
        pl.semaphore_signal(barrier, inc=1, device_id=peer, device_id_type=MESH)
    pl.semaphore_wait(barrier, 6)

    sends = []

    def push(src, dst, ssems, rsems, slot, peer):
        copy = pltpu.make_async_remote_copy(
            src_ref=src,
            dst_ref=dst,
            send_sem=ssems.at[slot],
            recv_sem=rsems.at[slot],
            device_id=peer,
            device_id_type=MESH,
        )
        copy.start()
        sends.append(copy)
        return copy

    top = pl.ds(0, HALF)
    bottom = pl.ds(HALF, HALF)
    halves = (top, bottom)

    def block(xx, rr):
        return at(xx, rr, core)

    rows_of = (h, 1 - h)

    own = block(x, h)
    c_r = {}
    c_l = {}
    c_r[0, 0] = push(nodes_hbm.at[top], gath.at[own, top], gsend, grecv, 0, right)
    c_l[0, 1] = push(nodes_hbm.at[bottom], gath.at[own, bottom], gsend, grecv, 5, left)
    c_y = [None, None]
    c_y[0] = push(nodes_hbm.at[top], gath.at[own, top], gsend, grecv, 12, across)
    c_y[1] = push(nodes_hbm.at[bottom], gath.at[own, bottom], gsend, grecv, 13, across)
    c_r[0, 1] = push(nodes_hbm.at[bottom], gath.at[own, bottom], gsend, grecv, 1, right)
    c_l[0, 0] = push(nodes_hbm.at[top], gath.at[own, top], gsend, grecv, 4, left)
    c_up = push(nodes_hbm, halo.at[0], gsend, grecv, 14, up)
    c_dn = push(nodes_hbm, halo.at[1], gsend, grecv, 15, down)
    c_list = push(list_hbm, lsib, gsend, grecv, 24, twin)
    c_tw = []
    c_tw.append(push(nodes_hbm, gath.at[own], gsend, grecv, 16, twin))

    ld_x.wait()
    own_copy = pltpu.make_async_copy(xv, gath.at[own], lsem.at[len(loads)])
    own_copy.start()

    x_full = xv[...].astype(F32)
    unit, inv_std = normalize(x_full)
    normed = unit.astype(BF16)
    ld_wk.wait()
    ld_wv.wait()
    kv[pl.ds(ROWS, ROWS), :] = dot(normed, wkv[...]).astype(BF16)
    ld_wq.wait()
    queries = dot(normed, wq[...]).astype(BF16) * jnp.asarray(0.125, BF16)
    for hp in range(PAIRS):
        stacked = head_stack(queries[:, hp * 128 : (hp + 1) * 128])
        q2[hp] = stacked
        q2t[hp] = jnp.transpose(stacked)

    fwd_r = [None, None]
    fwd_l = [None, None]

    def forward(rr):
        row = rows_of[rr]
        c_r[rr, 0].wait_recv()
        from_left = block(x + 3, row)
        fwd_r[rr] = push(gath.at[from_left, top], gath.at[from_left, top], gsend, grecv, 8 + rr, right)
        c_l[rr, 1].wait_recv()
        from_right = block(x + 1, row)
        fwd_l[rr] = push(
            gath.at[from_right, bottom], gath.at[from_right, bottom], gsend, grecv, 10 + rr, left
        )

    def to_twin(slot, who):
        c_tw.append(push(gath.at[who], gath.at[who], gsend, grecv, slot, twin))

    forward(0)
    other = block(x, 1 - h)
    c_y[0].wait_recv()
    c_r[1, 0] = push(gath.at[other, top], gath.at[other, top], gsend, grecv, 2, right)
    c_l[1, 0] = push(gath.at[other, top], gath.at[other, top], gsend, grecv, 6, left)
    c_y[1].wait_recv()
    c_l[1, 1] = push(gath.at[other, bottom], gath.at[other, bottom], gsend, grecv, 7, left)
    c_r[1, 1] = push(gath.at[other, bottom], gath.at[other, bottom], gsend, grecv, 3, right)
    to_twin(17, other)
    c_r[0, 1].wait_recv()
    to_twin(18, block(x + 3, h))
    c_l[0, 0].wait_recv()
    to_twin(19, block(x + 1, h))

    def project(raw, row0):
        unit_o, _ = normalize(raw.astype(F32))
        kv[pl.ds(row0, ROWS), :] = dot(unit_o.astype(BF16), wkv[...]).astype(BF16)

    def attend(base, count, which):
        for hp in range(PAIRS):
            k = kv[base : base + count, hp * 128 : (hp + 1) * 128]
            v = kv[base : base + count, D + hp * 128 : D + (hp + 1) * 128]
            s = dot_t(q2[hp], k)
            m = jnp.max(s, axis=1, keepdims=True)
            w = jnp.exp(s - m)
            wexp[hp, :, base : base + count] = w
            total = jnp.sum(w, axis=1, keepdims=True)
            oacc[which, hp] = dot(w.astype(BF16), v)
            mstat[which, hp] = jnp.broadcast_to(m, (2 * ROWS, 128))
            lstat[which, hp] = jnp.broadcast_to(total, (2 * ROWS, 128))

    c_up.wait_recv()
    project(halo[0], 0)
    c_dn.wait_recv()
    project(halo[1], 2 * ROWS)
    forward(1)
    attend(0, 3 * ROWS, 0)

    for rr in (0, 1):
        if rr == 1:
            c_r[1, 1].wait_recv()
            to_twin(20, block(x + 3, 1 - h))
            c_l[1, 0].wait_recv()
            to_twin(21, block(x + 1, 1 - h))
        fwd_r[rr].wait_recv()
        fwd_l[rr].wait_recv()
        to_twin(22 + rr, block(x + 2, rows_of[rr]))
    for copy in c_tw:
        copy.wait_recv()
    c_list.wait_recv()
    own_copy.wait()

    for e in range(4):
        project(gath[listed[0, e]], (3 + e) * ROWS)
    attend(3 * ROWS, 4 * ROWS, 1)

    for hp in range(PAIRS):
        m0, m1 = mstat[0, hp], mstat[1, hp]
        m = jnp.maximum(m0, m1)
        a0, a1 = jnp.exp(m0 - m), jnp.exp(m1 - m)
        inv = 1.0 / (a0 * lstat[0, hp] + a1 * lstat[1, hp])
        f0, f1 = a0 * inv, a1 * inv
        fstat[0, hp] = f0
        fstat[1, hp] = f1
        o = oacc[0, hp] * f0 + oacc[1, hp] * f1
        mixv[:, hp * 128 : (hp + 1) * 128] = head_join(o).astype(BF16)

    ld_wo.wait()
    mixed = mixv[...]
    resid = xv[...].astype(F32) + dot(mixed, wo[...])
    unit2, inv_std2 = normalize(resid)
    ld_wu.wait()
    pre = dot(unit2.astype(BF16), wu[...])
    ld_wd.wait()
    ld_cot.wait()
    cot = cotv[...]
    grad_act = dot_t(cot, wd[...])
    c0 = 0.7978845608028654
    sq = pre * pre
    th = jnp.tanh(c0 * (pre + 0.044715 * (sq * pre)))
    act = 0.5 * pre * (1.0 + th)
    slope = 0.5 * (1.0 + th) + 0.5 * pre * (1.0 - th * th) * (c0 * (1.0 + 3.0 * 0.044715 * sq))
    outv[...] = (resid + dot(act.astype(BF16), wd[...])).astype(BF16)
    st_out = pltpu.make_async_copy(outv, out_hbm, lsem.at[len(loads) + 1])
    st_out.start()
    grad_pre = (grad_act * slope).astype(BF16)
    grad_norm2 = dot_t(grad_pre, wu[...])
    grad_resid = cot.astype(F32) + normalize_back(unit2, inv_std2, grad_norm2)
    grad_mixed = dot_t(grad_resid.astype(BF16), wo[...]).astype(BF16)
    for hp in range(PAIRS):
        stacked = head_stack(grad_mixed[:, hp * 128 : (hp + 1) * 128])
        g2[hp] = stacked
        g2t[hp] = jnp.transpose(stacked)
        mixed_pair = mixed[:, hp * 128 : (hp + 1) * 128].astype(F32)
        both = jnp.concatenate([mixed_pair, mixed_pair], 0)
        d = jnp.sum(stacked.astype(F32) * both, axis=1, keepdims=True)
        delt[hp] = jnp.broadcast_to(d, (2 * ROWS, 128))

    def attend_back(base, count, which):
        for hp in range(PAIRS):
            k = kv[base : base + count, hp * 128 : (hp + 1) * 128]
            v = kv[base : base + count, D + hp * 128 : D + (hp + 1) * 128]
            p = wexp[hp, :, base : base + count] * fstat[which, hp][:, :1]
            dp = dot_t(g2[hp], v)
            ds = (p * (dp - delt[hp][:, :1])).astype(BF16)
            dt[hp * 128 : (hp + 1) * 128, base : base + count] = dot(q2t[hp], ds).astype(BF16)
            dt[D + hp * 128 : D + (hp + 1) * 128, base : base + count] = dot(
                g2t[hp], p.astype(BF16)
            ).astype(BF16)
            dq_part = dot(ds, k)
            dq[which, hp] = dq_part

    attend_back(3 * ROWS, 4 * ROWS, 1)

    zero_block = jnp.zeros((D, ROWS), BF16)
    part[4] = zero_block
    psib[4] = zero_block
    c_ps = []
    for e in range(4):
        cols = slice((3 + e) * ROWS, (4 + e) * ROWS)
        part[e] = dot(wkv[...], dt[:, cols]).astype(BF16)
        c_ps.append(push(part.at[e], psib.at[e], rsend, rrecv, e, twin))

    attend_back(0, 3 * ROWS, 0)
    hsend[0] = dot(wkv[...], dt[:, 0:ROWS]).astype(BF16)
    c_hd = push(hsend.at[0], hrecv.at[0], rsend, rrecv, 4, down)
    hsend[1] = dot(wkv[...], dt[:, 2 * ROWS : 3 * ROWS]).astype(BF16)
    c_hu = push(hsend.at[1], hrecv.at[1], rsend, rrecv, 5, up)

    for copy in c_ps:
        copy.wait_recv()

    def slot_of(lists, target):
        slot = jnp.int32(4)
        for e in range(4):
            slot = jnp.where(lists[0, e] == target, jnp.int32(e), slot)
        return slot

    def summed(xx, rr, cols):
        target = block(xx, rows_of[rr])
        return (
            part[slot_of(listed, target), cols, :].astype(F32)
            + psib[slot_of(lsib, target), cols, :].astype(F32)
        )

    da = pl.ds(0, DHALF)
    db = pl.ds(DHALF, DHALF)

    c_x = {}
    for rr in (1, 0):
        s0 = 8 + 6 * rr
        sbuf[rr, 0] = summed(x + 2, rr, da).astype(BF16)
        c_x[rr, 0] = push(sbuf.at[rr, 0], xo.at[rr, 0], rsend, rrecv, s0, right)
        sbuf[rr, 1] = summed(x + 2, rr, db).astype(BF16)
        c_x[rr, 1] = push(sbuf.at[rr, 1], xo.at[rr, 1], rsend, rrecv, s0 + 1, left)
        sbuf[rr, 2] = summed(x + 1, rr, db).astype(BF16)
        c_x[rr, 2] = push(sbuf.at[rr, 2], yl.at[rr, db], rsend, rrecv, s0 + 2, right)
        sbuf[rr, 3] = summed(x + 3, rr, da).astype(BF16)
        c_x[rr, 3] = push(sbuf.at[rr, 3], yr.at[rr, da], rsend, rrecv, s0 + 3, left)
    for rr in (1, 0):
        s0 = 8 + 6 * rr
        c_x[rr, 0].wait_recv()
        sbuf[rr, 4] = (summed(x + 1, rr, da) + xo[rr, 0].astype(F32)).astype(BF16)
        c_x[rr, 4] = push(sbuf.at[rr, 4], yl.at[rr, da], rsend, rrecv, s0 + 4, right)
        c_x[rr, 1].wait_recv()
        sbuf[rr, 5] = (summed(x + 3, rr, db) + xo[rr, 1].astype(F32)).astype(BF16)
        c_x[rr, 5] = push(sbuf.at[rr, 5], yr.at[rr, db], rsend, rrecv, s0 + 5, left)

    own_t = dot(wkv[...], dt[:, ROWS : 2 * ROWS])
    grad_q = jnp.concatenate([head_join(dq[0, hp] + dq[1, hp]) for hp in range(PAIRS)], 1)
    grad_in = dot_t((grad_q * 0.125).astype(BF16), wq[...])

    for slot in (2, 3, 4, 5):
        c_x[1, slot].wait_recv()
    for i, cols in enumerate((da, db)):
        tbuf[i] = (
            summed(x, 1, cols) + yl[1, cols, :].astype(F32) + yr[1, cols, :].astype(F32)
        ).astype(BF16)
        c_x[2, i] = push(tbuf.at[i], ybuf.at[i], rsend, rrecv, 6 + i, across)
    c_hd.wait_recv()
    c_hu.wait_recv()
    own_t = own_t + hrecv[0].astype(F32) + hrecv[1].astype(F32)
    for slot in (2, 3, 4, 5):
        c_x[0, slot].wait_recv()
    own_t = own_t + yl[0].astype(F32) + yr[0].astype(F32)
    own_t = own_t + jnp.concatenate([summed(x, 0, da), summed(x, 0, db)], 0)
    c_x[2, 0].wait_recv()
    c_x[2, 1].wait_recv()
    own_t = own_t + jnp.concatenate([ybuf[0], ybuf[1]], 0).astype(F32)
    grad_in = grad_in + jnp.transpose(own_t)
    unit_b, inv_b = normalize(xv[...].astype(F32))
    goutv[...] = (grad_resid + normalize_back(unit_b, inv_b, grad_in)).astype(BF16)
    st_gout = pltpu.make_async_copy(goutv, gout_hbm, lsem.at[len(loads) + 2])
    st_gout.start()
    for copy in sends:
        copy.wait_send()
    st_out.wait()
    st_gout.wait()


def on_device(nodes, experts_list, w_query, w_key, w_value, w_out, w_up, w_down, cotangent):
    rows, width = nodes.shape
    hbm = pl.BlockSpec(memory_space=pl.ANY)
    tile = lambda *shape, dtype=BF16: pltpu.VMEM(shape, dtype)
    out = jax.ShapeDtypeStruct((rows, width), BF16)
    return pl.pallas_call(
        kernel,
        out_shape=(out, out),
        in_specs=[pl.BlockSpec(memory_space=pltpu.SMEM)] + [hbm] * 9,
        out_specs=(hbm, hbm),
        scratch_shapes=[
            tile(ROWS, D),
            tile(ROWS, D),
            tile(D, D),
            tile(D, 2 * D),
            tile(D, D),
            tile(D, FF),
            tile(FF, D),
            tile(16, ROWS, D),
            tile(2, ROWS, D),
            tile(7 * ROWS, 2 * D),
            tile(PAIRS, 2 * ROWS, 128),
            tile(PAIRS, 128, 2 * ROWS),
            tile(PAIRS, 2 * ROWS, 128),
            tile(PAIRS, 128, 2 * ROWS),
            tile(PAIRS, 2 * ROWS, 7 * ROWS, dtype=F32),
            tile(2, PAIRS, 2 * ROWS, 128, dtype=F32),
            tile(2, PAIRS, 2 * ROWS, 128, dtype=F32),
            tile(2, PAIRS, 2 * ROWS, 128, dtype=F32),
            tile(2, PAIRS, 2 * ROWS, 128, dtype=F32),
            tile(ROWS, D),
            tile(PAIRS, 2 * ROWS, 128, dtype=F32),
            tile(2, PAIRS, 2 * ROWS, 128, dtype=F32),
            tile(2 * D, 7 * ROWS),
            tile(5, D, ROWS),
            tile(5, D, ROWS),
            pltpu.SMEM((1, 4), jnp.int32),
            tile(2, D, ROWS),
            tile(2, D, ROWS),
            tile(2, 2, DHALF, ROWS),
            tile(2, D, ROWS),
            tile(2, D, ROWS),
            tile(2, 6, DHALF, ROWS),
            tile(2, DHALF, ROWS),
            tile(2, DHALF, ROWS),
            tile(ROWS, D),
            tile(ROWS, D),
            pltpu.SemaphoreType.DMA((12,)),
            pltpu.SemaphoreType.DMA((25,)),
            pltpu.SemaphoreType.DMA((25,)),
            pltpu.SemaphoreType.DMA((20,)),
            pltpu.SemaphoreType.DMA((20,)),
        ],
        compiler_params=pltpu.CompilerParams(
            collective_id=0, has_side_effects=True, vmem_limit_bytes=60 * 1024 * 1024
        ),
        name="exphormer",
    )(
        experts_list,
        nodes,
        experts_list,
        w_query,
        w_key,
        w_value,
        w_out,
        w_up,
        w_down,
        cotangent,
    )


def solution(mesh):
    return jax.shard_map(
        on_device,
        mesh=mesh,
        in_specs=(
            P(("blk", "dom"), None),
            P(("blk", "dom"), None),
            P(),
            P(),
            P(),
            P(),
            P(),
            P(),
            P(("blk", "dom"), None),
        ),
        out_specs=(P(("blk", "dom"), None), P(("blk", "dom"), None)),
        check_vma=False,
    )
```

```python
import functools

import jax
import jax.numpy as jnp
from jax import lax
from jax.experimental import pallas as pl
from jax.experimental.pallas import tpu as pltpu
from jax.sharding import PartitionSpec as P

EPS = 1e-05
MESH = pl.DeviceIdType.MESH
D = 512
FF = 1024
ROWS = 128
HALF = 64
DHALF = 256
PAIRS = 4
F32 = jnp.float32
BF16 = jnp.bfloat16


def normalize(values):
    mean_v = jnp.mean(values, axis=-1, keepdims=True)
    centered = values - mean_v
    inv_std = lax.rsqrt(jnp.mean(centered * centered, axis=-1, keepdims=True) + EPS)
    return (centered * inv_std, inv_std)


def normalize_back(unit, inv_std, upstream):
    return inv_std * (
        upstream
        - jnp.mean(upstream, axis=-1, keepdims=True)
        - unit * jnp.mean(upstream * unit, axis=-1, keepdims=True)
    )


def dot(a, b):
    return jnp.dot(a, b, preferred_element_type=F32)


def dot_t(a, b):
    return lax.dot_general(a, b, (((1,), (1,)), ((), ())), preferred_element_type=F32)


def head_stack(tile):
    low = lax.broadcasted_iota(jnp.int32, tile.shape, 1) < 64
    zero = jnp.zeros_like(tile)
    return jnp.concatenate([jnp.where(low, tile, zero), jnp.where(low, zero, tile)], 0)


def head_join(stacked):
    low = lax.broadcasted_iota(jnp.int32, (ROWS, 128), 1) < 64
    return jnp.where(low, stacked[:ROWS], stacked[ROWS:])


def kernel(
    listed,
    nodes_hbm,
    list_hbm,
    wq_hbm,
    wk_hbm,
    wv_hbm,
    wo_hbm,
    wu_hbm,
    wd_hbm,
    cot_hbm,
    out_hbm,
    gout_hbm,
    xv,
    cotv,
    wq,
    wkv,
    wo,
    wu,
    wd,
    gath,
    halo,
    kv,
    q2,
    q2t,
    g2,
    g2t,
    wexp,
    mstat,
    lstat,
    oacc,
    fstat,
    mixv,
    delt,
    dq,
    dt,
    part,
    psib,
    lsib,
    hsend,
    hrecv,
    xo,
    yl,
    yr,
    sbuf,
    tbuf,
    ybuf,
    nbuf,
    actv,
    residv,
    gact,
    lsem,
    gsend,
    grecv,
    rsend,
    rrecv,
):
    blk = lax.axis_index("blk")
    dom = lax.axis_index("dom")
    ndom = lax.axis_size("dom")
    core = blk % 2
    x = (blk // 2) % 4
    h = blk // 8

    def at(xx, hh, cc):
        return hh * 8 + (xx % 4) * 2 + cc

    right = {"blk": at(x + 1, h, core), "dom": dom}
    left = {"blk": at(x + 3, h, core), "dom": dom}
    across = {"blk": at(x, 1 - h, core), "dom": dom}
    twin = {"blk": at(x, h, 1 - core), "dom": dom}
    up = {"blk": blk, "dom": (dom + 1) % ndom}
    down = {"blk": blk, "dom": (dom + ndom - 1) % ndom}

    barrier = pltpu.get_barrier_semaphore()
    for peer in (right, left, across, twin, up, down):
        pl.semaphore_signal(barrier, inc=1, device_id=peer, device_id_type=MESH)

    loads = []

    def load(src, dst):
        copy = pltpu.make_async_copy(src, dst, lsem.at[len(loads)])
        copy.start()
        loads.append(copy)
        return copy

    own = at(x, h, core)
    ld_x = load(nodes_hbm, xv)
    ld_wk = load(wk_hbm, wkv.at[:, pl.ds(0, D)])
    ld_wv = load(wv_hbm, wkv.at[:, pl.ds(D, D)])
    ld_wq = load(wq_hbm, wq)
    ld_own = load(nodes_hbm, gath.at[own])
    ld_cot = load(cot_hbm, cotv)
    ld_wd = load(wd_hbm, wd)
    ld_wo = load(wo_hbm, wo)
    ld_wu = load(wu_hbm, wu)

    pl.semaphore_wait(barrier, 6)

    sends = []

    def push(src, dst, ssems, rsems, slot, peer):
        copy = pltpu.make_async_remote_copy(
            src_ref=src,
            dst_ref=dst,
            send_sem=ssems.at[slot],
            recv_sem=rsems.at[slot],
            device_id=peer,
            device_id_type=MESH,
        )
        copy.start()
        sends.append(copy)
        return copy

    top = pl.ds(0, HALF)
    bottom = pl.ds(HALF, HALF)

    def block(xx, rr):
        return at(xx, rr, core)

    rows_of = (h, 1 - h)

    c_r = {}
    c_l = {}
    c_r[0, 0] = push(nodes_hbm.at[top], gath.at[own, top], gsend, grecv, 0, right)
    c_l[0, 1] = push(nodes_hbm.at[bottom], gath.at[own, bottom], gsend, grecv, 5, left)
    c_y = [None, None]
    c_y[0] = push(nodes_hbm.at[top], gath.at[own, top], gsend, grecv, 12, across)
    c_y[1] = push(nodes_hbm.at[bottom], gath.at[own, bottom], gsend, grecv, 13, across)
    c_r[0, 1] = push(nodes_hbm.at[bottom], gath.at[own, bottom], gsend, grecv, 1, right)
    c_l[0, 0] = push(nodes_hbm.at[top], gath.at[own, top], gsend, grecv, 4, left)
    c_up = push(nodes_hbm, halo.at[0], gsend, grecv, 14, up)
    c_dn = push(nodes_hbm, halo.at[1], gsend, grecv, 15, down)
    c_list = push(list_hbm, lsib, gsend, grecv, 24, twin)
    c_tw = []
    c_tw.append(push(nodes_hbm, gath.at[own], gsend, grecv, 16, twin))

    ld_x.wait()

    x_full = xv[...].astype(F32)
    unit, inv_std = normalize(x_full)
    normed = unit.astype(BF16)
    ld_wk.wait()
    ld_wv.wait()
    kv[pl.ds(2 * ROWS, ROWS), :] = dot(normed, wkv[...]).astype(BF16)
    ld_wq.wait()
    queries = dot(normed, wq[...]).astype(BF16) * jnp.asarray(0.125, BF16)
    for hp in range(PAIRS):
        stacked = head_stack(queries[:, hp * 128 : (hp + 1) * 128])
        q2[hp] = stacked
        q2t[hp] = jnp.transpose(stacked)

    fwd_r = [None, None]
    fwd_l = [None, None]

    def forward(rr):
        row = rows_of[rr]
        c_r[rr, 0].wait_recv()
        from_left = block(x + 3, row)
        fwd_r[rr] = push(gath.at[from_left, top], gath.at[from_left, top], gsend, grecv, 8 + rr, right)
        c_l[rr, 1].wait_recv()
        from_right = block(x + 1, row)
        fwd_l[rr] = push(
            gath.at[from_right, bottom], gath.at[from_right, bottom], gsend, grecv, 10 + rr, left
        )

    def to_twin(slot, who):
        c_tw.append(push(gath.at[who], gath.at[who], gsend, grecv, slot, twin))

    ld_wd.wait()
    ld_cot.wait()
    gact[...] = dot_t(cotv[...], wd[...])
    forward(0)
    other = block(x, 1 - h)
    c_y[0].wait_recv()
    c_r[1, 0] = push(gath.at[other, top], gath.at[other, top], gsend, grecv, 2, right)
    c_l[1, 0] = push(gath.at[other, top], gath.at[other, top], gsend, grecv, 6, left)
    c_y[1].wait_recv()
    c_l[1, 1] = push(gath.at[other, bottom], gath.at[other, bottom], gsend, grecv, 7, left)
    c_r[1, 1] = push(gath.at[other, bottom], gath.at[other, bottom], gsend, grecv, 3, right)
    to_twin(17, other)
    c_r[0, 1].wait_recv()
    to_twin(18, block(x + 3, h))
    c_l[0, 0].wait_recv()
    to_twin(19, block(x + 1, h))

    def project(raw, row0):
        unit_o, _ = normalize(raw.astype(F32))
        kv[pl.ds(row0, ROWS), :] = dot(unit_o.astype(BF16), wkv[...]).astype(BF16)

    def attend(base, count, which, pairs=range(PAIRS)):
        for hp in pairs:
            k = kv[base : base + count, hp * 128 : (hp + 1) * 128]
            v = kv[base : base + count, D + hp * 128 : D + (hp + 1) * 128]
            s = dot_t(q2[hp], k)
            m = jnp.max(s, axis=1, keepdims=True)
            w = jnp.exp(s - m)
            wexp[hp, :, base : base + count] = w
            total = jnp.sum(w, axis=1, keepdims=True)
            oacc[which, hp] = dot(w.astype(BF16), v)
            mstat[which, hp] = jnp.broadcast_to(m, (2 * ROWS, 128))
            lstat[which, hp] = jnp.broadcast_to(total, (2 * ROWS, 128))

    c_up.wait_recv()
    project(halo[0], 0)
    c_dn.wait_recv()
    project(halo[1], ROWS)
    attend(0, 3 * ROWS, 0, (0, 1))
    fwd_r[0].wait_recv()
    fwd_l[0].wait_recv()
    to_twin(22, block(x + 2, h))
    attend(0, 3 * ROWS, 0, (2, 3))
    forward(1)
    c_r[1, 1].wait_recv()
    to_twin(20, block(x + 3, 1 - h))
    c_l[1, 0].wait_recv()
    to_twin(21, block(x + 1, 1 - h))
    fwd_r[1].wait_recv()
    fwd_l[1].wait_recv()
    to_twin(23, block(x + 2, 1 - h))
    for copy in c_tw:
        copy.wait_recv()
    c_list.wait_recv()
    ld_own.wait()

    for e in range(4):
        unit_e, _ = normalize(gath[listed[0, e]].astype(F32))
        nbuf[e * ROWS : (e + 1) * ROWS] = unit_e.astype(BF16)
    kv[3 * ROWS : 7 * ROWS, :] = dot(nbuf[...], wkv[...]).astype(BF16)
    attend(3 * ROWS, 4 * ROWS, 1)

    for hp in range(PAIRS):
        m0, m1 = mstat[0, hp], mstat[1, hp]
        m = jnp.maximum(m0, m1)
        a0, a1 = jnp.exp(m0 - m), jnp.exp(m1 - m)
        inv = 1.0 / (a0 * lstat[0, hp] + a1 * lstat[1, hp])
        f0, f1 = a0 * inv, a1 * inv
        fstat[0, hp] = f0
        fstat[1, hp] = f1
        o = oacc[0, hp] * f0 + oacc[1, hp] * f1
        mixv[:, hp * 128 : (hp + 1) * 128] = head_join(o).astype(BF16)

    ld_wo.wait()
    mixed = mixv[...]
    resid = xv[...].astype(F32) + dot(mixed, wo[...])
    unit2, inv_std2 = normalize(resid)
    ld_wu.wait()
    pre = dot(unit2.astype(BF16), wu[...])
    cot = cotv[...]
    c0 = 0.7978845608028654
    sq = pre * pre
    th = jnp.tanh(c0 * (pre + 0.044715 * (sq * pre)))
    act = 0.5 * pre * (1.0 + th)
    slope = 0.5 * (1.0 + th) + 0.5 * pre * (1.0 - th * th) * (c0 * (1.0 + 3.0 * 0.044715 * sq))
    actv[...] = act.astype(BF16)
    residv[...] = resid
    grad_pre = (gact[...] * slope).astype(BF16)
    grad_norm2 = dot_t(grad_pre, wu[...])
    grad_resid = cot.astype(F32) + normalize_back(unit2, inv_std2, grad_norm2)
    grad_mixed = dot_t(grad_resid.astype(BF16), wo[...]).astype(BF16)
    for hp in range(PAIRS):
        stacked = head_stack(grad_mixed[:, hp * 128 : (hp + 1) * 128])
        g2[hp] = stacked
        g2t[hp] = jnp.transpose(stacked)
        mixed_pair = mixed[:, hp * 128 : (hp + 1) * 128].astype(F32)
        both = jnp.concatenate([mixed_pair, mixed_pair], 0)
        d = jnp.sum(stacked.astype(F32) * both, axis=1, keepdims=True)
        delt[hp] = jnp.broadcast_to(d, (2 * ROWS, 128))

    def attend_back(base, count, which, pairs=range(PAIRS)):
        for hp in pairs:
            k = kv[base : base + count, hp * 128 : (hp + 1) * 128]
            v = kv[base : base + count, D + hp * 128 : D + (hp + 1) * 128]
            p = wexp[hp, :, base : base + count] * fstat[which, hp][:, :1]
            dp = dot_t(g2[hp], v)
            ds = (p * (dp - delt[hp][:, :1])).astype(BF16)
            dt[hp * 128 : (hp + 1) * 128, base : base + count] = dot(q2t[hp], ds).astype(BF16)
            dt[D + hp * 128 : D + (hp + 1) * 128, base : base + count] = dot(
                g2t[hp], p.astype(BF16)
            ).astype(BF16)
            dq[which, hp] = dot(ds, k)

    attend_back(3 * ROWS, 4 * ROWS, 1)

    zero_block = jnp.zeros((D, ROWS), BF16)
    part[4] = zero_block
    psib[4] = zero_block
    c_ps = []
    for e in (0, 2):
        both = dot(wkv[...], dt[:, (3 + e) * ROWS : (5 + e) * ROWS]).astype(BF16)
        part[e] = both[:, :ROWS]
        part[e + 1] = both[:, ROWS:]
        c_ps.append(push(part.at[e], psib.at[e], rsend, rrecv, e, twin))
        c_ps.append(push(part.at[e + 1], psib.at[e + 1], rsend, rrecv, e + 1, twin))

    attend_back(0, 3 * ROWS, 0, (0, 1, 2))
    for copy in c_ps:
        copy.wait_recv()

    def slot_of(lists, target):
        slot = jnp.int32(4)
        for e in range(4):
            slot = jnp.where(lists[0, e] == target, jnp.int32(e), slot)
        return slot

    def summed(xx, rr, cols):
        target = block(xx, rows_of[rr])
        return (
            part[slot_of(listed, target), cols, :].astype(F32)
            + psib[slot_of(lsib, target), cols, :].astype(F32)
        )

    da = pl.ds(0, DHALF)
    db = pl.ds(DHALF, DHALF)

    c_x = {}

    def first_step(rr):
        s0 = 8 + 6 * rr
        sbuf[rr, 0] = summed(x + 2, rr, da).astype(BF16)
        c_x[rr, 0] = push(sbuf.at[rr, 0], xo.at[rr, 0], rsend, rrecv, s0, right)
        sbuf[rr, 1] = summed(x + 2, rr, db).astype(BF16)
        c_x[rr, 1] = push(sbuf.at[rr, 1], xo.at[rr, 1], rsend, rrecv, s0 + 1, left)
        sbuf[rr, 2] = summed(x + 1, rr, db).astype(BF16)
        c_x[rr, 2] = push(sbuf.at[rr, 2], yl.at[rr, db], rsend, rrecv, s0 + 2, right)
        sbuf[rr, 3] = summed(x + 3, rr, da).astype(BF16)
        c_x[rr, 3] = push(sbuf.at[rr, 3], yr.at[rr, da], rsend, rrecv, s0 + 3, left)

    def second_step(rr):
        s0 = 8 + 6 * rr
        c_x[rr, 0].wait_recv()
        sbuf[rr, 4] = (summed(x + 1, rr, da) + xo[rr, 0].astype(F32)).astype(BF16)
        c_x[rr, 4] = push(sbuf.at[rr, 4], yl.at[rr, da], rsend, rrecv, s0 + 4, right)
        c_x[rr, 1].wait_recv()
        sbuf[rr, 5] = (summed(x + 3, rr, db) + xo[rr, 1].astype(F32)).astype(BF16)
        c_x[rr, 5] = push(sbuf.at[rr, 5], yr.at[rr, db], rsend, rrecv, s0 + 5, left)

    first_step(1)
    attend_back(0, 3 * ROWS, 0, (3,))
    halves_t = dot(wkv[...], dt[:, 0 : 2 * ROWS]).astype(BF16)
    hsend[0] = halves_t[:, :ROWS]
    hsend[1] = halves_t[:, ROWS:]
    c_hd = push(hsend.at[0], hrecv.at[0], rsend, rrecv, 4, down)
    c_hu = push(hsend.at[1], hrecv.at[1], rsend, rrecv, 5, up)
    second_step(1)
    first_step(0)

    own_t = dot(wkv[...], dt[:, 2 * ROWS : 3 * ROWS])
    grad_q = jnp.concatenate([head_join(dq[0, hp] + dq[1, hp]) for hp in range(PAIRS)], 1)
    grad_in = dot_t((grad_q * 0.125).astype(BF16), wq[...])
    out_hbm[...] = (residv[...] + dot(actv[...], wd[...])).astype(BF16)

    second_step(0)
    for slot in (2, 3, 4, 5):
        c_x[1, slot].wait_recv()
    for i, cols in enumerate((da, db)):
        tbuf[i] = (
            summed(x, 1, cols) + yl[1, cols, :].astype(F32) + yr[1, cols, :].astype(F32)
        ).astype(BF16)
        c_x[2, i] = push(tbuf.at[i], ybuf.at[i], rsend, rrecv, 6 + i, across)
    c_hd.wait_recv()
    c_hu.wait_recv()
    own_t = own_t + hrecv[0].astype(F32) + hrecv[1].astype(F32)
    for slot in (2, 3, 4, 5):
        c_x[0, slot].wait_recv()
    own_t = own_t + yl[0].astype(F32) + yr[0].astype(F32)
    own_t = own_t + jnp.concatenate([summed(x, 0, da), summed(x, 0, db)], 0)
    grad_in = grad_in + jnp.transpose(own_t)
    unit_b, inv_b = normalize(xv[...].astype(F32))
    c_x[2, 0].wait_recv()
    c_x[2, 1].wait_recv()
    grad_in = grad_in + jnp.transpose(jnp.concatenate([ybuf[0], ybuf[1]], 0).astype(F32))
    gout_hbm[...] = (grad_resid + normalize_back(unit_b, inv_b, grad_in)).astype(BF16)
    for copy in sends:
        copy.wait_send()


def on_device(nodes, experts_list, w_query, w_key, w_value, w_out, w_up, w_down, cotangent):
    rows, width = nodes.shape
    hbm = pl.BlockSpec(memory_space=pltpu.HBM)
    tile = lambda *shape, dtype=BF16: pltpu.VMEM(shape, dtype)
    out = jax.ShapeDtypeStruct((rows, width), BF16)
    vm = pl.BlockSpec(memory_space=pltpu.VMEM)
    return pl.pallas_call(
        kernel,
        out_shape=(out, out),
        in_specs=[pl.BlockSpec(memory_space=pltpu.SMEM)] + [hbm] * 9,
        out_specs=(vm, vm),
        scratch_shapes=[
            tile(ROWS, D),
            tile(ROWS, D),
            tile(D, D),
            tile(D, 2 * D),
            tile(D, D),
            tile(D, FF),
            tile(FF, D),
            tile(16, ROWS, D),
            tile(2, ROWS, D),
            tile(7 * ROWS, 2 * D),
            tile(PAIRS, 2 * ROWS, 128),
            tile(PAIRS, 128, 2 * ROWS),
            tile(PAIRS, 2 * ROWS, 128),
            tile(PAIRS, 128, 2 * ROWS),
            tile(PAIRS, 2 * ROWS, 7 * ROWS, dtype=F32),
            tile(2, PAIRS, 2 * ROWS, 128, dtype=F32),
            tile(2, PAIRS, 2 * ROWS, 128, dtype=F32),
            tile(2, PAIRS, 2 * ROWS, 128, dtype=F32),
            tile(2, PAIRS, 2 * ROWS, 128, dtype=F32),
            tile(ROWS, D),
            tile(PAIRS, 2 * ROWS, 128, dtype=F32),
            tile(2, PAIRS, 2 * ROWS, 128, dtype=F32),
            tile(2 * D, 7 * ROWS),
            tile(5, D, ROWS),
            tile(5, D, ROWS),
            pltpu.SMEM((1, 4), jnp.int32),
            tile(2, D, ROWS),
            tile(2, D, ROWS),
            tile(2, 2, DHALF, ROWS),
            tile(2, D, ROWS),
            tile(2, D, ROWS),
            tile(2, 6, DHALF, ROWS),
            tile(2, DHALF, ROWS),
            tile(2, DHALF, ROWS),
            tile(4 * ROWS, D),
            tile(ROWS, FF),
            tile(ROWS, D, dtype=F32),
            tile(ROWS, FF, dtype=F32),
            pltpu.SemaphoreType.DMA((12,)),
            pltpu.SemaphoreType.DMA((25,)),
            pltpu.SemaphoreType.DMA((25,)),
            pltpu.SemaphoreType.DMA((20,)),
            pltpu.SemaphoreType.DMA((20,)),
        ],
        compiler_params=pltpu.CompilerParams(
            collective_id=0, has_side_effects=True, vmem_limit_bytes=28 * 1024 * 1024
        ),
        name="exphormer",
    )(
        experts_list,
        *(
            pltpu.with_memory_space_constraint(a, pltpu.HBM)
            for a in (nodes, experts_list, w_query, w_key, w_value, w_out, w_up, w_down, cotangent)
        ),
    )


def solution(mesh):
    return jax.shard_map(
        on_device,
        mesh=mesh,
        in_specs=(
            P(("blk", "dom"), None),
            P(("blk", "dom"), None),
            P(),
            P(),
            P(),
            P(),
            P(),
            P(),
            P(("blk", "dom"), None),
        ),
        out_specs=(P(("blk", "dom"), None), P(("blk", "dom"), None)),
        check_vma=False,
    )
```

```python
import functools

import jax
import jax.numpy as jnp
from jax import lax
from jax.experimental import pallas as pl
from jax.experimental.pallas import tpu as pltpu
from jax.sharding import PartitionSpec as P

EPS = 1e-05
MESH = pl.DeviceIdType.MESH
D = 512
FF = 1024
ROWS = 128
HALF = 64
DHALF = 256
PAIRS = 4
F32 = jnp.float32
BF16 = jnp.bfloat16


def normalize(values):
    mean_v = jnp.mean(values, axis=-1, keepdims=True)
    centered = values - mean_v
    inv_std = lax.rsqrt(jnp.mean(centered * centered, axis=-1, keepdims=True) + EPS)
    return (centered * inv_std, inv_std)


def normalize_back(unit, inv_std, upstream):
    return inv_std * (
        upstream
        - jnp.mean(upstream, axis=-1, keepdims=True)
        - unit * jnp.mean(upstream * unit, axis=-1, keepdims=True)
    )


def dot(a, b):
    return jnp.dot(a, b, preferred_element_type=F32)


def dot_t(a, b):
    return lax.dot_general(a, b, (((1,), (1,)), ((), ())), preferred_element_type=F32)


def head_stack(tile):
    low = lax.broadcasted_iota(jnp.int32, tile.shape, 1) < 64
    zero = jnp.zeros_like(tile)
    return jnp.concatenate([jnp.where(low, tile, zero), jnp.where(low, zero, tile)], 0)


def head_join(stacked):
    low = lax.broadcasted_iota(jnp.int32, (ROWS, 128), 1) < 64
    return jnp.where(low, stacked[:ROWS], stacked[ROWS:])


def kernel(
    listed,
    nodes_hbm,
    list_hbm,
    wq_hbm,
    wk_hbm,
    wv_hbm,
    wo_hbm,
    wu_hbm,
    wd_hbm,
    cot_hbm,
    out_hbm,
    gout_hbm,
    xv,
    cotv,
    wq,
    wkv,
    wo,
    wu,
    wd,
    gath,
    halo,
    kv,
    q2,
    q2t,
    g2,
    g2t,
    wexp,
    mstat,
    lstat,
    oacc,
    fstat,
    mixv,
    delt,
    dq,
    dt,
    part,
    psib,
    lsib,
    hsend,
    hrecv,
    xo,
    yl,
    yr,
    sbuf,
    tbuf,
    ybuf,
    nbuf,
    actv,
    residv,
    gact,
    lsem,
    gsend,
    grecv,
    rsend,
    rrecv,
):
    blk = lax.axis_index("blk")
    dom = lax.axis_index("dom")
    ndom = lax.axis_size("dom")
    core = blk % 2
    x = (blk // 2) % 4
    h = blk // 8

    def at(xx, hh, cc):
        return hh * 8 + (xx % 4) * 2 + cc

    right = {"blk": at(x + 1, h, core), "dom": dom}
    left = {"blk": at(x + 3, h, core), "dom": dom}
    across = {"blk": at(x, 1 - h, core), "dom": dom}
    twin = {"blk": at(x, h, 1 - core), "dom": dom}
    up = {"blk": blk, "dom": (dom + 1) % ndom}
    down = {"blk": blk, "dom": (dom + ndom - 1) % ndom}

    barrier = pltpu.get_barrier_semaphore()
    for peer in (right, left, across, twin, up, down):
        pl.semaphore_signal(barrier, inc=1, device_id=peer, device_id_type=MESH)

    pl.semaphore_wait(barrier, 6)

    sends = []

    def push(src, dst, ssems, rsems, slot, peer):
        copy = pltpu.make_async_remote_copy(
            src_ref=src,
            dst_ref=dst,
            send_sem=ssems.at[slot],
            recv_sem=rsems.at[slot],
            device_id=peer,
            device_id_type=MESH,
        )
        copy.start()
        sends.append(copy)
        return copy

    top = pl.ds(0, HALF)
    bottom = pl.ds(HALF, HALF)

    def block(xx, rr):
        return at(xx, rr, core)

    rows_of = (h, 1 - h)

    own = block(x, h)
    c_r = {}
    c_l = {}
    c_y = []
    c_y.append(push(nodes_hbm.at[top], gath.at[own, top], gsend, grecv, 12, across))
    c_r[0, 0] = push(nodes_hbm.at[top], gath.at[own, top], gsend, grecv, 0, right)
    c_l[0, 1] = push(nodes_hbm.at[bottom], gath.at[own, bottom], gsend, grecv, 5, left)
    c_y.append(push(nodes_hbm.at[bottom], gath.at[own, bottom], gsend, grecv, 13, across))
    c_r[0, 1] = push(nodes_hbm.at[bottom], gath.at[own, bottom], gsend, grecv, 1, right)
    c_l[0, 0] = push(nodes_hbm.at[top], gath.at[own, top], gsend, grecv, 4, left)

    loads = []

    def load(src, dst):
        copy = pltpu.make_async_copy(src, dst, lsem.at[len(loads)])
        copy.start()
        loads.append(copy)
        return copy

    ld_x = load(nodes_hbm, xv)
    ld_wk = load(wk_hbm, wkv.at[:, pl.ds(0, D)])
    ld_wv = load(wv_hbm, wkv.at[:, pl.ds(D, D)])
    ld_wq = load(wq_hbm, wq)
    ld_own = load(nodes_hbm, gath.at[own])
    ld_cot = load(cot_hbm, cotv)
    ld_wd = load(wd_hbm, wd)
    ld_wo = load(wo_hbm, wo)
    ld_wu = load(wu_hbm, wu)

    c_list = push(list_hbm, lsib, gsend, grecv, 24, twin)
    c_tw = [push(nodes_hbm, gath.at[own], gsend, grecv, 16, twin)]

    ld_x.wait()
    x_full = xv[...].astype(F32)
    unit, inv_std = normalize(x_full)
    normed = unit.astype(BF16)
    ld_wk.wait()
    ld_wv.wait()
    kv[pl.ds(2 * ROWS, ROWS), :] = dot(normed, wkv[...]).astype(BF16)
    ld_wq.wait()
    queries = dot(normed, wq[...]).astype(BF16) * jnp.asarray(0.125, BF16)
    for hp in range(PAIRS):
        stacked = head_stack(queries[:, hp * 128 : (hp + 1) * 128])
        q2[hp] = stacked
        q2t[hp] = jnp.transpose(stacked)

    fwd_r = [None, None]
    fwd_l = [None, None]

    def forward(rr):
        row = rows_of[rr]
        c_r[rr, 0].wait_recv()
        from_left = block(x + 3, row)
        fwd_r[rr] = push(gath.at[from_left, top], gath.at[from_left, top], gsend, grecv, 8 + rr, right)
        c_l[rr, 1].wait_recv()
        from_right = block(x + 1, row)
        fwd_l[rr] = push(
            gath.at[from_right, bottom], gath.at[from_right, bottom], gsend, grecv, 10 + rr, left
        )

    def to_twin(slot, who):
        c_tw.append(push(gath.at[who], gath.at[who], gsend, grecv, slot, twin))

    c_up = push(nodes_hbm, halo.at[0], gsend, grecv, 14, up)
    c_dn = push(nodes_hbm, halo.at[1], gsend, grecv, 15, down)
    ld_wd.wait()
    ld_cot.wait()
    gact[...] = dot_t(cotv[...], wd[...])
    forward(0)
    other = block(x, 1 - h)
    c_y[0].wait_recv()
    c_r[1, 0] = push(gath.at[other, top], gath.at[other, top], gsend, grecv, 2, right)
    c_l[1, 0] = push(gath.at[other, top], gath.at[other, top], gsend, grecv, 6, left)
    c_y[1].wait_recv()
    c_l[1, 1] = push(gath.at[other, bottom], gath.at[other, bottom], gsend, grecv, 7, left)
    c_r[1, 1] = push(gath.at[other, bottom], gath.at[other, bottom], gsend, grecv, 3, right)
    to_twin(17, other)
    c_r[0, 1].wait_recv()
    to_twin(18, block(x + 3, h))
    c_l[0, 0].wait_recv()
    to_twin(19, block(x + 1, h))

    def project(raw, row0):
        unit_o, _ = normalize(raw.astype(F32))
        kv[pl.ds(row0, ROWS), :] = dot(unit_o.astype(BF16), wkv[...]).astype(BF16)

    def attend(base, count, which, pairs=range(PAIRS)):
        for hp in pairs:
            k = kv[base : base + count, hp * 128 : (hp + 1) * 128]
            v = kv[base : base + count, D + hp * 128 : D + (hp + 1) * 128]
            s = dot_t(q2[hp], k)
            m = jnp.max(s, axis=1, keepdims=True)
            w = jnp.exp(s - m)
            wexp[hp, :, base : base + count] = w
            total = jnp.sum(w, axis=1, keepdims=True)
            oacc[which, hp] = dot(w.astype(BF16), v)
            mstat[which, hp] = jnp.broadcast_to(m, (2 * ROWS, 128))
            lstat[which, hp] = jnp.broadcast_to(total, (2 * ROWS, 128))

    forward(1)
    fwd_r[0].wait_recv()
    fwd_l[0].wait_recv()
    to_twin(22, block(x + 2, h))
    c_up.wait_recv()
    project(halo[0], 0)
    c_dn.wait_recv()
    project(halo[1], ROWS)
    c_r[1, 1].wait_recv()
    to_twin(20, block(x + 3, 1 - h))
    c_l[1, 0].wait_recv()
    to_twin(21, block(x + 1, 1 - h))
    attend(0, 3 * ROWS, 0)
    fwd_r[1].wait_recv()
    fwd_l[1].wait_recv()
    to_twin(23, block(x + 2, 1 - h))
    for copy in c_tw:
        copy.wait_recv()
    c_list.wait_recv()
    ld_own.wait()

    for e in range(4):
        unit_e, _ = normalize(gath[listed[0, e]].astype(F32))
        nbuf[e * ROWS : (e + 1) * ROWS] = unit_e.astype(BF16)
    kv[3 * ROWS : 7 * ROWS, :] = dot(nbuf[...], wkv[...]).astype(BF16)
    attend(3 * ROWS, 4 * ROWS, 1)

    for hp in range(PAIRS):
        m0, m1 = mstat[0, hp], mstat[1, hp]
        m = jnp.maximum(m0, m1)
        a0, a1 = jnp.exp(m0 - m), jnp.exp(m1 - m)
        inv = 1.0 / (a0 * lstat[0, hp] + a1 * lstat[1, hp])
        f0, f1 = a0 * inv, a1 * inv
        fstat[0, hp] = f0
        fstat[1, hp] = f1
        o = oacc[0, hp] * f0 + oacc[1, hp] * f1
        mixv[:, hp * 128 : (hp + 1) * 128] = head_join(o).astype(BF16)

    ld_wo.wait()
    mixed = mixv[...]
    resid = xv[...].astype(F32) + dot(mixed, wo[...])
    unit2, inv_std2 = normalize(resid)
    ld_wu.wait()
    pre = dot(unit2.astype(BF16), wu[...])
    cot = cotv[...]
    c0 = 0.7978845608028654
    sq = pre * pre
    th = jnp.tanh(c0 * (pre + 0.044715 * (sq * pre)))
    act = 0.5 * pre * (1.0 + th)
    slope = 0.5 * (1.0 + th) + 0.5 * pre * (1.0 - th * th) * (c0 * (1.0 + 3.0 * 0.044715 * sq))
    actv[...] = act.astype(BF16)
    residv[...] = resid
    grad_pre = (gact[...] * slope).astype(BF16)
    grad_norm2 = dot_t(grad_pre, wu[...])
    grad_resid = cot.astype(F32) + normalize_back(unit2, inv_std2, grad_norm2)
    grad_mixed = dot_t(grad_resid.astype(BF16), wo[...]).astype(BF16)
    for hp in range(PAIRS):
        stacked = head_stack(grad_mixed[:, hp * 128 : (hp + 1) * 128])
        g2[hp] = stacked
        g2t[hp] = jnp.transpose(stacked)
        mixed_pair = mixed[:, hp * 128 : (hp + 1) * 128].astype(F32)
        both = jnp.concatenate([mixed_pair, mixed_pair], 0)
        d = jnp.sum(stacked.astype(F32) * both, axis=1, keepdims=True)
        delt[hp] = jnp.broadcast_to(d, (2 * ROWS, 128))

    def attend_back(base, count, which, pairs=range(PAIRS)):
        for hp in pairs:
            k = kv[base : base + count, hp * 128 : (hp + 1) * 128]
            v = kv[base : base + count, D + hp * 128 : D + (hp + 1) * 128]
            p = wexp[hp, :, base : base + count] * fstat[which, hp][:, :1]
            dp = dot_t(g2[hp], v)
            ds = (p * (dp - delt[hp][:, :1])).astype(BF16)
            dt[hp * 128 : (hp + 1) * 128, base : base + count] = dot(q2t[hp], ds).astype(BF16)
            dt[D + hp * 128 : D + (hp + 1) * 128, base : base + count] = dot(
                g2t[hp], p.astype(BF16)
            ).astype(BF16)
            dq[which, hp] = dot(ds, k)

    attend_back(3 * ROWS, 4 * ROWS, 1)

    zero_block = jnp.zeros((D, ROWS), BF16)
    part[4] = zero_block
    psib[4] = zero_block
    c_ps = []
    for e in (0, 2):
        both = dot(wkv[...], dt[:, (3 + e) * ROWS : (5 + e) * ROWS]).astype(BF16)
        part[e] = both[:, :ROWS]
        part[e + 1] = both[:, ROWS:]
        c_ps.append(push(part.at[e], psib.at[e], rsend, rrecv, e, twin))
        c_ps.append(push(part.at[e + 1], psib.at[e + 1], rsend, rrecv, e + 1, twin))

    attend_back(0, 3 * ROWS, 0, (0, 1, 2))
    for copy in c_ps:
        copy.wait_recv()

    def slot_of(lists, target):
        slot = jnp.int32(4)
        for e in range(4):
            slot = jnp.where(lists[0, e] == target, jnp.int32(e), slot)
        return slot

    def summed(xx, rr, cols):
        target = block(xx, rows_of[rr])
        return (
            part[slot_of(listed, target), cols, :].astype(F32)
            + psib[slot_of(lsib, target), cols, :].astype(F32)
        )

    da = pl.ds(0, DHALF)
    db = pl.ds(DHALF, DHALF)

    c_x = {}

    def opposite_step(rr):
        s0 = 8 + 6 * rr
        sbuf[rr, 0] = summed(x + 2, rr, da).astype(BF16)
        c_x[rr, 0] = push(sbuf.at[rr, 0], xo.at[rr, 0], rsend, rrecv, s0, right)
        sbuf[rr, 1] = summed(x + 2, rr, db).astype(BF16)
        c_x[rr, 1] = push(sbuf.at[rr, 1], xo.at[rr, 1], rsend, rrecv, s0 + 1, left)

    def direct_step(rr):
        s0 = 8 + 6 * rr
        sbuf[rr, 2] = summed(x + 1, rr, db).astype(BF16)
        c_x[rr, 2] = push(sbuf.at[rr, 2], yl.at[rr, db], rsend, rrecv, s0 + 2, right)
        sbuf[rr, 3] = summed(x + 3, rr, da).astype(BF16)
        c_x[rr, 3] = push(sbuf.at[rr, 3], yr.at[rr, da], rsend, rrecv, s0 + 3, left)

    def second_step(rr):
        s0 = 8 + 6 * rr
        c_x[rr, 0].wait_recv()
        sbuf[rr, 4] = (summed(x + 1, rr, da) + xo[rr, 0].astype(F32)).astype(BF16)
        c_x[rr, 4] = push(sbuf.at[rr, 4], yl.at[rr, da], rsend, rrecv, s0 + 4, right)
        c_x[rr, 1].wait_recv()
        sbuf[rr, 5] = (summed(x + 3, rr, db) + xo[rr, 1].astype(F32)).astype(BF16)
        c_x[rr, 5] = push(sbuf.at[rr, 5], yr.at[rr, db], rsend, rrecv, s0 + 5, left)

    opposite_step(1)
    attend_back(0, 3 * ROWS, 0, (3,))
    halves_t = dot(wkv[...], dt[:, 0 : 2 * ROWS]).astype(BF16)
    hsend[0] = halves_t[:, :ROWS]
    hsend[1] = halves_t[:, ROWS:]
    c_hd = push(hsend.at[0], hrecv.at[0], rsend, rrecv, 4, down)
    c_hu = push(hsend.at[1], hrecv.at[1], rsend, rrecv, 5, up)
    direct_step(1)
    second_step(1)
    opposite_step(0)
    direct_step(0)

    own_t = dot(wkv[...], dt[:, 2 * ROWS : 3 * ROWS])
    grad_q = jnp.concatenate([head_join(dq[0, hp] + dq[1, hp]) for hp in range(PAIRS)], 1)
    grad_in = dot_t((grad_q * 0.125).astype(BF16), wq[...])
    out_hbm[...] = (residv[...] + dot(actv[...], wd[...])).astype(BF16)

    for slot in (2, 3, 4, 5):
        c_x[1, slot].wait_recv()
    for i, cols in enumerate((da, db)):
        tbuf[i] = (
            summed(x, 1, cols) + yl[1, cols, :].astype(F32) + yr[1, cols, :].astype(F32)
        ).astype(BF16)
        c_x[2, i] = push(tbuf.at[i], ybuf.at[i], rsend, rrecv, 6 + i, across)
    second_step(0)
    c_hd.wait_recv()
    c_hu.wait_recv()
    own_t = own_t + hrecv[0].astype(F32) + hrecv[1].astype(F32)
    for slot in (2, 3, 4, 5):
        c_x[0, slot].wait_recv()
    own_t = own_t + yl[0].astype(F32) + yr[0].astype(F32)
    own_t = own_t + jnp.concatenate([summed(x, 0, da), summed(x, 0, db)], 0)
    grad_in = grad_in + jnp.transpose(own_t)
    unit_b, inv_b = normalize(xv[...].astype(F32))
    c_x[2, 0].wait_recv()
    c_x[2, 1].wait_recv()
    grad_in = grad_in + jnp.transpose(jnp.concatenate([ybuf[0], ybuf[1]], 0).astype(F32))
    gout_hbm[...] = (grad_resid + normalize_back(unit_b, inv_b, grad_in)).astype(BF16)
    for copy in sends:
        copy.wait_send()


def on_device(nodes, experts_list, w_query, w_key, w_value, w_out, w_up, w_down, cotangent):
    rows, width = nodes.shape
    hbm = pl.BlockSpec(memory_space=pltpu.HBM)
    tile = lambda *shape, dtype=BF16: pltpu.VMEM(shape, dtype)
    out = jax.ShapeDtypeStruct((rows, width), BF16)
    vm = pl.BlockSpec(memory_space=pltpu.VMEM)
    return pl.pallas_call(
        kernel,
        out_shape=(out, out),
        in_specs=[pl.BlockSpec(memory_space=pltpu.SMEM)] + [hbm] * 9,
        out_specs=(vm, vm),
        scratch_shapes=[
            tile(ROWS, D),
            tile(ROWS, D),
            tile(D, D),
            tile(D, 2 * D),
            tile(D, D),
            tile(D, FF),
            tile(FF, D),
            tile(16, ROWS, D),
            tile(2, ROWS, D),
            tile(7 * ROWS, 2 * D),
            tile(PAIRS, 2 * ROWS, 128),
            tile(PAIRS, 128, 2 * ROWS),
            tile(PAIRS, 2 * ROWS, 128),
            tile(PAIRS, 128, 2 * ROWS),
            tile(PAIRS, 2 * ROWS, 7 * ROWS, dtype=F32),
            tile(2, PAIRS, 2 * ROWS, 128, dtype=F32),
            tile(2, PAIRS, 2 * ROWS, 128, dtype=F32),
            tile(2, PAIRS, 2 * ROWS, 128, dtype=F32),
            tile(2, PAIRS, 2 * ROWS, 128, dtype=F32),
            tile(ROWS, D),
            tile(PAIRS, 2 * ROWS, 128, dtype=F32),
            tile(2, PAIRS, 2 * ROWS, 128, dtype=F32),
            tile(2 * D, 7 * ROWS),
            tile(5, D, ROWS),
            tile(5, D, ROWS),
            pltpu.SMEM((1, 4), jnp.int32),
            tile(2, D, ROWS),
            tile(2, D, ROWS),
            tile(2, 2, DHALF, ROWS),
            tile(2, D, ROWS),
            tile(2, D, ROWS),
            tile(2, 6, DHALF, ROWS),
            tile(2, DHALF, ROWS),
            tile(2, DHALF, ROWS),
            tile(4 * ROWS, D),
            tile(ROWS, FF),
            tile(ROWS, D, dtype=F32),
            tile(ROWS, FF, dtype=F32),
            pltpu.SemaphoreType.DMA((12,)),
            pltpu.SemaphoreType.DMA((25,)),
            pltpu.SemaphoreType.DMA((25,)),
            pltpu.SemaphoreType.DMA((20,)),
            pltpu.SemaphoreType.DMA((20,)),
        ],
        compiler_params=pltpu.CompilerParams(
            collective_id=0, has_side_effects=True, vmem_limit_bytes=28 * 1024 * 1024
        ),
        name="exphormer",
    )(
        experts_list,
        *(
            pltpu.with_memory_space_constraint(a, pltpu.HBM)
            for a in (nodes, experts_list, w_query, w_key, w_value, w_out, w_up, w_down, cotangent)
        ),
    )


def solution(mesh):
    return jax.shard_map(
        on_device,
        mesh=mesh,
        in_specs=(
            P(("blk", "dom"), None),
            P(("blk", "dom"), None),
            P(),
            P(),
            P(),
            P(),
            P(),
            P(),
            P(("blk", "dom"), None),
        ),
        out_specs=(P(("blk", "dom"), None), P(("blk", "dom"), None)),
        check_vma=False,
    )
```

```python
import functools

import jax
import jax.numpy as jnp
from jax import lax
from jax.experimental import pallas as pl
from jax.experimental.pallas import tpu as pltpu
from jax.sharding import PartitionSpec as P

EPS = 1e-05
MESH = pl.DeviceIdType.MESH
D = 512
FF = 1024
ROWS = 128
HALF = 64
DHALF = 256
PAIRS = 4
F32 = jnp.float32
BF16 = jnp.bfloat16


def normalize(values):
    mean_v = jnp.mean(values, axis=-1, keepdims=True)
    centered = values - mean_v
    inv_std = lax.rsqrt(jnp.mean(centered * centered, axis=-1, keepdims=True) + EPS)
    return (centered * inv_std, inv_std)


def normalize_back(unit, inv_std, upstream):
    return inv_std * (
        upstream
        - jnp.mean(upstream, axis=-1, keepdims=True)
        - unit * jnp.mean(upstream * unit, axis=-1, keepdims=True)
    )


def dot(a, b):
    return jnp.dot(a, b, preferred_element_type=F32)


def dot_t(a, b):
    return lax.dot_general(a, b, (((1,), (1,)), ((), ())), preferred_element_type=F32)


def head_stack(tile):
    low = lax.broadcasted_iota(jnp.int32, tile.shape, 1) < 64
    zero = jnp.zeros_like(tile)
    return jnp.concatenate([jnp.where(low, tile, zero), jnp.where(low, zero, tile)], 0)


def head_join(stacked):
    low = lax.broadcasted_iota(jnp.int32, (ROWS, 128), 1) < 64
    return jnp.where(low, stacked[:ROWS], stacked[ROWS:])


def kernel(
    listed,
    nodes_hbm,
    list_hbm,
    wq_hbm,
    wk_hbm,
    wv_hbm,
    wo_hbm,
    wu_hbm,
    wd_hbm,
    cot_hbm,
    out_hbm,
    gout_hbm,
    xv,
    cotv,
    wq,
    wkv,
    wo,
    wu,
    wd,
    gath,
    halo,
    kv,
    q2,
    q2t,
    g2,
    g2t,
    wexp,
    mstat,
    lstat,
    oacc,
    fstat,
    mixv,
    delt,
    dq,
    dt,
    part,
    psib,
    lsib,
    hsend,
    hrecv,
    xo,
    yl,
    yr,
    sbuf,
    tbuf,
    ybuf,
    nbuf,
    actv,
    residv,
    gact,
    lsem,
    ready,
    gsend,
    grecv,
    rsend,
    rrecv,
):
    blk = lax.axis_index("blk")
    dom = lax.axis_index("dom")
    ndom = lax.axis_size("dom")
    core = blk % 2
    x = (blk // 2) % 4
    h = blk // 8

    def at(xx, hh, cc):
        return hh * 8 + (xx % 4) * 2 + cc

    right = {"blk": at(x + 1, h, core), "dom": dom}
    left = {"blk": at(x + 3, h, core), "dom": dom}
    across = {"blk": at(x, 1 - h, core), "dom": dom}
    twin = {"blk": at(x, h, 1 - core), "dom": dom}
    up = {"blk": blk, "dom": (dom + 1) % ndom}
    down = {"blk": blk, "dom": (dom + ndom - 1) % ndom}

    half = ndom // 2
    z = dom % half
    final = half - 1

    barrier = pltpu.get_barrier_semaphore()

    def greet(peer):
        pl.semaphore_signal(barrier, inc=1, device_id=peer, device_id_type=MESH)

    for peer in (right, left, across, twin):
        greet(peer)

    @pl.when(z < final)
    def _():
        greet(up)

    @pl.when(z == 0)
    def _():
        greet(down)

    pl.semaphore_wait(barrier, 4 + jnp.where(z > 0, 1, 0) + jnp.where(z == final, 1, 0))

    @pl.when(z > 0)
    def _():
        pl.semaphore_signal(ready.at[0], inc=1, device_id=down, device_id_type=MESH)

    @pl.when(z == final)
    def _():
        pl.semaphore_signal(ready.at[1], inc=1, device_id=up, device_id_type=MESH)

    sends = []

    def plan(src, dst, ssems, rsems, slot, peer):
        copy = pltpu.make_async_remote_copy(
            src_ref=src,
            dst_ref=dst,
            send_sem=ssems.at[slot],
            recv_sem=rsems.at[slot],
            device_id=peer,
            device_id_type=MESH,
        )
        sends.append(copy)
        return copy

    def push(*where):
        copy = plan(*where)
        copy.start()
        return copy

    top = pl.ds(0, HALF)
    bottom = pl.ds(HALF, HALF)

    def block(xx, rr):
        return at(xx, rr, core)

    rows_of = (h, 1 - h)

    own = block(x, h)
    c_r = {}
    c_l = {}
    c_y = []
    c_y.append(push(nodes_hbm.at[top], gath.at[own, top], gsend, grecv, 12, across))
    c_r[0, 0] = push(nodes_hbm.at[top], gath.at[own, top], gsend, grecv, 0, right)
    c_l[0, 1] = push(nodes_hbm.at[bottom], gath.at[own, bottom], gsend, grecv, 5, left)
    c_y.append(push(nodes_hbm.at[bottom], gath.at[own, bottom], gsend, grecv, 13, across))
    c_r[0, 1] = push(nodes_hbm.at[bottom], gath.at[own, bottom], gsend, grecv, 1, right)
    c_l[0, 0] = push(nodes_hbm.at[top], gath.at[own, top], gsend, grecv, 4, left)

    loads = []

    def load(src, dst):
        copy = pltpu.make_async_copy(src, dst, lsem.at[len(loads)])
        copy.start()
        loads.append(copy)
        return copy

    ld_x = load(nodes_hbm, xv)
    ld_wk = load(wk_hbm, wkv.at[:, pl.ds(0, D)])
    ld_wv = load(wv_hbm, wkv.at[:, pl.ds(D, D)])
    ld_wq = load(wq_hbm, wq)
    ld_own = load(nodes_hbm, gath.at[own])
    ld_cot = load(cot_hbm, cotv)
    ld_wd = load(wd_hbm, wd)
    ld_wo = load(wo_hbm, wo)
    ld_wu = load(wu_hbm, wu)

    c_list = push(list_hbm, lsib, gsend, grecv, 24, twin)
    c_tw = [push(nodes_hbm, gath.at[own], gsend, grecv, 16, twin)]

    ld_x.wait()
    x_full = xv[...].astype(F32)
    unit, inv_std = normalize(x_full)
    normed = unit.astype(BF16)
    ld_wk.wait()
    ld_wv.wait()
    kv[pl.ds(2 * ROWS, ROWS), :] = dot(normed, wkv[...]).astype(BF16)
    ld_wq.wait()
    queries = dot(normed, wq[...]).astype(BF16) * jnp.asarray(0.125, BF16)
    for hp in range(PAIRS):
        stacked = head_stack(queries[:, hp * 128 : (hp + 1) * 128])
        q2[hp] = stacked
        q2t[hp] = jnp.transpose(stacked)

    fwd_r = [None, None]
    fwd_l = [None, None]

    def forward(rr):
        row = rows_of[rr]
        c_r[rr, 0].wait_recv()
        from_left = block(x + 3, row)
        fwd_r[rr] = push(gath.at[from_left, top], gath.at[from_left, top], gsend, grecv, 8 + rr, right)
        c_l[rr, 1].wait_recv()
        from_right = block(x + 1, row)
        fwd_l[rr] = push(
            gath.at[from_right, bottom], gath.at[from_right, bottom], gsend, grecv, 10 + rr, left
        )

    def to_twin(slot, who):
        c_tw.append(push(gath.at[who], gath.at[who], gsend, grecv, slot, twin))

    c_up = plan(nodes_hbm, halo.at[0], gsend, grecv, 14, up)
    c_dn = plan(nodes_hbm, halo.at[1], gsend, grecv, 15, down)

    @pl.when(z > 0)
    def _():
        c_dn.start()

    @pl.when(z == final)
    def _():
        c_up.start()

    ld_wd.wait()
    ld_cot.wait()
    gact[...] = dot_t(cotv[...], wd[...])
    forward(0)
    other = block(x, 1 - h)
    c_y[0].wait_recv()
    c_r[1, 0] = push(gath.at[other, top], gath.at[other, top], gsend, grecv, 2, right)
    c_l[1, 0] = push(gath.at[other, top], gath.at[other, top], gsend, grecv, 6, left)
    c_y[1].wait_recv()
    c_l[1, 1] = push(gath.at[other, bottom], gath.at[other, bottom], gsend, grecv, 7, left)
    c_r[1, 1] = push(gath.at[other, bottom], gath.at[other, bottom], gsend, grecv, 3, right)
    to_twin(17, other)
    c_r[0, 1].wait_recv()
    to_twin(18, block(x + 3, h))
    c_l[0, 0].wait_recv()
    to_twin(19, block(x + 1, h))

    @pl.when(z < final)
    def _():
        pl.semaphore_wait(ready.at[0], 1)
        c_up.start()


    def project(raw, row0):
        unit_o, _ = normalize(raw.astype(F32))
        kv[pl.ds(row0, ROWS), :] = dot(unit_o.astype(BF16), wkv[...]).astype(BF16)

    def attend(base, count, which, pairs=range(PAIRS)):
        for hp in pairs:
            k = kv[base : base + count, hp * 128 : (hp + 1) * 128]
            v = kv[base : base + count, D + hp * 128 : D + (hp + 1) * 128]
            s = dot_t(q2[hp], k)
            m = jnp.max(s, axis=1, keepdims=True)
            w = jnp.exp(s - m)
            wexp[hp, :, base : base + count] = w
            total = jnp.sum(w, axis=1, keepdims=True)
            oacc[which, hp] = dot(w.astype(BF16), v)
            mstat[which, hp] = jnp.broadcast_to(m, (2 * ROWS, 128))
            lstat[which, hp] = jnp.broadcast_to(total, (2 * ROWS, 128))

    forward(1)
    fwd_r[0].wait_recv()
    fwd_l[0].wait_recv()
    to_twin(22, block(x + 2, h))
    @pl.when(z == 0)
    def _():
        pl.semaphore_wait(ready.at[1], 1)
        c_dn.start()

    c_up.wait_recv()
    project(halo[0], 0)
    c_dn.wait_recv()
    project(halo[1], ROWS)
    c_r[1, 1].wait_recv()
    to_twin(20, block(x + 3, 1 - h))
    c_l[1, 0].wait_recv()
    to_twin(21, block(x + 1, 1 - h))
    attend(0, 3 * ROWS, 0)
    fwd_r[1].wait_recv()
    fwd_l[1].wait_recv()
    to_twin(23, block(x + 2, 1 - h))
    for copy in c_tw:
        copy.wait_recv()
    c_list.wait_recv()
    ld_own.wait()

    for e in range(4):
        unit_e, _ = normalize(gath[listed[0, e]].astype(F32))
        nbuf[e * ROWS : (e + 1) * ROWS] = unit_e.astype(BF16)
    kv[3 * ROWS : 7 * ROWS, :] = dot(nbuf[...], wkv[...]).astype(BF16)
    attend(3 * ROWS, 4 * ROWS, 1)

    for hp in range(PAIRS):
        m0, m1 = mstat[0, hp], mstat[1, hp]
        m = jnp.maximum(m0, m1)
        a0, a1 = jnp.exp(m0 - m), jnp.exp(m1 - m)
        inv = 1.0 / (a0 * lstat[0, hp] + a1 * lstat[1, hp])
        f0, f1 = a0 * inv, a1 * inv
        fstat[0, hp] = f0
        fstat[1, hp] = f1
        o = oacc[0, hp] * f0 + oacc[1, hp] * f1
        mixv[:, hp * 128 : (hp + 1) * 128] = head_join(o).astype(BF16)

    ld_wo.wait()
    mixed = mixv[...]
    resid = xv[...].astype(F32) + dot(mixed, wo[...])
    unit2, inv_std2 = normalize(resid)
    ld_wu.wait()
    pre = dot(unit2.astype(BF16), wu[...])
    cot = cotv[...]
    c0 = 0.7978845608028654
    sq = pre * pre
    th = jnp.tanh(c0 * (pre + 0.044715 * (sq * pre)))
    act = 0.5 * pre * (1.0 + th)
    slope = 0.5 * (1.0 + th) + 0.5 * pre * (1.0 - th * th) * (c0 * (1.0 + 3.0 * 0.044715 * sq))
    actv[...] = act.astype(BF16)
    residv[...] = resid
    grad_pre = (gact[...] * slope).astype(BF16)
    grad_norm2 = dot_t(grad_pre, wu[...])
    grad_resid = cot.astype(F32) + normalize_back(unit2, inv_std2, grad_norm2)
    grad_mixed = dot_t(grad_resid.astype(BF16), wo[...]).astype(BF16)
    for hp in range(PAIRS):
        stacked = head_stack(grad_mixed[:, hp * 128 : (hp + 1) * 128])
        g2[hp] = stacked
        g2t[hp] = jnp.transpose(stacked)
        mixed_pair = mixed[:, hp * 128 : (hp + 1) * 128].astype(F32)
        both = jnp.concatenate([mixed_pair, mixed_pair], 0)
        d = jnp.sum(stacked.astype(F32) * both, axis=1, keepdims=True)
        delt[hp] = jnp.broadcast_to(d, (2 * ROWS, 128))

    def attend_back(base, count, which, pairs=range(PAIRS)):
        for hp in pairs:
            k = kv[base : base + count, hp * 128 : (hp + 1) * 128]
            v = kv[base : base + count, D + hp * 128 : D + (hp + 1) * 128]
            p = wexp[hp, :, base : base + count] * fstat[which, hp][:, :1]
            dp = dot_t(g2[hp], v)
            ds = (p * (dp - delt[hp][:, :1])).astype(BF16)
            dt[hp * 128 : (hp + 1) * 128, base : base + count] = dot(q2t[hp], ds).astype(BF16)
            dt[D + hp * 128 : D + (hp + 1) * 128, base : base + count] = dot(
                g2t[hp], p.astype(BF16)
            ).astype(BF16)
            dq[which, hp] = dot(ds, k)

    attend_back(3 * ROWS, 4 * ROWS, 1)

    zero_block = jnp.zeros((D, ROWS), BF16)
    part[4] = zero_block
    psib[4] = zero_block
    c_ps = []
    for e in (0, 2):
        both = dot(wkv[...], dt[:, (3 + e) * ROWS : (5 + e) * ROWS]).astype(BF16)
        part[e] = both[:, :ROWS]
        part[e + 1] = both[:, ROWS:]
        c_ps.append(push(part.at[e], psib.at[e], rsend, rrecv, e, twin))
        c_ps.append(push(part.at[e + 1], psib.at[e + 1], rsend, rrecv, e + 1, twin))

    attend_back(0, 3 * ROWS, 0, (0, 1, 2))
    for copy in c_ps:
        copy.wait_recv()

    def slot_of(lists, target):
        slot = jnp.int32(4)
        for e in range(4):
            slot = jnp.where(lists[0, e] == target, jnp.int32(e), slot)
        return slot

    def summed(xx, rr, cols):
        target = block(xx, rows_of[rr])
        return (
            part[slot_of(listed, target), cols, :].astype(F32)
            + psib[slot_of(lsib, target), cols, :].astype(F32)
        )

    da = pl.ds(0, DHALF)
    db = pl.ds(DHALF, DHALF)

    c_x = {}

    def opposite_step(rr):
        s0 = 8 + 6 * rr
        sbuf[rr, 0] = summed(x + 2, rr, da).astype(BF16)
        c_x[rr, 0] = push(sbuf.at[rr, 0], xo.at[rr, 0], rsend, rrecv, s0, right)
        sbuf[rr, 1] = summed(x + 2, rr, db).astype(BF16)
        c_x[rr, 1] = push(sbuf.at[rr, 1], xo.at[rr, 1], rsend, rrecv, s0 + 1, left)

    def direct_step(rr):
        s0 = 8 + 6 * rr
        sbuf[rr, 2] = summed(x + 1, rr, db).astype(BF16)
        c_x[rr, 2] = push(sbuf.at[rr, 2], yl.at[rr, db], rsend, rrecv, s0 + 2, right)
        sbuf[rr, 3] = summed(x + 3, rr, da).astype(BF16)
        c_x[rr, 3] = push(sbuf.at[rr, 3], yr.at[rr, da], rsend, rrecv, s0 + 3, left)

    def second_step(rr):
        s0 = 8 + 6 * rr
        c_x[rr, 0].wait_recv()
        sbuf[rr, 4] = (summed(x + 1, rr, da) + xo[rr, 0].astype(F32)).astype(BF16)
        c_x[rr, 4] = push(sbuf.at[rr, 4], yl.at[rr, da], rsend, rrecv, s0 + 4, right)
        c_x[rr, 1].wait_recv()
        sbuf[rr, 5] = (summed(x + 3, rr, db) + xo[rr, 1].astype(F32)).astype(BF16)
        c_x[rr, 5] = push(sbuf.at[rr, 5], yr.at[rr, db], rsend, rrecv, s0 + 5, left)

    opposite_step(1)
    attend_back(0, 3 * ROWS, 0, (3,))
    halves_t = dot(wkv[...], dt[:, 0 : 2 * ROWS]).astype(BF16)
    hsend[0] = halves_t[:, :ROWS]
    hsend[1] = halves_t[:, ROWS:]
    c_hd = push(hsend.at[0], hrecv.at[0], rsend, rrecv, 4, down)
    c_hu = push(hsend.at[1], hrecv.at[1], rsend, rrecv, 5, up)
    direct_step(1)
    second_step(1)
    opposite_step(0)
    direct_step(0)

    own_t = dot(wkv[...], dt[:, 2 * ROWS : 3 * ROWS])
    grad_q = jnp.concatenate([head_join(dq[0, hp] + dq[1, hp]) for hp in range(PAIRS)], 1)
    grad_in = dot_t((grad_q * 0.125).astype(BF16), wq[...])
    out_hbm[...] = (residv[...] + dot(actv[...], wd[...])).astype(BF16)

    for slot in (2, 3, 4, 5):
        c_x[1, slot].wait_recv()
    for i, cols in enumerate((da, db)):
        tbuf[i] = (
            summed(x, 1, cols) + yl[1, cols, :].astype(F32) + yr[1, cols, :].astype(F32)
        ).astype(BF16)
        c_x[2, i] = push(tbuf.at[i], ybuf.at[i], rsend, rrecv, 6 + i, across)
    second_step(0)
    c_hd.wait_recv()
    c_hu.wait_recv()
    own_t = own_t + hrecv[0].astype(F32) + hrecv[1].astype(F32)
    for slot in (2, 3, 4, 5):
        c_x[0, slot].wait_recv()
    own_t = own_t + yl[0].astype(F32) + yr[0].astype(F32)
    own_t = own_t + jnp.concatenate([summed(x, 0, da), summed(x, 0, db)], 0)
    grad_in = grad_in + jnp.transpose(own_t)
    unit_b, inv_b = normalize(xv[...].astype(F32))
    c_x[2, 0].wait_recv()
    c_x[2, 1].wait_recv()
    grad_in = grad_in + jnp.transpose(jnp.concatenate([ybuf[0], ybuf[1]], 0).astype(F32))
    gout_hbm[...] = (grad_resid + normalize_back(unit_b, inv_b, grad_in)).astype(BF16)
    for copy in sends:
        copy.wait_send()


def on_device(nodes, experts_list, w_query, w_key, w_value, w_out, w_up, w_down, cotangent):
    rows, width = nodes.shape
    hbm = pl.BlockSpec(memory_space=pltpu.HBM)
    tile = lambda *shape, dtype=BF16: pltpu.VMEM(shape, dtype)
    out = jax.ShapeDtypeStruct((rows, width), BF16)
    vm = pl.BlockSpec(memory_space=pltpu.VMEM)
    return pl.pallas_call(
        kernel,
        out_shape=(out, out),
        in_specs=[pl.BlockSpec(memory_space=pltpu.SMEM)] + [hbm] * 9,
        out_specs=(vm, vm),
        scratch_shapes=[
            tile(ROWS, D),
            tile(ROWS, D),
            tile(D, D),
            tile(D, 2 * D),
            tile(D, D),
            tile(D, FF),
            tile(FF, D),
            tile(16, ROWS, D),
            tile(2, ROWS, D),
            tile(7 * ROWS, 2 * D),
            tile(PAIRS, 2 * ROWS, 128),
            tile(PAIRS, 128, 2 * ROWS),
            tile(PAIRS, 2 * ROWS, 128),
            tile(PAIRS, 128, 2 * ROWS),
            tile(PAIRS, 2 * ROWS, 7 * ROWS, dtype=F32),
            tile(2, PAIRS, 2 * ROWS, 128, dtype=F32),
            tile(2, PAIRS, 2 * ROWS, 128, dtype=F32),
            tile(2, PAIRS, 2 * ROWS, 128, dtype=F32),
            tile(2, PAIRS, 2 * ROWS, 128, dtype=F32),
            tile(ROWS, D),
            tile(PAIRS, 2 * ROWS, 128, dtype=F32),
            tile(2, PAIRS, 2 * ROWS, 128, dtype=F32),
            tile(2 * D, 7 * ROWS),
            tile(5, D, ROWS),
            tile(5, D, ROWS),
            pltpu.SMEM((1, 4), jnp.int32),
            tile(2, D, ROWS),
            tile(2, D, ROWS),
            tile(2, 2, DHALF, ROWS),
            tile(2, D, ROWS),
            tile(2, D, ROWS),
            tile(2, 6, DHALF, ROWS),
            tile(2, DHALF, ROWS),
            tile(2, DHALF, ROWS),
            tile(4 * ROWS, D),
            tile(ROWS, FF),
            tile(ROWS, D, dtype=F32),
            tile(ROWS, FF, dtype=F32),
            pltpu.SemaphoreType.DMA((9,)),
            pltpu.SemaphoreType.REGULAR((2,)),
            pltpu.SemaphoreType.DMA((25,)),
            pltpu.SemaphoreType.DMA((25,)),
            pltpu.SemaphoreType.DMA((20,)),
            pltpu.SemaphoreType.DMA((20,)),
        ],
        compiler_params=pltpu.CompilerParams(
            collective_id=0, has_side_effects=True, vmem_limit_bytes=28 * 1024 * 1024
        ),
        name="exphormer",
    )(
        experts_list,
        *(
            pltpu.with_memory_space_constraint(a, pltpu.HBM)
            for a in (nodes, experts_list, w_query, w_key, w_value, w_out, w_up, w_down, cotangent)
        ),
    )


def solution(mesh):
    return jax.shard_map(
        on_device,
        mesh=mesh,
        in_specs=(
            P(("blk", "dom"), None),
            P(("blk", "dom"), None),
            P(),
            P(),
            P(),
            P(),
            P(),
            P(),
            P(("blk", "dom"), None),
        ),
        out_specs=(P(("blk", "dom"), None), P(("blk", "dom"), None)),
        check_vma=False,
    )
```

```python
import functools

import jax
import jax.numpy as jnp
from jax import lax
from jax.experimental import pallas as pl
from jax.experimental.pallas import tpu as pltpu
from jax.sharding import PartitionSpec as P

EPS = 1e-05
MESH = pl.DeviceIdType.MESH
D = 512
FF = 1024
ROWS = 128
HALF = 64
DHALF = 256
PAIRS = 4
F32 = jnp.float32
BF16 = jnp.bfloat16


def normalize(values):
    mean_v = jnp.mean(values, axis=-1, keepdims=True)
    centered = values - mean_v
    inv_std = lax.rsqrt(jnp.mean(centered * centered, axis=-1, keepdims=True) + EPS)
    return (centered * inv_std, inv_std)


def normalize_back(unit, inv_std, upstream):
    return inv_std * (
        upstream
        - jnp.mean(upstream, axis=-1, keepdims=True)
        - unit * jnp.mean(upstream * unit, axis=-1, keepdims=True)
    )


def dot(a, b):
    return jnp.dot(a, b, preferred_element_type=F32)


def dot_t(a, b):
    return lax.dot_general(a, b, (((1,), (1,)), ((), ())), preferred_element_type=F32)


def head_stack(tile):
    low = lax.broadcasted_iota(jnp.int32, tile.shape, 1) < 64
    zero = jnp.zeros_like(tile)
    return jnp.concatenate([jnp.where(low, tile, zero), jnp.where(low, zero, tile)], 0)


def head_join(stacked):
    low = lax.broadcasted_iota(jnp.int32, (ROWS, 128), 1) < 64
    return jnp.where(low, stacked[:ROWS], stacked[ROWS:])


def kernel(
    listed,
    nodes_hbm,
    list_hbm,
    wq_hbm,
    wk_hbm,
    wv_hbm,
    wo_hbm,
    wu_hbm,
    wd_hbm,
    cot_hbm,
    out_hbm,
    gout_hbm,
    xv,
    cotv,
    wq,
    wkv,
    wo,
    wu,
    wd,
    gath,
    halo,
    kv,
    q2,
    q2t,
    g2,
    g2t,
    dpv,
    pbv,
    dsv,
    wexp,
    mstat,
    lstat,
    oacc,
    fstat,
    mixv,
    delt,
    dq,
    dt,
    part,
    psib,
    lsib,
    hsend,
    hrecv,
    xo,
    yl,
    yr,
    sbuf,
    tbuf,
    ybuf,
    nbuf,
    actv,
    residv,
    gact,
    lsem,
    ready,
    ssem,
    grecv,
    rrecv,
):
    blk = lax.axis_index("blk")
    dom = lax.axis_index("dom")
    ndom = lax.axis_size("dom")
    core = blk % 2
    x = (blk // 2) % 4
    h = blk // 8

    def at(xx, hh, cc):
        return hh * 8 + (xx % 4) * 2 + cc

    right = {"blk": at(x + 1, h, core), "dom": dom}
    left = {"blk": at(x + 3, h, core), "dom": dom}
    across = {"blk": at(x, 1 - h, core), "dom": dom}
    twin = {"blk": at(x, h, 1 - core), "dom": dom}
    up = {"blk": blk, "dom": (dom + 1) % ndom}
    down = {"blk": blk, "dom": (dom + ndom - 1) % ndom}

    half = ndom // 2
    z = dom % half
    final = half - 1

    barrier = pltpu.get_barrier_semaphore()

    def greet(peer):
        pl.semaphore_signal(barrier, inc=1, device_id=peer, device_id_type=MESH)

    for peer in (right, left, across, twin):
        greet(peer)

    @pl.when(z < final)
    def _():
        greet(up)

    @pl.when(z == 0)
    def _():
        greet(down)

    pl.semaphore_wait(barrier, 4 + jnp.where(z > 0, 1, 0) + jnp.where(z == final, 1, 0))

    @pl.when(z > 0)
    def _():
        pl.semaphore_signal(ready.at[0], inc=1, device_id=down, device_id_type=MESH)

    @pl.when(z == final)
    def _():
        pl.semaphore_signal(ready.at[1], inc=1, device_id=up, device_id_type=MESH)

    sends = []

    pool = list(range(19))

    def plan(src, dst, rsems, slot, peer):
        index = pool.pop(0)
        copy = pltpu.make_async_remote_copy(
            src_ref=src,
            dst_ref=dst,
            send_sem=ssem.at[index],
            recv_sem=rsems.at[slot],
            device_id=peer,
            device_id_type=MESH,
        )
        sends.append((copy, index))
        return copy

    def reclaim(keep=()):
        held = [entry for entry in sends if any(entry[0] is copy for copy in keep)]
        for copy, index in sends:
            if not any(copy is entry[0] for entry in held):
                copy.wait_send()
                pool.append(index)
        sends[:] = held

    def push(*where):
        copy = plan(*where)
        copy.start()
        return copy

    top = pl.ds(0, HALF)
    bottom = pl.ds(HALF, HALF)

    def block(xx, rr):
        return at(xx, rr, core)

    rows_of = (h, 1 - h)

    own = block(x, h)
    c_r = {}
    c_l = {}
    c_y = []
    c_y.append(push(nodes_hbm.at[top], gath.at[own, top], grecv, 12, across))
    c_r[0, 0] = push(nodes_hbm.at[top], gath.at[own, top], grecv, 0, right)
    c_l[0, 1] = push(nodes_hbm.at[bottom], gath.at[own, bottom], grecv, 5, left)
    c_y.append(push(nodes_hbm.at[bottom], gath.at[own, bottom], grecv, 13, across))
    c_r[0, 1] = push(nodes_hbm.at[bottom], gath.at[own, bottom], grecv, 1, right)
    c_l[0, 0] = push(nodes_hbm.at[top], gath.at[own, top], grecv, 4, left)

    loads = []

    def load(src, dst):
        copy = pltpu.make_async_copy(src, dst, lsem.at[len(loads)])
        copy.start()
        loads.append(copy)
        return copy

    ld_x = load(nodes_hbm, xv)
    ld_wk = load(wk_hbm, wkv.at[:, pl.ds(0, D)])
    ld_wv = load(wv_hbm, wkv.at[:, pl.ds(D, D)])
    ld_wq = load(wq_hbm, wq)
    ld_own = load(nodes_hbm, gath.at[own])
    ld_cot = load(cot_hbm, cotv)
    ld_wd = load(wd_hbm, wd)
    ld_wo = load(wo_hbm, wo)
    ld_wu = load(wu_hbm, wu)

    c_list = push(list_hbm, lsib, grecv, 24, twin)
    c_tw = [push(nodes_hbm, gath.at[own], grecv, 16, twin)]

    ld_x.wait()
    x_full = xv[...].astype(F32)
    unit, inv_std = normalize(x_full)
    normed = unit.astype(BF16)
    ld_wk.wait()
    ld_wv.wait()
    kv[pl.ds(2 * ROWS, ROWS), :] = dot(normed, wkv[...]).astype(BF16)
    ld_wq.wait()
    queries = dot(normed, wq[...]).astype(BF16) * jnp.asarray(0.125, BF16)
    for hp in range(PAIRS):
        stacked = head_stack(queries[:, hp * 128 : (hp + 1) * 128])
        q2[hp] = stacked
        q2t[hp] = jnp.transpose(stacked)

    fwd_r = [None, None]
    fwd_l = [None, None]

    def forward(rr):
        row = rows_of[rr]
        c_r[rr, 0].wait_recv()
        from_left = block(x + 3, row)
        fwd_r[rr] = push(gath.at[from_left, top], gath.at[from_left, top], grecv, 8 + rr, right)
        c_l[rr, 1].wait_recv()
        from_right = block(x + 1, row)
        fwd_l[rr] = push(
            gath.at[from_right, bottom], gath.at[from_right, bottom], grecv, 10 + rr, left
        )

    def to_twin(slot, who):
        c_tw.append(push(gath.at[who], gath.at[who], grecv, slot, twin))

    c_up = plan(nodes_hbm, halo.at[0], grecv, 14, up)
    c_dn = plan(nodes_hbm, halo.at[1], grecv, 15, down)

    @pl.when(z > 0)
    def _():
        c_dn.start()

    @pl.when(z == final)
    def _():
        c_up.start()

    ld_wd.wait()
    ld_cot.wait()
    gact[...] = dot_t(cotv[...], wd[...])
    forward(0)
    other = block(x, 1 - h)
    c_y[0].wait_recv()
    c_r[1, 0] = push(gath.at[other, top], gath.at[other, top], grecv, 2, right)
    c_l[1, 0] = push(gath.at[other, top], gath.at[other, top], grecv, 6, left)
    c_y[1].wait_recv()
    c_l[1, 1] = push(gath.at[other, bottom], gath.at[other, bottom], grecv, 7, left)
    c_r[1, 1] = push(gath.at[other, bottom], gath.at[other, bottom], grecv, 3, right)
    to_twin(17, other)
    c_r[0, 1].wait_recv()
    to_twin(18, block(x + 3, h))
    c_l[0, 0].wait_recv()
    to_twin(19, block(x + 1, h))

    @pl.when(z < final)
    def _():
        pl.semaphore_wait(ready.at[0], 1)
        c_up.start()


    def project(raw, row0):
        unit_o, _ = normalize(raw.astype(F32))
        kv[pl.ds(row0, ROWS), :] = dot(unit_o.astype(BF16), wkv[...]).astype(BF16)

    def attend(base, count, which, pairs=range(PAIRS)):
        for hp in pairs:
            k = kv[base : base + count, hp * 128 : (hp + 1) * 128]
            wexp[hp, :, base : base + count] = dot_t(q2[hp], k)
        for hp in pairs:
            s = wexp[hp, :, base : base + count]
            m = jnp.max(s, axis=1, keepdims=True)
            w = jnp.exp(s - m)
            wexp[hp, :, base : base + count] = w
            total = jnp.sum(w, axis=1, keepdims=True)
            mstat[which, hp] = jnp.broadcast_to(m, (2 * ROWS, 128))
            lstat[which, hp] = jnp.broadcast_to(total, (2 * ROWS, 128))
        for hp in pairs:
            v = kv[base : base + count, D + hp * 128 : D + (hp + 1) * 128]
            oacc[which, hp] = dot(wexp[hp, :, base : base + count].astype(BF16), v)

    reclaim([copy for copy, _ in sends[8:]])
    forward(1)
    fwd_r[0].wait_recv()
    fwd_l[0].wait_recv()
    to_twin(22, block(x + 2, h))
    @pl.when(z == 0)
    def _():
        pl.semaphore_wait(ready.at[1], 1)
        c_dn.start()

    c_up.wait_recv()
    project(halo[0], 0)
    c_dn.wait_recv()
    project(halo[1], ROWS)
    c_r[1, 1].wait_recv()
    to_twin(20, block(x + 3, 1 - h))
    c_l[1, 0].wait_recv()
    to_twin(21, block(x + 1, 1 - h))
    attend(0, 3 * ROWS, 0)
    fwd_r[1].wait_recv()
    fwd_l[1].wait_recv()
    to_twin(23, block(x + 2, 1 - h))
    for copy in c_tw:
        copy.wait_recv()
    c_list.wait_recv()
    ld_own.wait()

    for e in range(4):
        unit_e, _ = normalize(gath[listed[0, e]].astype(F32))
        nbuf[e * ROWS : (e + 1) * ROWS] = unit_e.astype(BF16)
    kv[3 * ROWS : 7 * ROWS, :] = dot(nbuf[...], wkv[...]).astype(BF16)
    attend(3 * ROWS, 4 * ROWS, 1)

    for hp in range(PAIRS):
        m0, m1 = mstat[0, hp], mstat[1, hp]
        m = jnp.maximum(m0, m1)
        a0, a1 = jnp.exp(m0 - m), jnp.exp(m1 - m)
        inv = 1.0 / (a0 * lstat[0, hp] + a1 * lstat[1, hp])
        f0, f1 = a0 * inv, a1 * inv
        fstat[0, hp] = f0
        fstat[1, hp] = f1
        o = oacc[0, hp] * f0 + oacc[1, hp] * f1
        mixv[:, hp * 128 : (hp + 1) * 128] = head_join(o).astype(BF16)

    ld_wo.wait()
    mixed = mixv[...]
    resid = xv[...].astype(F32) + dot(mixed, wo[...])
    unit2, inv_std2 = normalize(resid)
    ld_wu.wait()
    pre = dot(unit2.astype(BF16), wu[...])
    cot = cotv[...]
    c0 = 0.7978845608028654
    sq = pre * pre
    th = jnp.tanh(c0 * (pre + 0.044715 * (sq * pre)))
    act = 0.5 * pre * (1.0 + th)
    slope = 0.5 * (1.0 + th) + 0.5 * pre * (1.0 - th * th) * (c0 * (1.0 + 3.0 * 0.044715 * sq))
    actv[...] = act.astype(BF16)
    residv[...] = resid
    grad_pre = (gact[...] * slope).astype(BF16)
    grad_norm2 = dot_t(grad_pre, wu[...])
    grad_resid = cot.astype(F32) + normalize_back(unit2, inv_std2, grad_norm2)
    grad_mixed = dot_t(grad_resid.astype(BF16), wo[...]).astype(BF16)
    for hp in range(PAIRS):
        stacked = head_stack(grad_mixed[:, hp * 128 : (hp + 1) * 128])
        g2[hp] = stacked
        g2t[hp] = jnp.transpose(stacked)
        mixed_pair = mixed[:, hp * 128 : (hp + 1) * 128].astype(F32)
        both = jnp.concatenate([mixed_pair, mixed_pair], 0)
        d = jnp.sum(stacked.astype(F32) * both, axis=1, keepdims=True)
        delt[hp] = jnp.broadcast_to(d, (2 * ROWS, 128))

    def attend_back(base, count, which):
        tiles = count // 128
        for hp in range(PAIRS):
            v = kv[base : base + count, D + hp * 128 : D + (hp + 1) * 128]
            dpv[hp, :, :count] = dot_t(g2[hp], v)
        for hp in range(PAIRS):
            scale = jnp.concatenate([fstat[which, hp]] * tiles, 1)
            shift = jnp.concatenate([delt[hp]] * tiles, 1)
            p = wexp[hp, :, base : base + count] * scale
            pbv[hp, :, :count] = p.astype(BF16)
            dsv[hp, :, :count] = (p * (dpv[hp, :, :count] - shift)).astype(BF16)
        for hp in range(PAIRS):
            dt[D + hp * 128 : D + (hp + 1) * 128, base : base + count] = dot(
                g2t[hp], pbv[hp, :, :count]
            ).astype(BF16)
            dt[hp * 128 : (hp + 1) * 128, base : base + count] = dot(
                q2t[hp], dsv[hp, :, :count]
            ).astype(BF16)
            k = kv[base : base + count, hp * 128 : (hp + 1) * 128]
            dq[which, hp] = dot(dsv[hp, :, :count], k)

    attend_back(3 * ROWS, 4 * ROWS, 1)

    reclaim((c_up, c_dn))
    zero_block = jnp.zeros((D, ROWS), BF16)
    part[4] = zero_block
    psib[4] = zero_block
    c_ps = []
    da = pl.ds(0, DHALF)
    db = pl.ds(DHALF, DHALF)
    first4 = pl.ds(0, 4)
    for i, cols in enumerate((da, db)):
        every = dot(wkv[cols, :], dt[:, 3 * ROWS : 7 * ROWS]).astype(BF16)
        for e in range(4):
            part[e, cols, :] = every[:, e * ROWS : (e + 1) * ROWS]
        c_ps.append(
            push(part.at[first4, cols], psib.at[first4, cols], rrecv, i, twin)
        )

    attend_back(0, 3 * ROWS, 0)
    for copy in c_ps:
        copy.wait_recv()

    def slot_of(lists, target):
        slot = jnp.int32(4)
        for e in range(4):
            slot = jnp.where(lists[0, e] == target, jnp.int32(e), slot)
        return slot

    def summed(xx, rr, cols):
        target = block(xx, rows_of[rr])
        return (
            part[slot_of(listed, target), cols, :].astype(F32)
            + psib[slot_of(lsib, target), cols, :].astype(F32)
        )

    c_x = {}

    def opposite_step(rr):
        s0 = 5 + 6 * rr
        sbuf[rr, 0] = summed(x + 2, rr, da).astype(BF16)
        c_x[rr, 0] = push(sbuf.at[rr, 0], xo.at[rr, 0], rrecv, s0, right)
        sbuf[rr, 1] = summed(x + 2, rr, db).astype(BF16)
        c_x[rr, 1] = push(sbuf.at[rr, 1], xo.at[rr, 1], rrecv, s0 + 1, left)

    def direct_step(rr):
        s0 = 5 + 6 * rr
        sbuf[rr, 2] = summed(x + 1, rr, db).astype(BF16)
        c_x[rr, 2] = push(sbuf.at[rr, 2], yl.at[rr, db], rrecv, s0 + 2, right)
        sbuf[rr, 3] = summed(x + 3, rr, da).astype(BF16)
        c_x[rr, 3] = push(sbuf.at[rr, 3], yr.at[rr, da], rrecv, s0 + 3, left)

    def second_step(rr):
        s0 = 5 + 6 * rr
        c_x[rr, 0].wait_recv()
        sbuf[rr, 4] = (summed(x + 1, rr, da) + xo[rr, 0].astype(F32)).astype(BF16)
        c_x[rr, 4] = push(sbuf.at[rr, 4], yl.at[rr, da], rrecv, s0 + 4, right)
        c_x[rr, 1].wait_recv()
        sbuf[rr, 5] = (summed(x + 3, rr, db) + xo[rr, 1].astype(F32)).astype(BF16)
        c_x[rr, 5] = push(sbuf.at[rr, 5], yr.at[rr, db], rrecv, s0 + 5, left)

    opposite_step(1)
    halves_t = dot(wkv[...], dt[:, 0 : 2 * ROWS]).astype(BF16)
    hsend[0] = halves_t[:, :ROWS]
    hsend[1] = halves_t[:, ROWS:]
    c_hd = push(hsend.at[0], hrecv.at[0], rrecv, 2, down)
    c_hu = push(hsend.at[1], hrecv.at[1], rrecv, 3, up)
    direct_step(1)
    second_step(1)
    opposite_step(0)
    direct_step(0)

    own_t = dot(wkv[...], dt[:, 2 * ROWS : 3 * ROWS])
    grad_q = jnp.concatenate([head_join(dq[0, hp] + dq[1, hp]) for hp in range(PAIRS)], 1)
    grad_in = dot_t((grad_q * 0.125).astype(BF16), wq[...])
    out_hbm[...] = (residv[...] + dot(actv[...], wd[...])).astype(BF16)

    for slot in (2, 3, 4, 5):
        c_x[1, slot].wait_recv()
    for cols in (da, db):
        tbuf[cols] = (
            summed(x, 1, cols) + yl[1, cols, :].astype(F32) + yr[1, cols, :].astype(F32)
        ).astype(BF16)
    c_t = push(tbuf, ybuf, rrecv, 4, across)
    second_step(0)
    c_hd.wait_recv()
    c_hu.wait_recv()
    own_t = own_t + hrecv[0].astype(F32) + hrecv[1].astype(F32)
    for slot in (2, 3, 4, 5):
        c_x[0, slot].wait_recv()
    own_t = own_t + yl[0].astype(F32) + yr[0].astype(F32)
    own_t = own_t + jnp.concatenate([summed(x, 0, da), summed(x, 0, db)], 0)
    grad_in = grad_in + jnp.transpose(own_t)
    unit_b, inv_b = normalize(xv[...].astype(F32))
    c_t.wait_recv()
    grad_in = grad_in + jnp.transpose(ybuf[...].astype(F32))
    gout_hbm[...] = (grad_resid + normalize_back(unit_b, inv_b, grad_in)).astype(BF16)
    reclaim()


def on_device(nodes, experts_list, w_query, w_key, w_value, w_out, w_up, w_down, cotangent):
    rows, width = nodes.shape
    hbm = pl.BlockSpec(memory_space=pltpu.HBM)
    tile = lambda *shape, dtype=BF16: pltpu.VMEM(shape, dtype)
    out = jax.ShapeDtypeStruct((rows, width), BF16)
    vm = pl.BlockSpec(memory_space=pltpu.VMEM)
    return pl.pallas_call(
        kernel,
        out_shape=(out, out),
        in_specs=[pl.BlockSpec(memory_space=pltpu.SMEM)] + [hbm] * 9,
        out_specs=(vm, vm),
        scratch_shapes=[
            tile(ROWS, D),
            tile(ROWS, D),
            tile(D, D),
            tile(D, 2 * D),
            tile(D, D),
            tile(D, FF),
            tile(FF, D),
            tile(16, ROWS, D),
            tile(2, ROWS, D),
            tile(7 * ROWS, 2 * D),
            tile(PAIRS, 2 * ROWS, 128),
            tile(PAIRS, 128, 2 * ROWS),
            tile(PAIRS, 2 * ROWS, 128),
            tile(PAIRS, 128, 2 * ROWS),
            tile(PAIRS, 2 * ROWS, 4 * ROWS, dtype=F32),
            tile(PAIRS, 2 * ROWS, 4 * ROWS),
            tile(PAIRS, 2 * ROWS, 4 * ROWS),
            tile(PAIRS, 2 * ROWS, 7 * ROWS, dtype=F32),
            tile(2, PAIRS, 2 * ROWS, 128, dtype=F32),
            tile(2, PAIRS, 2 * ROWS, 128, dtype=F32),
            tile(2, PAIRS, 2 * ROWS, 128, dtype=F32),
            tile(2, PAIRS, 2 * ROWS, 128, dtype=F32),
            tile(ROWS, D),
            tile(PAIRS, 2 * ROWS, 128, dtype=F32),
            tile(2, PAIRS, 2 * ROWS, 128, dtype=F32),
            tile(2 * D, 7 * ROWS),
            tile(5, D, ROWS),
            tile(5, D, ROWS),
            pltpu.SMEM((1, 4), jnp.int32),
            tile(2, D, ROWS),
            tile(2, D, ROWS),
            tile(2, 2, DHALF, ROWS),
            tile(2, D, ROWS),
            tile(2, D, ROWS),
            tile(2, 6, DHALF, ROWS),
            tile(D, ROWS),
            tile(D, ROWS),
            tile(4 * ROWS, D),
            tile(ROWS, FF),
            tile(ROWS, D, dtype=F32),
            tile(ROWS, FF, dtype=F32),
            pltpu.SemaphoreType.DMA((9,)),
            pltpu.SemaphoreType.REGULAR((2,)),
            pltpu.SemaphoreType.DMA((19,)),
            pltpu.SemaphoreType.DMA((25,)),
            pltpu.SemaphoreType.DMA((17,)),
        ],
        compiler_params=pltpu.CompilerParams(
            collective_id=0, has_side_effects=True, vmem_limit_bytes=28 * 1024 * 1024
        ),
        name="exphormer",
    )(
        experts_list,
        *(
            pltpu.with_memory_space_constraint(a, pltpu.HBM)
            for a in (nodes, experts_list, w_query, w_key, w_value, w_out, w_up, w_down, cotangent)
        ),
    )


def solution(mesh):
    return jax.shard_map(
        on_device,
        mesh=mesh,
        in_specs=(
            P(("blk", "dom"), None),
            P(("blk", "dom"), None),
            P(),
            P(),
            P(),
            P(),
            P(),
            P(),
            P(("blk", "dom"), None),
        ),
        out_specs=(P(("blk", "dom"), None), P(("blk", "dom"), None)),
        check_vma=False,
    )
```

```python
import functools

import jax
import jax.numpy as jnp
from jax import lax
from jax.experimental import pallas as pl
from jax.experimental.pallas import tpu as pltpu
from jax.sharding import PartitionSpec as P

EPS = 1e-05
MESH = pl.DeviceIdType.MESH
D = 512
FF = 1024
ROWS = 128
HALF = 64
DHALF = 256
PAIRS = 4
F32 = jnp.float32
BF16 = jnp.bfloat16


def normalize(values):
    mean_v = jnp.mean(values, axis=-1, keepdims=True)
    centered = values - mean_v
    inv_std = lax.rsqrt(jnp.mean(centered * centered, axis=-1, keepdims=True) + EPS)
    return (centered * inv_std, inv_std)


def normalize_back(unit, inv_std, upstream):
    return inv_std * (
        upstream
        - jnp.mean(upstream, axis=-1, keepdims=True)
        - unit * jnp.mean(upstream * unit, axis=-1, keepdims=True)
    )


def dot(a, b):
    return jnp.dot(a, b, preferred_element_type=F32)


def dot_t(a, b):
    return lax.dot_general(a, b, (((1,), (1,)), ((), ())), preferred_element_type=F32)


def head_stack(tile):
    low = lax.broadcasted_iota(jnp.int32, tile.shape, 1) < 64
    zero = jnp.zeros_like(tile)
    return jnp.concatenate([jnp.where(low, tile, zero), jnp.where(low, zero, tile)], 0)


def head_join(stacked):
    low = lax.broadcasted_iota(jnp.int32, (ROWS, 128), 1) < 64
    return jnp.where(low, stacked[:ROWS], stacked[ROWS:])


def kernel(
    nodes_hbm,
    list_hbm,
    wq_hbm,
    wk_hbm,
    wv_hbm,
    wo_hbm,
    wu_hbm,
    wd_hbm,
    cot_hbm,
    both_out,
    xv,
    cotv,
    wq,
    wkv,
    wo,
    wu,
    wd,
    gath,
    halo,
    kv,
    q2,
    q2t,
    g2,
    g2t,
    dpv,
    pbv,
    dsv,
    wexp,
    mstat,
    lstat,
    oacc,
    fstat,
    mixv,
    delt,
    dq,
    dt,
    part,
    psib,
    listed,
    lsib,
    hsend,
    hrecv,
    xo,
    yl,
    yr,
    sbuf,
    tbuf,
    ybuf,
    nbuf,
    actv,
    residv,
    gact,
    lsem,
    ready,
    ssem,
    grecv,
    rrecv,
):
    blk = lax.axis_index("blk")
    dom = lax.axis_index("dom")
    ndom = lax.axis_size("dom")
    core = blk % 2
    x = (blk // 2) % 4
    h = blk // 8

    def at(xx, hh, cc):
        return hh * 8 + (xx % 4) * 2 + cc

    right = {"blk": at(x + 1, h, core), "dom": dom}
    left = {"blk": at(x + 3, h, core), "dom": dom}
    across = {"blk": at(x, 1 - h, core), "dom": dom}
    twin = {"blk": at(x, h, 1 - core), "dom": dom}
    up = {"blk": blk, "dom": (dom + 1) % ndom}
    down = {"blk": blk, "dom": (dom + ndom - 1) % ndom}

    half = ndom // 2
    z = dom % half
    final = half - 1

    barrier = pltpu.get_barrier_semaphore()

    def greet(peer):
        pl.semaphore_signal(barrier, inc=1, device_id=peer, device_id_type=MESH)

    greet(across)

    @pl.when(z < final)
    def _():
        greet(up)

    @pl.when(z == 0)
    def _():
        greet(down)

    for peer in (right, left, twin):
        greet(peer)

    pl.semaphore_wait(barrier, 4 + jnp.where(z > 0, 1, 0) + jnp.where(z == final, 1, 0))

    @pl.when(z > 0)
    def _():
        pl.semaphore_signal(ready.at[0], inc=1, device_id=down, device_id_type=MESH)

    @pl.when(z == final)
    def _():
        pl.semaphore_signal(ready.at[1], inc=1, device_id=up, device_id_type=MESH)

    sends = []

    pool = list(range(19))

    def plan(src, dst, rsems, slot, peer):
        index = pool.pop(0)
        copy = pltpu.make_async_remote_copy(
            src_ref=src,
            dst_ref=dst,
            send_sem=ssem.at[index],
            recv_sem=rsems.at[slot],
            device_id=peer,
            device_id_type=MESH,
        )
        sends.append((copy, index))
        return copy

    def reclaim(keep=()):
        held = [entry for entry in sends if any(entry[0] is copy for copy in keep)]
        for copy, index in sends:
            if not any(copy is entry[0] for entry in held):
                copy.wait_send()
                pool.append(index)
        sends[:] = held

    def push(*where):
        copy = plan(*where)
        copy.start()
        return copy

    top = pl.ds(0, HALF)
    bottom = pl.ds(HALF, HALF)

    def block(xx, rr):
        return at(xx, rr, core)

    rows_of = (h, 1 - h)

    own = block(x, h)
    c_r = {}
    c_l = {}
    c_y = []
    c_y.append(push(nodes_hbm.at[top], gath.at[own, top], grecv, 12, across))
    c_r[0, 0] = push(nodes_hbm.at[top], gath.at[own, top], grecv, 0, right)
    c_l[0, 1] = push(nodes_hbm.at[bottom], gath.at[own, bottom], grecv, 5, left)
    c_y.append(push(nodes_hbm.at[bottom], gath.at[own, bottom], grecv, 13, across))

    loads = []

    def load(src, dst):
        copy = pltpu.make_async_copy(src, dst, lsem.at[len(loads)])
        copy.start()
        loads.append(copy)
        return copy

    ld_x = load(nodes_hbm, xv)
    ld_wk = load(wk_hbm, wkv.at[:, pl.ds(0, D)])
    ld_wv = load(wv_hbm, wkv.at[:, pl.ds(D, D)])
    ld_wq = load(wq_hbm, wq)
    ld_own = load(nodes_hbm, gath.at[own])
    ld_list = load(list_hbm, listed)
    ld_cot = load(cot_hbm, cotv)
    ld_wd = load(wd_hbm, wd)
    ld_wo = load(wo_hbm, wo)
    ld_wu = load(wu_hbm, wu)

    c_list = push(list_hbm, lsib, grecv, 24, twin)
    c_tw = [push(nodes_hbm, gath.at[own], grecv, 16, twin)]

    ld_x.wait()
    x_full = xv[...].astype(F32)
    unit, inv_std = normalize(x_full)
    normed = unit.astype(BF16)
    ld_wk.wait()
    ld_wv.wait()
    kv[pl.ds(2 * ROWS, ROWS), :] = dot(normed, wkv[...]).astype(BF16)
    ld_wq.wait()
    queries = dot(normed, wq[...]).astype(BF16) * jnp.asarray(0.125, BF16)
    for hp in range(PAIRS):
        stacked = head_stack(queries[:, hp * 128 : (hp + 1) * 128])
        q2[hp] = stacked
        q2t[hp] = jnp.transpose(stacked)

    fwd_r = [None, None]
    fwd_l = [None, None]

    def forward(rr):
        row = rows_of[rr]
        c_r[rr, 0].wait_recv()
        from_left = block(x + 3, row)
        fwd_r[rr] = push(gath.at[from_left, top], gath.at[from_left, top], grecv, 8 + rr, right)
        c_l[rr, 1].wait_recv()
        from_right = block(x + 1, row)
        fwd_l[rr] = push(
            gath.at[from_right, bottom], gath.at[from_right, bottom], grecv, 10 + rr, left
        )

    def to_twin(slot, who):
        c_tw.append(push(gath.at[who], gath.at[who], grecv, slot, twin))

    c_r[0, 1] = push(nodes_hbm.at[bottom], gath.at[own, bottom], grecv, 1, right)
    c_l[0, 0] = push(nodes_hbm.at[top], gath.at[own, top], grecv, 4, left)
    c_up = plan(nodes_hbm, halo.at[0], grecv, 14, up)
    c_dn = plan(nodes_hbm, halo.at[1], grecv, 15, down)

    @pl.when(z > 0)
    def _():
        c_dn.start()

    @pl.when(z == final)
    def _():
        c_up.start()

    ld_wd.wait()
    ld_cot.wait()
    gact[...] = dot_t(cotv[...], wd[...])
    forward(0)
    other = block(x, 1 - h)
    c_y[0].wait_recv()
    c_r[1, 0] = push(gath.at[other, top], gath.at[other, top], grecv, 2, right)
    c_y[1].wait_recv()
    c_l[1, 1] = push(gath.at[other, bottom], gath.at[other, bottom], grecv, 7, left)
    c_l[1, 0] = push(gath.at[other, top], gath.at[other, top], grecv, 6, left)
    c_r[1, 1] = push(gath.at[other, bottom], gath.at[other, bottom], grecv, 3, right)
    to_twin(17, other)

    @pl.when(z < final)
    def _():
        pl.semaphore_wait(ready.at[0], 1)
        c_up.start()


    def project(raw, row0):
        unit_o, _ = normalize(raw.astype(F32))
        kv[pl.ds(row0, ROWS), :] = dot(unit_o.astype(BF16), wkv[...]).astype(BF16)

    def attend(base, count, which, pairs=range(PAIRS)):
        for hp in pairs:
            k = kv[base : base + count, hp * 128 : (hp + 1) * 128]
            wexp[hp, :, base : base + count] = dot_t(q2[hp], k)
        for hp in pairs:
            s = wexp[hp, :, base : base + count]
            m = jnp.max(s, axis=1, keepdims=True)
            w = jnp.exp(s - m)
            wexp[hp, :, base : base + count] = w
            total = jnp.sum(w, axis=1, keepdims=True)
            mstat[which, hp] = jnp.broadcast_to(m, (2 * ROWS, 128))
            lstat[which, hp] = jnp.broadcast_to(total, (2 * ROWS, 128))
        for hp in pairs:
            v = kv[base : base + count, D + hp * 128 : D + (hp + 1) * 128]
            oacc[which, hp] = dot(wexp[hp, :, base : base + count].astype(BF16), v)

    reclaim([copy for copy, _ in sends[8:]])
    forward(1)
    c_r[0, 1].wait_recv()
    to_twin(18, block(x + 3, h))
    c_l[0, 0].wait_recv()
    to_twin(19, block(x + 1, h))
    fwd_r[0].wait_recv()
    fwd_l[0].wait_recv()
    to_twin(22, block(x + 2, h))
    @pl.when(z == 0)
    def _():
        pl.semaphore_wait(ready.at[1], 1)
        c_dn.start()

    c_up.wait_recv()
    project(halo[0], 0)
    c_dn.wait_recv()
    project(halo[1], ROWS)
    c_r[1, 1].wait_recv()
    to_twin(20, block(x + 3, 1 - h))
    c_l[1, 0].wait_recv()
    to_twin(21, block(x + 1, 1 - h))
    attend(0, 3 * ROWS, 0)
    fwd_r[1].wait_recv()
    fwd_l[1].wait_recv()
    to_twin(23, block(x + 2, 1 - h))
    for copy in c_tw:
        copy.wait_recv()
    c_list.wait_recv()
    ld_own.wait()
    ld_list.wait()

    for e in range(4):
        unit_e, _ = normalize(gath[listed[0, e]].astype(F32))
        nbuf[e * ROWS : (e + 1) * ROWS] = unit_e.astype(BF16)
    kv[3 * ROWS : 7 * ROWS, :] = dot(nbuf[...], wkv[...]).astype(BF16)
    attend(3 * ROWS, 4 * ROWS, 1)

    for hp in range(PAIRS):
        m0, m1 = mstat[0, hp], mstat[1, hp]
        m = jnp.maximum(m0, m1)
        a0, a1 = jnp.exp(m0 - m), jnp.exp(m1 - m)
        inv = 1.0 / (a0 * lstat[0, hp] + a1 * lstat[1, hp])
        f0, f1 = a0 * inv, a1 * inv
        fstat[0, hp] = f0
        fstat[1, hp] = f1
        o = oacc[0, hp] * f0 + oacc[1, hp] * f1
        mixv[:, hp * 128 : (hp + 1) * 128] = head_join(o).astype(BF16)

    ld_wo.wait()
    mixed = mixv[...]
    resid = xv[...].astype(F32) + dot(mixed, wo[...])
    unit2, inv_std2 = normalize(resid)
    ld_wu.wait()
    pre = dot(unit2.astype(BF16), wu[...])
    cot = cotv[...]
    c0 = 0.7978845608028654
    sq = pre * pre
    th = jnp.tanh(c0 * (pre + 0.044715 * (sq * pre)))
    act = 0.5 * pre * (1.0 + th)
    slope = 0.5 * (1.0 + th) + 0.5 * pre * (1.0 - th * th) * (c0 * (1.0 + 3.0 * 0.044715 * sq))
    actv[...] = act.astype(BF16)
    residv[...] = resid
    grad_pre = (gact[...] * slope).astype(BF16)
    grad_norm2 = dot_t(grad_pre, wu[...])
    grad_resid = cot.astype(F32) + normalize_back(unit2, inv_std2, grad_norm2)
    grad_mixed = dot_t(grad_resid.astype(BF16), wo[...]).astype(BF16)
    for hp in range(PAIRS):
        stacked = head_stack(grad_mixed[:, hp * 128 : (hp + 1) * 128])
        g2[hp] = stacked
        g2t[hp] = jnp.transpose(stacked)
        mixed_pair = mixed[:, hp * 128 : (hp + 1) * 128].astype(F32)
        both = jnp.concatenate([mixed_pair, mixed_pair], 0)
        d = jnp.sum(stacked.astype(F32) * both, axis=1, keepdims=True)
        delt[hp] = jnp.broadcast_to(d, (2 * ROWS, 128))

    def attend_back(base, count, which):
        tiles = count // 128
        for hp in range(PAIRS):
            v = kv[base : base + count, D + hp * 128 : D + (hp + 1) * 128]
            dpv[hp, :, :count] = dot_t(g2[hp], v)
        for hp in range(PAIRS):
            scale = jnp.concatenate([fstat[which, hp]] * tiles, 1)
            shift = jnp.concatenate([delt[hp]] * tiles, 1)
            p = wexp[hp, :, base : base + count] * scale
            pbv[hp, :, :count] = p.astype(BF16)
            dsv[hp, :, :count] = (p * (dpv[hp, :, :count] - shift)).astype(BF16)
        for hp in range(PAIRS):
            dt[D + hp * 128 : D + (hp + 1) * 128, base : base + count] = dot(
                g2t[hp], pbv[hp, :, :count]
            ).astype(BF16)
            dt[hp * 128 : (hp + 1) * 128, base : base + count] = dot(
                q2t[hp], dsv[hp, :, :count]
            ).astype(BF16)
            k = kv[base : base + count, hp * 128 : (hp + 1) * 128]
            dq[which, hp] = dot(dsv[hp, :, :count], k)

    attend_back(3 * ROWS, 4 * ROWS, 1)

    reclaim((c_up, c_dn))
    zero_block = jnp.zeros((D, ROWS), BF16)
    part[4] = zero_block
    psib[4] = zero_block
    c_ps = []
    da = pl.ds(0, DHALF)
    db = pl.ds(DHALF, DHALF)
    first4 = pl.ds(0, 4)
    for i, cols in enumerate((da, db)):
        every = dot(wkv[cols, :], dt[:, 3 * ROWS : 7 * ROWS]).astype(BF16)
        for e in range(4):
            part[e, cols, :] = every[:, e * ROWS : (e + 1) * ROWS]
        c_ps.append(
            push(part.at[first4, cols], psib.at[first4, cols], rrecv, i, twin)
        )

    attend_back(0, 3 * ROWS, 0)
    for copy in c_ps:
        copy.wait_recv()

    def slot_of(lists, target):
        slot = jnp.int32(4)
        for e in range(4):
            slot = jnp.where(lists[0, e] == target, jnp.int32(e), slot)
        return slot

    def summed(xx, rr, cols):
        target = block(xx, rows_of[rr])
        return (
            part[slot_of(listed, target), cols, :].astype(F32)
            + psib[slot_of(lsib, target), cols, :].astype(F32)
        )

    c_x = {}

    def opposite_step(rr):
        s0 = 5 + 6 * rr
        sbuf[rr, 0] = summed(x + 2, rr, da).astype(BF16)
        c_x[rr, 0] = push(sbuf.at[rr, 0], xo.at[rr, 0], rrecv, s0, right)
        sbuf[rr, 1] = summed(x + 2, rr, db).astype(BF16)
        c_x[rr, 1] = push(sbuf.at[rr, 1], xo.at[rr, 1], rrecv, s0 + 1, left)

    def direct_step(rr):
        s0 = 5 + 6 * rr
        sbuf[rr, 2] = summed(x + 1, rr, db).astype(BF16)
        c_x[rr, 2] = push(sbuf.at[rr, 2], yl.at[rr, db], rrecv, s0 + 2, right)
        sbuf[rr, 3] = summed(x + 3, rr, da).astype(BF16)
        c_x[rr, 3] = push(sbuf.at[rr, 3], yr.at[rr, da], rrecv, s0 + 3, left)

    def second_step(rr):
        s0 = 5 + 6 * rr
        c_x[rr, 0].wait_recv()
        sbuf[rr, 4] = (summed(x + 1, rr, da) + xo[rr, 0].astype(F32)).astype(BF16)
        c_x[rr, 4] = push(sbuf.at[rr, 4], yl.at[rr, da], rrecv, s0 + 4, right)
        c_x[rr, 1].wait_recv()
        sbuf[rr, 5] = (summed(x + 3, rr, db) + xo[rr, 1].astype(F32)).astype(BF16)
        c_x[rr, 5] = push(sbuf.at[rr, 5], yr.at[rr, db], rrecv, s0 + 5, left)

    opposite_step(1)
    halves_t = dot(wkv[...], dt[:, 0 : 2 * ROWS]).astype(BF16)
    hsend[0] = halves_t[:, :ROWS]
    hsend[1] = halves_t[:, ROWS:]
    c_hd = push(hsend.at[0], hrecv.at[0], rrecv, 2, down)
    c_hu = push(hsend.at[1], hrecv.at[1], rrecv, 3, up)
    direct_step(1)
    second_step(1)
    opposite_step(0)
    direct_step(0)

    own_t = dot(wkv[...], dt[:, 2 * ROWS : 3 * ROWS])
    grad_q = jnp.concatenate([head_join(dq[0, hp] + dq[1, hp]) for hp in range(PAIRS)], 1)
    grad_in = dot_t((grad_q * 0.125).astype(BF16), wq[...])
    both_out[:, 0:D] = residv[...] + dot(actv[...], wd[...])

    for slot in (2, 3, 4, 5):
        c_x[1, slot].wait_recv()
    for cols in (da, db):
        tbuf[cols] = (
            summed(x, 1, cols) + yl[1, cols, :].astype(F32) + yr[1, cols, :].astype(F32)
        ).astype(BF16)
    c_t = push(tbuf, ybuf, rrecv, 4, across)
    second_step(0)
    c_hd.wait_recv()
    c_hu.wait_recv()
    own_t = own_t + hrecv[0].astype(F32) + hrecv[1].astype(F32)
    for slot in (2, 3, 4, 5):
        c_x[0, slot].wait_recv()
    own_t = own_t + yl[0].astype(F32) + yr[0].astype(F32)
    own_t = own_t + jnp.concatenate([summed(x, 0, da), summed(x, 0, db)], 0)
    grad_in = grad_in + jnp.transpose(own_t)
    unit_b, inv_b = normalize(xv[...].astype(F32))
    c_t.wait_recv()
    grad_in = grad_in + jnp.transpose(ybuf[...].astype(F32))
    both_out[:, D : 2 * D] = grad_resid + normalize_back(unit_b, inv_b, grad_in)
    reclaim()


def on_device(nodes, experts_list, w_query, w_key, w_value, w_out, w_up, w_down, cotangent):
    rows, width = nodes.shape
    hbm = pl.BlockSpec(memory_space=pltpu.HBM)
    tile = lambda *shape, dtype=BF16: pltpu.VMEM(shape, dtype)
    out = jax.ShapeDtypeStruct((rows, width), BF16)
    vm = pl.BlockSpec(memory_space=pltpu.VMEM)
    both = pl.pallas_call(
        kernel,
        out_shape=jax.ShapeDtypeStruct((rows, 2 * width), F32),
        in_specs=[hbm] * 9,
        out_specs=vm,
        scratch_shapes=[
            tile(ROWS, D),
            tile(ROWS, D),
            tile(D, D),
            tile(D, 2 * D),
            tile(D, D),
            tile(D, FF),
            tile(FF, D),
            tile(16, ROWS, D),
            tile(2, ROWS, D),
            tile(7 * ROWS, 2 * D),
            tile(PAIRS, 2 * ROWS, 128),
            tile(PAIRS, 128, 2 * ROWS),
            tile(PAIRS, 2 * ROWS, 128),
            tile(PAIRS, 128, 2 * ROWS),
            tile(PAIRS, 2 * ROWS, 4 * ROWS, dtype=F32),
            tile(PAIRS, 2 * ROWS, 4 * ROWS),
            tile(PAIRS, 2 * ROWS, 4 * ROWS),
            tile(PAIRS, 2 * ROWS, 7 * ROWS, dtype=F32),
            tile(2, PAIRS, 2 * ROWS, 128, dtype=F32),
            tile(2, PAIRS, 2 * ROWS, 128, dtype=F32),
            tile(2, PAIRS, 2 * ROWS, 128, dtype=F32),
            tile(2, PAIRS, 2 * ROWS, 128, dtype=F32),
            tile(ROWS, D),
            tile(PAIRS, 2 * ROWS, 128, dtype=F32),
            tile(2, PAIRS, 2 * ROWS, 128, dtype=F32),
            tile(2 * D, 7 * ROWS),
            tile(5, D, ROWS),
            tile(5, D, ROWS),
            pltpu.SMEM((1, 4), jnp.int32),
            pltpu.SMEM((1, 4), jnp.int32),
            tile(2, D, ROWS),
            tile(2, D, ROWS),
            tile(2, 2, DHALF, ROWS),
            tile(2, D, ROWS),
            tile(2, D, ROWS),
            tile(2, 6, DHALF, ROWS),
            tile(D, ROWS),
            tile(D, ROWS),
            tile(4 * ROWS, D),
            tile(ROWS, FF),
            tile(ROWS, D, dtype=F32),
            tile(ROWS, FF, dtype=F32),
            pltpu.SemaphoreType.DMA((10,)),
            pltpu.SemaphoreType.REGULAR((2,)),
            pltpu.SemaphoreType.DMA((19,)),
            pltpu.SemaphoreType.DMA((25,)),
            pltpu.SemaphoreType.DMA((17,)),
        ],
        compiler_params=pltpu.CompilerParams(
            collective_id=0, has_side_effects=True, vmem_limit_bytes=28 * 1024 * 1024
        ),
        name="exphormer",
    )(
        *(
            pltpu.with_memory_space_constraint(a, pltpu.HBM)
            for a in (nodes, experts_list, w_query, w_key, w_value, w_out, w_up, w_down, cotangent)
        ),
    )
    return (both[:, :width].astype(BF16), both[:, width:].astype(BF16))


def solution(mesh):
    return jax.shard_map(
        on_device,
        mesh=mesh,
        in_specs=(
            P(("blk", "dom"), None),
            P(("blk", "dom"), None),
            P(),
            P(),
            P(),
            P(),
            P(),
            P(),
            P(("blk", "dom"), None),
        ),
        out_specs=(P(("blk", "dom"), None), P(("blk", "dom"), None)),
        check_vma=False,
    )
```

```python
import functools

import jax
import jax.numpy as jnp
from jax import lax
from jax.experimental import pallas as pl
from jax.experimental.pallas import tpu as pltpu
from jax.sharding import PartitionSpec as P

EPS = 1e-05
MESH = pl.DeviceIdType.MESH
D = 512
FF = 1024
ROWS = 128
HALF = 64
DHALF = 256
PAIRS = 4
F32 = jnp.float32
BF16 = jnp.bfloat16


def normalize(values):
    mean_v = jnp.mean(values, axis=-1, keepdims=True)
    centered = values - mean_v
    inv_std = lax.rsqrt(jnp.mean(centered * centered, axis=-1, keepdims=True) + EPS)
    return (centered * inv_std, inv_std)


def normalize_back(unit, inv_std, upstream):
    return inv_std * (
        upstream
        - jnp.mean(upstream, axis=-1, keepdims=True)
        - unit * jnp.mean(upstream * unit, axis=-1, keepdims=True)
    )


def dot(a, b):
    return jnp.dot(a, b, preferred_element_type=F32)


def dot_t(a, b):
    return lax.dot_general(a, b, (((1,), (1,)), ((), ())), preferred_element_type=F32)


def head_stack(tile):
    low = lax.broadcasted_iota(jnp.int32, tile.shape, 1) < 64
    zero = jnp.zeros_like(tile)
    return jnp.concatenate([jnp.where(low, tile, zero), jnp.where(low, zero, tile)], 0)


def head_join(stacked):
    low = lax.broadcasted_iota(jnp.int32, (ROWS, 128), 1) < 64
    return jnp.where(low, stacked[:ROWS], stacked[ROWS:])


def kernel(
    nodes_hbm,
    list_hbm,
    wq_hbm,
    wk_hbm,
    wv_hbm,
    wo_hbm,
    wu_hbm,
    wd_hbm,
    cot_hbm,
    both_out,
    xv,
    cotv,
    wq,
    wkv,
    wo,
    wu,
    wd,
    gath,
    halo,
    kv,
    q2,
    q2t,
    g2,
    g2t,
    dpv,
    pbv,
    dsv,
    wexp,
    mstat,
    lstat,
    oacc,
    fstat,
    mixv,
    delt,
    dq,
    dt,
    part,
    psib,
    listed,
    lsib,
    hsend,
    hrecv,
    xo,
    yl,
    yr,
    sbuf,
    tbuf,
    ybuf,
    nbuf,
    actv,
    residv,
    gact,
    lsem,
    ready,
    ssem,
    grecv,
    rrecv,
):
    blk = lax.axis_index("blk")
    dom = lax.axis_index("dom")
    ndom = lax.axis_size("dom")
    core = blk % 2
    x = (blk // 2) % 4
    h = blk // 8

    def at(xx, hh, cc):
        return hh * 8 + (xx % 4) * 2 + cc

    right = {"blk": at(x + 1, h, core), "dom": dom}
    left = {"blk": at(x + 3, h, core), "dom": dom}
    across = {"blk": at(x, 1 - h, core), "dom": dom}
    twin = {"blk": at(x, h, 1 - core), "dom": dom}
    up = {"blk": blk, "dom": (dom + 1) % ndom}
    down = {"blk": blk, "dom": (dom + ndom - 1) % ndom}

    half = ndom // 2
    z = dom % half
    final = half - 1

    barrier = pltpu.get_barrier_semaphore()

    def greet(peer):
        pl.semaphore_signal(barrier, inc=1, device_id=peer, device_id_type=MESH)

    greet(across)

    @pl.when(z < final)
    def _():
        greet(up)

    @pl.when(z == 0)
    def _():
        greet(down)

    for peer in (right, left, twin):
        greet(peer)

    pl.semaphore_wait(barrier, 4 + jnp.where(z > 0, 1, 0) + jnp.where(z == final, 1, 0))

    @pl.when(z > 0)
    def _():
        pl.semaphore_signal(ready.at[0], inc=1, device_id=down, device_id_type=MESH)

    @pl.when(z == final)
    def _():
        pl.semaphore_signal(ready.at[1], inc=1, device_id=up, device_id_type=MESH)

    sends = []

    pool = list(range(19))

    def plan(src, dst, rsems, slot, peer):
        index = pool.pop(0)
        copy = pltpu.make_async_remote_copy(
            src_ref=src,
            dst_ref=dst,
            send_sem=ssem.at[index],
            recv_sem=rsems.at[slot],
            device_id=peer,
            device_id_type=MESH,
        )
        sends.append((copy, index))
        return copy

    def reclaim(keep=()):
        held = [entry for entry in sends if any(entry[0] is copy for copy in keep)]
        for copy, index in sends:
            if not any(copy is entry[0] for entry in held):
                copy.wait_send()
                pool.append(index)
        sends[:] = held

    def push(*where):
        copy = plan(*where)
        copy.start()
        return copy

    top = pl.ds(0, HALF)
    bottom = pl.ds(HALF, HALF)

    def block(xx, rr):
        return at(xx, rr, core)

    rows_of = (h, 1 - h)

    own = block(x, h)
    c_r = {}
    c_l = {}
    c_y = []
    c_y.append(push(nodes_hbm.at[top], gath.at[own, top], grecv, 12, across))
    c_r[0, 0] = push(nodes_hbm.at[top], gath.at[own, top], grecv, 0, right)
    c_l[0, 1] = push(nodes_hbm.at[bottom], gath.at[own, bottom], grecv, 5, left)
    c_y.append(push(nodes_hbm.at[bottom], gath.at[own, bottom], grecv, 13, across))

    loads = []

    def load(src, dst):
        copy = pltpu.make_async_copy(src, dst, lsem.at[len(loads)])
        copy.start()
        loads.append(copy)
        return copy

    ld_x = load(nodes_hbm, xv)
    ld_wk = load(wk_hbm, wkv.at[:, pl.ds(0, D)])
    ld_wv = load(wv_hbm, wkv.at[:, pl.ds(D, D)])
    ld_wq = load(wq_hbm, wq)
    ld_own = load(nodes_hbm, gath.at[own])
    ld_list = load(list_hbm, listed)
    ld_cot = load(cot_hbm, cotv)
    ld_wd = load(wd_hbm, wd)
    ld_wo = load(wo_hbm, wo)
    ld_wu = load(wu_hbm, wu)

    c_list = push(list_hbm, lsib, grecv, 24, twin)
    c_tw = [push(nodes_hbm, gath.at[own], grecv, 16, twin)]

    ld_x.wait()
    x_full = xv[...].astype(F32)
    unit, inv_std = normalize(x_full)
    normed = unit.astype(BF16)
    ld_wk.wait()
    ld_wv.wait()
    kv[pl.ds(2 * ROWS, ROWS), :] = dot(normed, wkv[...]).astype(BF16)
    ld_wq.wait()
    queries = dot(normed, wq[...]).astype(BF16) * jnp.asarray(0.125, BF16)
    for hp in range(PAIRS):
        stacked = head_stack(queries[:, hp * 128 : (hp + 1) * 128])
        q2[hp] = stacked
        q2t[hp] = jnp.transpose(stacked)

    fwd_r = [None, None]
    fwd_l = [None, None]

    def forward(rr):
        row = rows_of[rr]
        c_r[rr, 0].wait_recv()
        from_left = block(x + 3, row)
        fwd_r[rr] = push(gath.at[from_left, top], gath.at[from_left, top], grecv, 8 + rr, right)
        c_l[rr, 1].wait_recv()
        from_right = block(x + 1, row)
        fwd_l[rr] = push(
            gath.at[from_right, bottom], gath.at[from_right, bottom], grecv, 10 + rr, left
        )

    def to_twin(slot, who):
        c_tw.append(push(gath.at[who], gath.at[who], grecv, slot, twin))

    c_r[0, 1] = push(nodes_hbm.at[bottom], gath.at[own, bottom], grecv, 1, right)
    c_l[0, 0] = push(nodes_hbm.at[top], gath.at[own, top], grecv, 4, left)
    c_up = plan(nodes_hbm, halo.at[0], grecv, 14, up)
    c_dn = plan(nodes_hbm, halo.at[1], grecv, 15, down)

    @pl.when(z > 0)
    def _():
        c_dn.start()

    @pl.when(z == final)
    def _():
        c_up.start()

    ld_wd.wait()
    ld_cot.wait()
    gact[...] = dot_t(cotv[...], wd[...])
    forward(0)
    other = block(x, 1 - h)
    c_y[0].wait_recv()
    c_r[1, 0] = push(gath.at[other, top], gath.at[other, top], grecv, 2, right)
    c_y[1].wait_recv()
    c_l[1, 1] = push(gath.at[other, bottom], gath.at[other, bottom], grecv, 7, left)
    c_l[1, 0] = push(gath.at[other, top], gath.at[other, top], grecv, 6, left)
    c_r[1, 1] = push(gath.at[other, bottom], gath.at[other, bottom], grecv, 3, right)
    to_twin(17, other)

    @pl.when(z < final)
    def _():
        pl.semaphore_wait(ready.at[0], 1)
        c_up.start()


    def project(raw, row0):
        unit_o, _ = normalize(raw.astype(F32))
        kv[pl.ds(row0, ROWS), :] = dot(unit_o.astype(BF16), wkv[...]).astype(BF16)

    def attend(base, count, which, pairs=range(PAIRS)):
        for hp in pairs:
            k = kv[base : base + count, hp * 128 : (hp + 1) * 128]
            wexp[hp, :, base : base + count] = dot_t(q2[hp], k)
        for hp in pairs:
            s = wexp[hp, :, base : base + count]
            m = jnp.max(s, axis=1, keepdims=True)
            w = jnp.exp(s - m)
            wexp[hp, :, base : base + count] = w
            total = jnp.sum(w, axis=1, keepdims=True)
            mstat[which, hp] = jnp.broadcast_to(m, (2 * ROWS, 128))
            lstat[which, hp] = jnp.broadcast_to(total, (2 * ROWS, 128))
        for hp in pairs:
            v = kv[base : base + count, D + hp * 128 : D + (hp + 1) * 128]
            oacc[which, hp] = dot(wexp[hp, :, base : base + count].astype(BF16), v)

    reclaim([copy for copy, _ in sends[8:]])
    forward(1)
    c_r[0, 1].wait_recv()
    to_twin(18, block(x + 3, h))
    c_l[0, 0].wait_recv()
    to_twin(19, block(x + 1, h))
    fwd_r[0].wait_recv()
    fwd_l[0].wait_recv()
    to_twin(22, block(x + 2, h))
    @pl.when(z == 0)
    def _():
        pl.semaphore_wait(ready.at[1], 1)
        c_dn.start()

    c_r[1, 1].wait_recv()
    to_twin(20, block(x + 3, 1 - h))
    c_l[1, 0].wait_recv()
    to_twin(21, block(x + 1, 1 - h))
    fwd_r[1].wait_recv()
    fwd_l[1].wait_recv()
    to_twin(23, block(x + 2, 1 - h))
    c_up.wait_recv()
    project(halo[0], 0)
    c_dn.wait_recv()
    project(halo[1], ROWS)
    attend(0, 3 * ROWS, 0)
    for copy in c_tw:
        copy.wait_recv()
    c_list.wait_recv()
    ld_own.wait()
    ld_list.wait()

    for e in range(4):
        unit_e, _ = normalize(gath[listed[0, e]].astype(F32))
        nbuf[e * ROWS : (e + 1) * ROWS] = unit_e.astype(BF16)
    kv[3 * ROWS : 7 * ROWS, :] = dot(nbuf[...], wkv[...]).astype(BF16)
    attend(3 * ROWS, 4 * ROWS, 1)

    for hp in range(PAIRS):
        m0, m1 = mstat[0, hp], mstat[1, hp]
        m = jnp.maximum(m0, m1)
        a0, a1 = jnp.exp(m0 - m), jnp.exp(m1 - m)
        inv = 1.0 / (a0 * lstat[0, hp] + a1 * lstat[1, hp])
        f0, f1 = a0 * inv, a1 * inv
        fstat[0, hp] = f0
        fstat[1, hp] = f1
        o = oacc[0, hp] * f0 + oacc[1, hp] * f1
        mixv[:, hp * 128 : (hp + 1) * 128] = head_join(o).astype(BF16)

    ld_wo.wait()
    mixed = mixv[...]
    resid = xv[...].astype(F32) + dot(mixed, wo[...])
    unit2, inv_std2 = normalize(resid)
    ld_wu.wait()
    pre = dot(unit2.astype(BF16), wu[...])
    cot = cotv[...]
    c0 = 0.7978845608028654
    sq = pre * pre
    th = jnp.tanh(c0 * (pre + 0.044715 * (sq * pre)))
    act = 0.5 * pre * (1.0 + th)
    slope = 0.5 * (1.0 + th) + 0.5 * pre * (1.0 - th * th) * (c0 * (1.0 + 3.0 * 0.044715 * sq))
    actv[...] = act.astype(BF16)
    residv[...] = resid
    grad_pre = (gact[...] * slope).astype(BF16)
    grad_norm2 = dot_t(grad_pre, wu[...])
    grad_resid = cot.astype(F32) + normalize_back(unit2, inv_std2, grad_norm2)
    grad_mixed = dot_t(grad_resid.astype(BF16), wo[...]).astype(BF16)
    for hp in range(PAIRS):
        stacked = head_stack(grad_mixed[:, hp * 128 : (hp + 1) * 128])
        g2[hp] = stacked
        g2t[hp] = jnp.transpose(stacked)
        mixed_pair = mixed[:, hp * 128 : (hp + 1) * 128].astype(F32)
        both = jnp.concatenate([mixed_pair, mixed_pair], 0)
        d = jnp.sum(stacked.astype(F32) * both, axis=1, keepdims=True)
        delt[hp] = jnp.broadcast_to(d, (2 * ROWS, 128))

    def attend_back(base, count, which):
        tiles = count // 128
        for hp in range(PAIRS):
            v = kv[base : base + count, D + hp * 128 : D + (hp + 1) * 128]
            dpv[hp, :, :count] = dot_t(g2[hp], v)
        for hp in range(PAIRS):
            scale = jnp.concatenate([fstat[which, hp]] * tiles, 1)
            shift = jnp.concatenate([delt[hp]] * tiles, 1)
            p = wexp[hp, :, base : base + count] * scale
            pbv[hp, :, :count] = p.astype(BF16)
            dsv[hp, :, :count] = (p * (dpv[hp, :, :count] - shift)).astype(BF16)
        for hp in range(PAIRS):
            dt[D + hp * 128 : D + (hp + 1) * 128, base : base + count] = dot(
                g2t[hp], pbv[hp, :, :count]
            ).astype(BF16)
            dt[hp * 128 : (hp + 1) * 128, base : base + count] = dot(
                q2t[hp], dsv[hp, :, :count]
            ).astype(BF16)
            k = kv[base : base + count, hp * 128 : (hp + 1) * 128]
            dq[which, hp] = dot(dsv[hp, :, :count], k)

    attend_back(3 * ROWS, 4 * ROWS, 1)

    reclaim((c_up, c_dn))
    zero_block = jnp.zeros((D, ROWS), BF16)
    part[4] = zero_block
    psib[4] = zero_block
    c_ps = []
    da = pl.ds(0, DHALF)
    db = pl.ds(DHALF, DHALF)
    first4 = pl.ds(0, 4)
    for i, cols in enumerate((da, db)):
        every = dot(wkv[cols, :], dt[:, 3 * ROWS : 7 * ROWS]).astype(BF16)
        for e in range(4):
            part[e, cols, :] = every[:, e * ROWS : (e + 1) * ROWS]
        c_ps.append(
            push(part.at[first4, cols], psib.at[first4, cols], rrecv, i, twin)
        )

    attend_back(0, 3 * ROWS, 0)
    halves_t = dot(wkv[...], dt[:, 0 : 2 * ROWS]).astype(BF16)
    hsend[0] = halves_t[:, :ROWS]
    hsend[1] = halves_t[:, ROWS:]
    c_hd = push(hsend.at[0], hrecv.at[0], rrecv, 2, down)
    c_hu = push(hsend.at[1], hrecv.at[1], rrecv, 3, up)
    for copy in c_ps:
        copy.wait_recv()

    def slot_of(lists, target):
        slot = jnp.int32(4)
        for e in range(4):
            slot = jnp.where(lists[0, e] == target, jnp.int32(e), slot)
        return slot

    def summed(xx, rr, cols):
        target = block(xx, rows_of[rr])
        return (
            part[slot_of(listed, target), cols, :].astype(F32)
            + psib[slot_of(lsib, target), cols, :].astype(F32)
        )

    c_x = {}

    def opposite_step(rr):
        s0 = 5 + 6 * rr
        sbuf[rr, 0] = summed(x + 2, rr, da).astype(BF16)
        c_x[rr, 0] = push(sbuf.at[rr, 0], xo.at[rr, 0], rrecv, s0, right)
        sbuf[rr, 1] = summed(x + 2, rr, db).astype(BF16)
        c_x[rr, 1] = push(sbuf.at[rr, 1], xo.at[rr, 1], rrecv, s0 + 1, left)

    def direct_step(rr):
        s0 = 5 + 6 * rr
        sbuf[rr, 2] = summed(x + 1, rr, db).astype(BF16)
        c_x[rr, 2] = push(sbuf.at[rr, 2], yl.at[rr, db], rrecv, s0 + 2, right)
        sbuf[rr, 3] = summed(x + 3, rr, da).astype(BF16)
        c_x[rr, 3] = push(sbuf.at[rr, 3], yr.at[rr, da], rrecv, s0 + 3, left)

    def second_step(rr):
        s0 = 5 + 6 * rr
        c_x[rr, 0].wait_recv()
        sbuf[rr, 4] = (summed(x + 1, rr, da) + xo[rr, 0].astype(F32)).astype(BF16)
        c_x[rr, 4] = push(sbuf.at[rr, 4], yl.at[rr, da], rrecv, s0 + 4, right)
        c_x[rr, 1].wait_recv()
        sbuf[rr, 5] = (summed(x + 3, rr, db) + xo[rr, 1].astype(F32)).astype(BF16)
        c_x[rr, 5] = push(sbuf.at[rr, 5], yr.at[rr, db], rrecv, s0 + 5, left)

    opposite_step(1)
    own_t = dot(wkv[...], dt[:, 2 * ROWS : 3 * ROWS])
    grad_q = jnp.concatenate([head_join(dq[0, hp] + dq[1, hp]) for hp in range(PAIRS)], 1)
    grad_in = dot_t((grad_q * 0.125).astype(BF16), wq[...])
    both_out[:, 0:D] = residv[...] + dot(actv[...], wd[...])
    direct_step(1)
    second_step(1)
    opposite_step(0)
    direct_step(0)

    for slot in (2, 3, 4, 5):
        c_x[1, slot].wait_recv()
    for cols in (da, db):
        tbuf[cols] = (
            summed(x, 1, cols) + yl[1, cols, :].astype(F32) + yr[1, cols, :].astype(F32)
        ).astype(BF16)
    c_t = push(tbuf, ybuf, rrecv, 4, across)
    second_step(0)
    c_hd.wait_recv()
    c_hu.wait_recv()
    own_t = own_t + hrecv[0].astype(F32) + hrecv[1].astype(F32)
    for slot in (2, 3, 4, 5):
        c_x[0, slot].wait_recv()
    own_t = own_t + yl[0].astype(F32) + yr[0].astype(F32)
    own_t = own_t + jnp.concatenate([summed(x, 0, da), summed(x, 0, db)], 0)
    grad_in = grad_in + jnp.transpose(own_t)
    unit_b, inv_b = normalize(xv[...].astype(F32))
    c_t.wait_recv()
    grad_in = grad_in + jnp.transpose(ybuf[...].astype(F32))
    both_out[:, D : 2 * D] = grad_resid + normalize_back(unit_b, inv_b, grad_in)
    reclaim()


def on_device(nodes, experts_list, w_query, w_key, w_value, w_out, w_up, w_down, cotangent):
    rows, width = nodes.shape
    hbm = pl.BlockSpec(memory_space=pltpu.HBM)
    tile = lambda *shape, dtype=BF16: pltpu.VMEM(shape, dtype)
    out = jax.ShapeDtypeStruct((rows, width), BF16)
    vm = pl.BlockSpec(memory_space=pltpu.VMEM)
    both = pl.pallas_call(
        kernel,
        out_shape=jax.ShapeDtypeStruct((rows, 2 * width), F32),
        in_specs=[hbm] * 9,
        out_specs=vm,
        scratch_shapes=[
            tile(ROWS, D),
            tile(ROWS, D),
            tile(D, D),
            tile(D, 2 * D),
            tile(D, D),
            tile(D, FF),
            tile(FF, D),
            tile(16, ROWS, D),
            tile(2, ROWS, D),
            tile(7 * ROWS, 2 * D),
            tile(PAIRS, 2 * ROWS, 128),
            tile(PAIRS, 128, 2 * ROWS),
            tile(PAIRS, 2 * ROWS, 128),
            tile(PAIRS, 128, 2 * ROWS),
            tile(PAIRS, 2 * ROWS, 4 * ROWS, dtype=F32),
            tile(PAIRS, 2 * ROWS, 4 * ROWS),
            tile(PAIRS, 2 * ROWS, 4 * ROWS),
            tile(PAIRS, 2 * ROWS, 7 * ROWS, dtype=F32),
            tile(2, PAIRS, 2 * ROWS, 128, dtype=F32),
            tile(2, PAIRS, 2 * ROWS, 128, dtype=F32),
            tile(2, PAIRS, 2 * ROWS, 128, dtype=F32),
            tile(2, PAIRS, 2 * ROWS, 128, dtype=F32),
            tile(ROWS, D),
            tile(PAIRS, 2 * ROWS, 128, dtype=F32),
            tile(2, PAIRS, 2 * ROWS, 128, dtype=F32),
            tile(2 * D, 7 * ROWS),
            tile(5, D, ROWS),
            tile(5, D, ROWS),
            pltpu.SMEM((1, 4), jnp.int32),
            pltpu.SMEM((1, 4), jnp.int32),
            tile(2, D, ROWS),
            tile(2, D, ROWS),
            tile(2, 2, DHALF, ROWS),
            tile(2, D, ROWS),
            tile(2, D, ROWS),
            tile(2, 6, DHALF, ROWS),
            tile(D, ROWS),
            tile(D, ROWS),
            tile(4 * ROWS, D),
            tile(ROWS, FF),
            tile(ROWS, D, dtype=F32),
            tile(ROWS, FF, dtype=F32),
            pltpu.SemaphoreType.DMA((10,)),
            pltpu.SemaphoreType.REGULAR((2,)),
            pltpu.SemaphoreType.DMA((19,)),
            pltpu.SemaphoreType.DMA((25,)),
            pltpu.SemaphoreType.DMA((17,)),
        ],
        compiler_params=pltpu.CompilerParams(
            collective_id=0, has_side_effects=True, vmem_limit_bytes=28 * 1024 * 1024
        ),
        name="exphormer",
    )(
        *(
            pltpu.with_memory_space_constraint(a, pltpu.HBM)
            for a in (nodes, experts_list, w_query, w_key, w_value, w_out, w_up, w_down, cotangent)
        ),
    )
    return (both[:, :width].astype(BF16), both[:, width:].astype(BF16))


def solution(mesh):
    return jax.shard_map(
        on_device,
        mesh=mesh,
        in_specs=(
            P(("blk", "dom"), None),
            P(("blk", "dom"), None),
            P(),
            P(),
            P(),
            P(),
            P(),
            P(),
            P(("blk", "dom"), None),
        ),
        out_specs=(P(("blk", "dom"), None), P(("blk", "dom"), None)),
        check_vma=False,
    )
```

```python
import functools

import jax
import jax.numpy as jnp
from jax import lax
from jax.experimental import pallas as pl
from jax.experimental.pallas import tpu as pltpu
from jax.sharding import PartitionSpec as P

EPS = 1e-05
MESH = pl.DeviceIdType.MESH
D = 512
FF = 1024
ROWS = 128
HALF = 64
DHALF = 256
PAIRS = 4
F32 = jnp.float32
BF16 = jnp.bfloat16


def normalize(values):
    mean_v = jnp.mean(values, axis=-1, keepdims=True)
    centered = values - mean_v
    inv_std = lax.rsqrt(jnp.mean(centered * centered, axis=-1, keepdims=True) + EPS)
    return (centered * inv_std, inv_std)


def normalize_back(unit, inv_std, upstream):
    return inv_std * (
        upstream
        - jnp.mean(upstream, axis=-1, keepdims=True)
        - unit * jnp.mean(upstream * unit, axis=-1, keepdims=True)
    )


def dot(a, b):
    return jnp.dot(a, b, preferred_element_type=F32)


def dot_t(a, b):
    return lax.dot_general(a, b, (((1,), (1,)), ((), ())), preferred_element_type=F32)


def head_stack(tile):
    low = lax.broadcasted_iota(jnp.int32, tile.shape, 1) < 64
    zero = jnp.zeros_like(tile)
    return jnp.concatenate([jnp.where(low, tile, zero), jnp.where(low, zero, tile)], 0)


def head_join(stacked):
    low = lax.broadcasted_iota(jnp.int32, (ROWS, 128), 1) < 64
    return jnp.where(low, stacked[:ROWS], stacked[ROWS:])


def kernel(
    nodes_hbm,
    list_hbm,
    wq_hbm,
    wk_hbm,
    wv_hbm,
    wo_hbm,
    wu_hbm,
    wd_hbm,
    cot_hbm,
    both_out,
    xv,
    cotv,
    wq,
    wkv,
    wo,
    wu,
    wd,
    gath,
    halo,
    kv,
    q2,
    q2t,
    g2,
    g2t,
    dpv,
    pbv,
    dsv,
    wexp,
    mstat,
    lstat,
    oacc,
    fstat,
    mixv,
    delt,
    dq,
    dt,
    part,
    psib,
    listed,
    lsib,
    hsend,
    hrecv,
    xo,
    yl,
    yr,
    sbuf,
    tbuf,
    ybuf,
    wot,
    wut,
    nbuf,
    actv,
    residv,
    gact,
    lsem,
    ready,
    ssem,
    grecv,
    rrecv,
):
    blk = lax.axis_index("blk")
    dom = lax.axis_index("dom")
    ndom = lax.axis_size("dom")
    core = blk % 2
    x = (blk // 2) % 4
    h = blk // 8

    def at(xx, hh, cc):
        return hh * 8 + (xx % 4) * 2 + cc

    right = {"blk": at(x + 1, h, core), "dom": dom}
    left = {"blk": at(x + 3, h, core), "dom": dom}
    across = {"blk": at(x, 1 - h, core), "dom": dom}
    twin = {"blk": at(x, h, 1 - core), "dom": dom}
    up = {"blk": blk, "dom": (dom + 1) % ndom}
    down = {"blk": blk, "dom": (dom + ndom - 1) % ndom}

    half = ndom // 2
    z = dom % half
    final = half - 1

    barrier = pltpu.get_barrier_semaphore()

    def greet(peer):
        pl.semaphore_signal(barrier, inc=1, device_id=peer, device_id_type=MESH)

    greet(across)

    @pl.when(z < final)
    def _():
        greet(up)

    @pl.when(z == 0)
    def _():
        greet(down)

    for peer in (right, left, twin):
        greet(peer)

    pl.semaphore_wait(barrier, 4 + jnp.where(z > 0, 1, 0) + jnp.where(z == final, 1, 0))

    @pl.when(z > 0)
    def _():
        pl.semaphore_signal(ready.at[0], inc=1, device_id=down, device_id_type=MESH)

    @pl.when(z == final)
    def _():
        pl.semaphore_signal(ready.at[1], inc=1, device_id=up, device_id_type=MESH)

    sends = []

    pool = list(range(19))

    def plan(src, dst, rsems, slot, peer):
        index = pool.pop(0)
        copy = pltpu.make_async_remote_copy(
            src_ref=src,
            dst_ref=dst,
            send_sem=ssem.at[index],
            recv_sem=rsems.at[slot],
            device_id=peer,
            device_id_type=MESH,
        )
        sends.append((copy, index))
        return copy

    def reclaim(keep=()):
        held = [entry for entry in sends if any(entry[0] is copy for copy in keep)]
        for copy, index in sends:
            if not any(copy is entry[0] for entry in held):
                copy.wait_send()
                pool.append(index)
        sends[:] = held

    def push(*where):
        copy = plan(*where)
        copy.start()
        return copy

    top = pl.ds(0, HALF)
    bottom = pl.ds(HALF, HALF)

    def block(xx, rr):
        return at(xx, rr, core)

    rows_of = (h, 1 - h)

    own = block(x, h)
    c_r = {}
    c_l = {}
    c_y = []
    c_y.append(push(nodes_hbm.at[top], gath.at[own, top], grecv, 12, across))
    c_r[0, 0] = push(nodes_hbm.at[top], gath.at[own, top], grecv, 0, right)
    c_l[0, 1] = push(nodes_hbm.at[bottom], gath.at[own, bottom], grecv, 5, left)
    c_y.append(push(nodes_hbm.at[bottom], gath.at[own, bottom], grecv, 13, across))

    loads = []

    def load(src, dst):
        copy = pltpu.make_async_copy(src, dst, lsem.at[len(loads)])
        copy.start()
        loads.append(copy)
        return copy

    ld_x = load(nodes_hbm, xv)
    ld_wk = load(wk_hbm, wkv.at[:, pl.ds(0, D)])
    ld_wv = load(wv_hbm, wkv.at[:, pl.ds(D, D)])
    ld_wq = load(wq_hbm, wq)
    ld_own = load(nodes_hbm, gath.at[own])
    ld_list = load(list_hbm, listed)
    ld_cot = load(cot_hbm, cotv)
    ld_wd = load(wd_hbm, wd)
    ld_wo = load(wo_hbm, wo)
    ld_wu = load(wu_hbm, wu)

    c_list = push(list_hbm, lsib, grecv, 24, twin)
    c_tw = [push(nodes_hbm, gath.at[own], grecv, 16, twin)]

    ld_x.wait()
    x_full = xv[...].astype(F32)
    unit, inv_std = normalize(x_full)
    normed = unit.astype(BF16)
    ld_wk.wait()
    ld_wv.wait()
    kv[pl.ds(2 * ROWS, ROWS), :] = dot(normed, wkv[...]).astype(BF16)
    ld_wq.wait()
    queries = dot(normed, wq[...]).astype(BF16) * jnp.asarray(0.125, BF16)
    for hp in range(PAIRS):
        stacked = head_stack(queries[:, hp * 128 : (hp + 1) * 128])
        q2[hp] = stacked
        q2t[hp] = jnp.transpose(stacked)

    fwd_r = [None, None]
    fwd_l = [None, None]

    def forward(rr):
        row = rows_of[rr]
        c_r[rr, 0].wait_recv()
        from_left = block(x + 3, row)
        fwd_r[rr] = push(gath.at[from_left, top], gath.at[from_left, top], grecv, 8 + rr, right)
        c_l[rr, 1].wait_recv()
        from_right = block(x + 1, row)
        fwd_l[rr] = push(
            gath.at[from_right, bottom], gath.at[from_right, bottom], grecv, 10 + rr, left
        )

    def to_twin(slot, who):
        c_tw.append(push(gath.at[who], gath.at[who], grecv, slot, twin))

    c_r[0, 1] = push(nodes_hbm.at[bottom], gath.at[own, bottom], grecv, 1, right)
    c_l[0, 0] = push(nodes_hbm.at[top], gath.at[own, top], grecv, 4, left)
    c_up = plan(nodes_hbm, halo.at[0], grecv, 14, up)
    c_dn = plan(nodes_hbm, halo.at[1], grecv, 15, down)

    @pl.when(z > 0)
    def _():
        c_dn.start()

    @pl.when(z == final)
    def _():
        c_up.start()

    ld_wd.wait()
    ld_cot.wait()
    gact[...] = dot_t(cotv[...], wd[...])
    forward(0)
    other = block(x, 1 - h)
    c_y[0].wait_recv()
    c_r[1, 0] = push(gath.at[other, top], gath.at[other, top], grecv, 2, right)
    c_y[1].wait_recv()
    c_l[1, 1] = push(gath.at[other, bottom], gath.at[other, bottom], grecv, 7, left)
    c_l[1, 0] = push(gath.at[other, top], gath.at[other, top], grecv, 6, left)
    c_r[1, 1] = push(gath.at[other, bottom], gath.at[other, bottom], grecv, 3, right)
    to_twin(17, other)

    @pl.when(z < final)
    def _():
        pl.semaphore_wait(ready.at[0], 1)
        c_up.start()


    def project(raw, row0):
        unit_o, _ = normalize(raw.astype(F32))
        kv[pl.ds(row0, ROWS), :] = dot(unit_o.astype(BF16), wkv[...]).astype(BF16)

    def attend(base, count, which, pairs=range(PAIRS)):
        for hp in pairs:
            k = kv[base : base + count, hp * 128 : (hp + 1) * 128]
            wexp[hp, :, base : base + count] = dot_t(q2[hp], k)
        for hp in pairs:
            s = wexp[hp, :, base : base + count]
            m = jnp.max(s, axis=1, keepdims=True)
            w = jnp.exp(s - m)
            wexp[hp, :, base : base + count] = w
            total = jnp.sum(w, axis=1, keepdims=True)
            mstat[which, hp] = jnp.broadcast_to(m, (2 * ROWS, 128))
            lstat[which, hp] = jnp.broadcast_to(total, (2 * ROWS, 128))
        for hp in pairs:
            v = kv[base : base + count, D + hp * 128 : D + (hp + 1) * 128]
            oacc[which, hp] = dot(wexp[hp, :, base : base + count].astype(BF16), v)

    ld_wo.wait()
    ld_wu.wait()
    wot[...] = jnp.transpose(wo[...])
    wut[...] = jnp.transpose(wu[...])
    reclaim([copy for copy, _ in sends[8:]])
    forward(1)
    c_r[0, 1].wait_recv()
    to_twin(18, block(x + 3, h))
    c_l[0, 0].wait_recv()
    to_twin(19, block(x + 1, h))
    fwd_r[0].wait_recv()
    fwd_l[0].wait_recv()
    to_twin(22, block(x + 2, h))
    @pl.when(z == 0)
    def _():
        pl.semaphore_wait(ready.at[1], 1)
        c_dn.start()

    c_r[1, 1].wait_recv()
    to_twin(20, block(x + 3, 1 - h))
    c_l[1, 0].wait_recv()
    to_twin(21, block(x + 1, 1 - h))
    fwd_r[1].wait_recv()
    fwd_l[1].wait_recv()
    to_twin(23, block(x + 2, 1 - h))
    c_up.wait_recv()
    project(halo[0], 0)
    c_dn.wait_recv()
    project(halo[1], ROWS)
    attend(0, 3 * ROWS, 0)
    for copy in c_tw:
        copy.wait_recv()
    c_list.wait_recv()
    ld_own.wait()
    ld_list.wait()

    for e in range(4):
        unit_e, _ = normalize(gath[listed[0, e]].astype(F32))
        nbuf[e * ROWS : (e + 1) * ROWS] = unit_e.astype(BF16)
    kv[3 * ROWS : 7 * ROWS, :] = dot(nbuf[...], wkv[...]).astype(BF16)
    attend(3 * ROWS, 4 * ROWS, 1)

    for hp in range(PAIRS):
        m0, m1 = mstat[0, hp], mstat[1, hp]
        m = jnp.maximum(m0, m1)
        a0, a1 = jnp.exp(m0 - m), jnp.exp(m1 - m)
        inv = 1.0 / (a0 * lstat[0, hp] + a1 * lstat[1, hp])
        f0, f1 = a0 * inv, a1 * inv
        fstat[0, hp] = f0
        fstat[1, hp] = f1
        o = oacc[0, hp] * f0 + oacc[1, hp] * f1
        mixv[:, hp * 128 : (hp + 1) * 128] = head_join(o).astype(BF16)

    mixed = mixv[...]
    resid = xv[...].astype(F32) + dot(mixed, wo[...])
    unit2, inv_std2 = normalize(resid)
    pre = dot(unit2.astype(BF16), wu[...])
    cot = cotv[...]
    c0 = 0.7978845608028654
    sq = pre * pre
    th = jnp.tanh(c0 * (pre + 0.044715 * (sq * pre)))
    act = 0.5 * pre * (1.0 + th)
    slope = 0.5 * (1.0 + th) + 0.5 * pre * (1.0 - th * th) * (c0 * (1.0 + 3.0 * 0.044715 * sq))
    actv[...] = act.astype(BF16)
    residv[...] = resid
    grad_pre = (gact[...] * slope).astype(BF16)
    grad_norm2 = dot(grad_pre, wut[...])
    grad_resid = cot.astype(F32) + normalize_back(unit2, inv_std2, grad_norm2)
    grad_mixed = dot(grad_resid.astype(BF16), wot[...]).astype(BF16)
    for hp in range(PAIRS):
        stacked = head_stack(grad_mixed[:, hp * 128 : (hp + 1) * 128])
        g2[hp] = stacked
        g2t[hp] = jnp.transpose(stacked)
        mixed_pair = mixed[:, hp * 128 : (hp + 1) * 128].astype(F32)
        both = jnp.concatenate([mixed_pair, mixed_pair], 0)
        d = jnp.sum(stacked.astype(F32) * both, axis=1, keepdims=True)
        delt[hp] = jnp.broadcast_to(d, (2 * ROWS, 128))

    def attend_back(base, count, which):
        tiles = count // 128
        for hp in range(PAIRS):
            v = kv[base : base + count, D + hp * 128 : D + (hp + 1) * 128]
            dpv[hp, :, :count] = dot_t(g2[hp], v)
        for hp in range(PAIRS):
            scale = jnp.concatenate([fstat[which, hp]] * tiles, 1)
            shift = jnp.concatenate([delt[hp]] * tiles, 1)
            p = wexp[hp, :, base : base + count] * scale
            pbv[hp, :, :count] = p.astype(BF16)
            dsv[hp, :, :count] = (p * (dpv[hp, :, :count] - shift)).astype(BF16)
        for hp in range(PAIRS):
            dt[D + hp * 128 : D + (hp + 1) * 128, base : base + count] = dot(
                g2t[hp], pbv[hp, :, :count]
            ).astype(BF16)
            dt[hp * 128 : (hp + 1) * 128, base : base + count] = dot(
                q2t[hp], dsv[hp, :, :count]
            ).astype(BF16)
            k = kv[base : base + count, hp * 128 : (hp + 1) * 128]
            dq[which, hp] = dot(dsv[hp, :, :count], k)

    attend_back(3 * ROWS, 4 * ROWS, 1)

    reclaim((c_up, c_dn))
    zero_block = jnp.zeros((D, ROWS), BF16)
    part[4] = zero_block
    psib[4] = zero_block
    c_ps = []
    da = pl.ds(0, DHALF)
    db = pl.ds(DHALF, DHALF)
    first4 = pl.ds(0, 4)
    for i, cols in enumerate((da, db)):
        every = dot(wkv[cols, :], dt[:, 3 * ROWS : 7 * ROWS]).astype(BF16)
        for e in range(4):
            part[e, cols, :] = every[:, e * ROWS : (e + 1) * ROWS]
        c_ps.append(
            push(part.at[first4, cols], psib.at[first4, cols], rrecv, i, twin)
        )

    attend_back(0, 3 * ROWS, 0)
    halves_t = dot(wkv[...], dt[:, 0 : 2 * ROWS]).astype(BF16)
    hsend[0] = halves_t[:, :ROWS]
    hsend[1] = halves_t[:, ROWS:]
    c_hd = push(hsend.at[0], hrecv.at[0], rrecv, 2, down)
    c_hu = push(hsend.at[1], hrecv.at[1], rrecv, 3, up)
    for copy in c_ps:
        copy.wait_recv()

    def slot_of(lists, target):
        slot = jnp.int32(4)
        for e in range(4):
            slot = jnp.where(lists[0, e] == target, jnp.int32(e), slot)
        return slot

    def summed(xx, rr, cols):
        target = block(xx, rows_of[rr])
        return (
            part[slot_of(listed, target), cols, :].astype(F32)
            + psib[slot_of(lsib, target), cols, :].astype(F32)
        )

    c_x = {}

    def opposite_step(rr):
        s0 = 5 + 6 * rr
        sbuf[rr, 0] = summed(x + 2, rr, da).astype(BF16)
        c_x[rr, 0] = push(sbuf.at[rr, 0], xo.at[rr, 0], rrecv, s0, right)
        sbuf[rr, 1] = summed(x + 2, rr, db).astype(BF16)
        c_x[rr, 1] = push(sbuf.at[rr, 1], xo.at[rr, 1], rrecv, s0 + 1, left)

    def direct_step(rr):
        s0 = 5 + 6 * rr
        sbuf[rr, 2] = summed(x + 1, rr, db).astype(BF16)
        c_x[rr, 2] = push(sbuf.at[rr, 2], yl.at[rr, db], rrecv, s0 + 2, right)
        sbuf[rr, 3] = summed(x + 3, rr, da).astype(BF16)
        c_x[rr, 3] = push(sbuf.at[rr, 3], yr.at[rr, da], rrecv, s0 + 3, left)

    def second_step(rr):
        s0 = 5 + 6 * rr
        c_x[rr, 0].wait_recv()
        sbuf[rr, 4] = (summed(x + 1, rr, da) + xo[rr, 0].astype(F32)).astype(BF16)
        c_x[rr, 4] = push(sbuf.at[rr, 4], yl.at[rr, da], rrecv, s0 + 4, right)
        c_x[rr, 1].wait_recv()
        sbuf[rr, 5] = (summed(x + 3, rr, db) + xo[rr, 1].astype(F32)).astype(BF16)
        c_x[rr, 5] = push(sbuf.at[rr, 5], yr.at[rr, db], rrecv, s0 + 5, left)

    opposite_step(1)
    own_t = dot(wkv[...], dt[:, 2 * ROWS : 3 * ROWS])
    grad_q = jnp.concatenate([head_join(dq[0, hp] + dq[1, hp]) for hp in range(PAIRS)], 1)
    grad_in = dot_t((grad_q * 0.125).astype(BF16), wq[...])
    both_out[:, 0:D] = residv[...] + dot(actv[...], wd[...])
    direct_step(1)
    second_step(1)
    opposite_step(0)
    direct_step(0)

    for slot in (2, 3, 4, 5):
        c_x[1, slot].wait_recv()
    for cols in (da, db):
        tbuf[cols] = (
            summed(x, 1, cols) + yl[1, cols, :].astype(F32) + yr[1, cols, :].astype(F32)
        ).astype(BF16)
    c_t = push(tbuf, ybuf, rrecv, 4, across)
    second_step(0)
    c_hd.wait_recv()
    c_hu.wait_recv()
    own_t = own_t + hrecv[0].astype(F32) + hrecv[1].astype(F32)
    for slot in (2, 3, 4, 5):
        c_x[0, slot].wait_recv()
    own_t = own_t + yl[0].astype(F32) + yr[0].astype(F32)
    own_t = own_t + jnp.concatenate([summed(x, 0, da), summed(x, 0, db)], 0)
    grad_in = grad_in + jnp.transpose(own_t)
    unit_b, inv_b = normalize(xv[...].astype(F32))
    c_t.wait_recv()
    grad_in = grad_in + jnp.transpose(ybuf[...].astype(F32))
    both_out[:, D : 2 * D] = grad_resid + normalize_back(unit_b, inv_b, grad_in)
    reclaim()


def on_device(nodes, experts_list, w_query, w_key, w_value, w_out, w_up, w_down, cotangent):
    rows, width = nodes.shape
    hbm = pl.BlockSpec(memory_space=pltpu.HBM)
    tile = lambda *shape, dtype=BF16: pltpu.VMEM(shape, dtype)
    out = jax.ShapeDtypeStruct((rows, width), BF16)
    vm = pl.BlockSpec(memory_space=pltpu.VMEM)
    both = pl.pallas_call(
        kernel,
        out_shape=jax.ShapeDtypeStruct((rows, 2 * width), F32),
        in_specs=[hbm] * 9,
        out_specs=vm,
        scratch_shapes=[
            tile(ROWS, D),
            tile(ROWS, D),
            tile(D, D),
            tile(D, 2 * D),
            tile(D, D),
            tile(D, FF),
            tile(FF, D),
            tile(16, ROWS, D),
            tile(2, ROWS, D),
            tile(7 * ROWS, 2 * D),
            tile(PAIRS, 2 * ROWS, 128),
            tile(PAIRS, 128, 2 * ROWS),
            tile(PAIRS, 2 * ROWS, 128),
            tile(PAIRS, 128, 2 * ROWS),
            tile(PAIRS, 2 * ROWS, 4 * ROWS, dtype=F32),
            tile(PAIRS, 2 * ROWS, 4 * ROWS),
            tile(PAIRS, 2 * ROWS, 4 * ROWS),
            tile(PAIRS, 2 * ROWS, 7 * ROWS, dtype=F32),
            tile(2, PAIRS, 2 * ROWS, 128, dtype=F32),
            tile(2, PAIRS, 2 * ROWS, 128, dtype=F32),
            tile(2, PAIRS, 2 * ROWS, 128, dtype=F32),
            tile(2, PAIRS, 2 * ROWS, 128, dtype=F32),
            tile(ROWS, D),
            tile(PAIRS, 2 * ROWS, 128, dtype=F32),
            tile(2, PAIRS, 2 * ROWS, 128, dtype=F32),
            tile(2 * D, 7 * ROWS),
            tile(5, D, ROWS),
            tile(5, D, ROWS),
            pltpu.SMEM((1, 4), jnp.int32),
            pltpu.SMEM((1, 4), jnp.int32),
            tile(2, D, ROWS),
            tile(2, D, ROWS),
            tile(2, 2, DHALF, ROWS),
            tile(2, D, ROWS),
            tile(2, D, ROWS),
            tile(2, 6, DHALF, ROWS),
            tile(D, ROWS),
            tile(D, ROWS),
            tile(D, D),
            tile(FF, D),
            tile(4 * ROWS, D),
            tile(ROWS, FF),
            tile(ROWS, D, dtype=F32),
            tile(ROWS, FF, dtype=F32),
            pltpu.SemaphoreType.DMA((10,)),
            pltpu.SemaphoreType.REGULAR((2,)),
            pltpu.SemaphoreType.DMA((19,)),
            pltpu.SemaphoreType.DMA((25,)),
            pltpu.SemaphoreType.DMA((17,)),
        ],
        compiler_params=pltpu.CompilerParams(
            collective_id=0, has_side_effects=True, vmem_limit_bytes=28 * 1024 * 1024
        ),
        name="exphormer",
    )(
        *(
            pltpu.with_memory_space_constraint(a, pltpu.HBM)
            for a in (nodes, experts_list, w_query, w_key, w_value, w_out, w_up, w_down, cotangent)
        ),
    )
    return (both[:, :width].astype(BF16), both[:, width:].astype(BF16))


def solution(mesh):
    return jax.shard_map(
        on_device,
        mesh=mesh,
        in_specs=(
            P(("blk", "dom"), None),
            P(("blk", "dom"), None),
            P(),
            P(),
            P(),
            P(),
            P(),
            P(),
            P(("blk", "dom"), None),
        ),
        out_specs=(P(("blk", "dom"), None), P(("blk", "dom"), None)),
        check_vma=False,
    )
```

```python
import functools

import jax
import jax.numpy as jnp
from jax import lax
from jax.experimental import pallas as pl
from jax.experimental.pallas import tpu as pltpu
from jax.sharding import PartitionSpec as P

EPS = 1e-05
MESH = pl.DeviceIdType.MESH
D = 512
FF = 1024
ROWS = 128
HALF = 64
DHALF = 256
PAIRS = 4
F32 = jnp.float32
BF16 = jnp.bfloat16


def normalize(values):
    mean_v = jnp.mean(values, axis=-1, keepdims=True)
    centered = values - mean_v
    inv_std = lax.rsqrt(jnp.mean(centered * centered, axis=-1, keepdims=True) + EPS)
    return (centered * inv_std, inv_std)


def normalize_back(unit, inv_std, upstream):
    return inv_std * (
        upstream
        - jnp.mean(upstream, axis=-1, keepdims=True)
        - unit * jnp.mean(upstream * unit, axis=-1, keepdims=True)
    )


def dot(a, b):
    return jnp.dot(a, b, preferred_element_type=F32)


def dot_t(a, b):
    return lax.dot_general(a, b, (((1,), (1,)), ((), ())), preferred_element_type=F32)


def head_stack(tile):
    low = lax.broadcasted_iota(jnp.int32, tile.shape, 1) < 64
    zero = jnp.zeros_like(tile)
    return jnp.concatenate([jnp.where(low, tile, zero), jnp.where(low, zero, tile)], 0)


def head_join(stacked):
    low = lax.broadcasted_iota(jnp.int32, (ROWS, 128), 1) < 64
    return jnp.where(low, stacked[:ROWS], stacked[ROWS:])


def kernel(
    nodes_hbm,
    list_hbm,
    wq_hbm,
    wk_hbm,
    wv_hbm,
    wo_hbm,
    wu_hbm,
    wd_hbm,
    cot_hbm,
    both_out,
    xv,
    cotv,
    wq,
    wkv,
    wo,
    wu,
    wd,
    gath,
    halo,
    kv,
    q2,
    q2t,
    g2,
    g2t,
    dpv,
    pbv,
    dsv,
    wexp,
    mstat,
    lstat,
    oacc,
    fstat,
    mixv,
    delt,
    dq,
    dt,
    part,
    psib,
    listed,
    lsib,
    hsend,
    hrecv,
    xo,
    yl,
    yr,
    sbuf,
    tbuf,
    ybuf,
    wot,
    wut,
    nbuf,
    actv,
    residv,
    gact,
    lsem,
    ready,
    ssem,
    grecv,
    rrecv,
):
    blk = lax.axis_index("blk")
    dom = lax.axis_index("dom")
    ndom = lax.axis_size("dom")
    core = blk % 2
    x = (blk // 2) % 4
    h = blk // 8

    def at(xx, hh, cc):
        return hh * 8 + (xx % 4) * 2 + cc

    right = {"blk": at(x + 1, h, core), "dom": dom}
    left = {"blk": at(x + 3, h, core), "dom": dom}
    across = {"blk": at(x, 1 - h, core), "dom": dom}
    twin = {"blk": at(x, h, 1 - core), "dom": dom}
    up = {"blk": blk, "dom": (dom + 1) % ndom}
    down = {"blk": blk, "dom": (dom + ndom - 1) % ndom}

    half = ndom // 2
    z = dom % half
    final = half - 1

    barrier = pltpu.get_barrier_semaphore()

    def greet(peer):
        pl.semaphore_signal(barrier, inc=1, device_id=peer, device_id_type=MESH)

    greet(across)

    @pl.when(z < final)
    def _():
        greet(up)

    @pl.when(z == 0)
    def _():
        greet(down)

    for peer in (right, left, twin):
        greet(peer)

    pl.semaphore_wait(barrier, 4 + jnp.where(z > 0, 1, 0) + jnp.where(z == final, 1, 0))

    @pl.when(z > 0)
    def _():
        pl.semaphore_signal(ready.at[0], inc=1, device_id=down, device_id_type=MESH)

    @pl.when(z == final)
    def _():
        pl.semaphore_signal(ready.at[1], inc=1, device_id=up, device_id_type=MESH)

    sends = []

    pool = list(range(20))

    def plan(src, dst, rsems, slot, peer):
        index = pool.pop(0)
        copy = pltpu.make_async_remote_copy(
            src_ref=src,
            dst_ref=dst,
            send_sem=ssem.at[index],
            recv_sem=rsems.at[slot],
            device_id=peer,
            device_id_type=MESH,
        )
        sends.append((copy, index))
        return copy

    def reclaim(keep=()):
        held = [entry for entry in sends if any(entry[0] is copy for copy in keep)]
        for copy, index in sends:
            if not any(copy is entry[0] for entry in held):
                copy.wait_send()
                pool.append(index)
        sends[:] = held

    def push(*where):
        copy = plan(*where)
        copy.start()
        return copy

    top = pl.ds(0, HALF)
    bottom = pl.ds(HALF, HALF)

    def block(xx, rr):
        return at(xx, rr, core)

    rows_of = (h, 1 - h)

    own = block(x, h)
    c_r = {}
    c_l = {}
    c_y = []
    c_y.append(push(nodes_hbm.at[top], gath.at[own, top], grecv, 12, across))
    c_r[0, 0] = push(nodes_hbm.at[top], gath.at[own, top], grecv, 0, right)
    c_l[0, 1] = push(nodes_hbm.at[bottom], gath.at[own, bottom], grecv, 5, left)
    c_y.append(push(nodes_hbm.at[bottom], gath.at[own, bottom], grecv, 13, across))

    loads = []

    def load(src, dst):
        copy = pltpu.make_async_copy(src, dst, lsem.at[len(loads)])
        copy.start()
        loads.append(copy)
        return copy

    ld_x = load(nodes_hbm, xv)
    ld_wk = load(wk_hbm, wkv.at[:, pl.ds(0, D)])
    ld_wv = load(wv_hbm, wkv.at[:, pl.ds(D, D)])
    ld_wq = load(wq_hbm, wq)
    ld_own = load(nodes_hbm, gath.at[own])
    ld_list = load(list_hbm, listed)
    ld_cot = load(cot_hbm, cotv)
    ld_wd = load(wd_hbm, wd)
    ld_wo = load(wo_hbm, wo)
    ld_wu = load(wu_hbm, wu)

    c_list = push(list_hbm, lsib, grecv, 24, twin)
    c_tw = [push(nodes_hbm, gath.at[own], grecv, 16, twin)]

    ld_x.wait()
    x_full = xv[...].astype(F32)
    unit, inv_std = normalize(x_full)
    normed = unit.astype(BF16)
    ld_wk.wait()
    ld_wv.wait()
    kv[pl.ds(2 * ROWS, ROWS), :] = dot(normed, wkv[...]).astype(BF16)
    ld_wq.wait()
    queries = dot(normed, wq[...]).astype(BF16) * jnp.asarray(0.125, BF16)
    for hp in range(PAIRS):
        stacked = head_stack(queries[:, hp * 128 : (hp + 1) * 128])
        q2[hp] = stacked
        q2t[hp] = jnp.transpose(stacked)

    fwd_r = [None, None]
    fwd_l = [None, None]

    def forward(rr):
        row = rows_of[rr]
        c_r[rr, 0].wait_recv()
        from_left = block(x + 3, row)
        fwd_r[rr] = push(gath.at[from_left, top], gath.at[from_left, top], grecv, 8 + rr, right)
        c_l[rr, 1].wait_recv()
        from_right = block(x + 1, row)
        fwd_l[rr] = push(
            gath.at[from_right, bottom], gath.at[from_right, bottom], grecv, 10 + rr, left
        )

    def to_twin(slot, who):
        c_tw.append(push(gath.at[who], gath.at[who], grecv, slot, twin))

    c_r[0, 1] = push(nodes_hbm.at[bottom], gath.at[own, bottom], grecv, 1, right)
    c_l[0, 0] = push(nodes_hbm.at[top], gath.at[own, top], grecv, 4, left)
    c_up = plan(nodes_hbm, halo.at[0], grecv, 14, up)
    c_dn = plan(nodes_hbm, halo.at[1], grecv, 15, down)

    @pl.when(z > 0)
    def _():
        c_dn.start()

    @pl.when(z == final)
    def _():
        c_up.start()

    ld_wd.wait()
    ld_cot.wait()
    gact[...] = dot_t(cotv[...], wd[...])
    forward(0)
    other = block(x, 1 - h)
    c_y[0].wait_recv()
    c_r[1, 0] = push(gath.at[other, top], gath.at[other, top], grecv, 2, right)
    c_y[1].wait_recv()
    c_l[1, 1] = push(gath.at[other, bottom], gath.at[other, bottom], grecv, 7, left)
    c_l[1, 0] = push(gath.at[other, top], gath.at[other, top], grecv, 6, left)
    c_r[1, 1] = push(gath.at[other, bottom], gath.at[other, bottom], grecv, 3, right)
    to_twin(17, other)

    @pl.when(z < final)
    def _():
        pl.semaphore_wait(ready.at[0], 1)
        c_up.start()


    def project(raw, row0):
        unit_o, _ = normalize(raw.astype(F32))
        kv[pl.ds(row0, ROWS), :] = dot(unit_o.astype(BF16), wkv[...]).astype(BF16)

    def attend(base, count, which, pairs=range(PAIRS)):
        for hp in pairs:
            k = kv[base : base + count, hp * 128 : (hp + 1) * 128]
            wexp[hp, :, base : base + count] = dot_t(q2[hp], k)
        for hp in pairs:
            s = wexp[hp, :, base : base + count]
            m = jnp.max(s, axis=1, keepdims=True)
            w = jnp.exp(s - m)
            wexp[hp, :, base : base + count] = w
            total = jnp.sum(w, axis=1, keepdims=True)
            mstat[which, hp] = jnp.broadcast_to(m, (2 * ROWS, 128))
            lstat[which, hp] = jnp.broadcast_to(total, (2 * ROWS, 128))
        for hp in pairs:
            v = kv[base : base + count, D + hp * 128 : D + (hp + 1) * 128]
            oacc[which, hp] = dot(wexp[hp, :, base : base + count].astype(BF16), v)

    ld_wo.wait()
    ld_wu.wait()
    wot[...] = jnp.transpose(wo[...])
    wut[...] = jnp.transpose(wu[...])
    reclaim([copy for copy, _ in sends[8:]])
    forward(1)
    c_r[0, 1].wait_recv()
    to_twin(18, block(x + 3, h))
    c_l[0, 0].wait_recv()
    to_twin(19, block(x + 1, h))
    fwd_r[0].wait_recv()
    fwd_l[0].wait_recv()
    to_twin(22, block(x + 2, h))
    @pl.when(z == 0)
    def _():
        pl.semaphore_wait(ready.at[1], 1)
        c_dn.start()

    c_r[1, 1].wait_recv()
    to_twin(20, block(x + 3, 1 - h))
    c_l[1, 0].wait_recv()
    to_twin(21, block(x + 1, 1 - h))
    fwd_r[1].wait_recv()
    fwd_l[1].wait_recv()
    to_twin(23, block(x + 2, 1 - h))
    c_up.wait_recv()
    project(halo[0], 0)
    c_dn.wait_recv()
    project(halo[1], ROWS)
    attend(0, 3 * ROWS, 0)
    for copy in c_tw:
        copy.wait_recv()
    c_list.wait_recv()
    ld_own.wait()
    ld_list.wait()

    for e in range(4):
        unit_e, _ = normalize(gath[listed[0, e]].astype(F32))
        nbuf[e * ROWS : (e + 1) * ROWS] = unit_e.astype(BF16)
    kv[3 * ROWS : 7 * ROWS, :] = dot(nbuf[...], wkv[...]).astype(BF16)
    attend(3 * ROWS, 4 * ROWS, 1)

    for hp in range(PAIRS):
        m0, m1 = mstat[0, hp], mstat[1, hp]
        m = jnp.maximum(m0, m1)
        a0, a1 = jnp.exp(m0 - m), jnp.exp(m1 - m)
        inv = 1.0 / (a0 * lstat[0, hp] + a1 * lstat[1, hp])
        f0, f1 = a0 * inv, a1 * inv
        fstat[0, hp] = f0
        fstat[1, hp] = f1
        o = oacc[0, hp] * f0 + oacc[1, hp] * f1
        mixv[:, hp * 128 : (hp + 1) * 128] = head_join(o).astype(BF16)

    mixed = mixv[...]
    resid = xv[...].astype(F32) + dot(mixed, wo[...])
    unit2, inv_std2 = normalize(resid)
    pre = dot(unit2.astype(BF16), wu[...])
    cot = cotv[...]
    c0 = 0.7978845608028654
    sq = pre * pre
    th = jnp.tanh(c0 * (pre + 0.044715 * (sq * pre)))
    act = 0.5 * pre * (1.0 + th)
    slope = 0.5 * (1.0 + th) + 0.5 * pre * (1.0 - th * th) * (c0 * (1.0 + 3.0 * 0.044715 * sq))
    actv[...] = act.astype(BF16)
    residv[...] = resid
    grad_pre = (gact[...] * slope).astype(BF16)
    grad_norm2 = dot(grad_pre, wut[...])
    grad_resid = cot.astype(F32) + normalize_back(unit2, inv_std2, grad_norm2)
    grad_mixed = dot(grad_resid.astype(BF16), wot[...]).astype(BF16)
    for hp in range(PAIRS):
        stacked = head_stack(grad_mixed[:, hp * 128 : (hp + 1) * 128])
        g2[hp] = stacked
        g2t[hp] = jnp.transpose(stacked)
        mixed_pair = mixed[:, hp * 128 : (hp + 1) * 128].astype(F32)
        both = jnp.concatenate([mixed_pair, mixed_pair], 0)
        d = jnp.sum(stacked.astype(F32) * both, axis=1, keepdims=True)
        delt[hp] = jnp.broadcast_to(d, (2 * ROWS, 128))

    def attend_back(base, count, which):
        tiles = count // 128
        for hp in range(PAIRS):
            v = kv[base : base + count, D + hp * 128 : D + (hp + 1) * 128]
            dpv[hp, :, :count] = dot_t(g2[hp], v)
        for hp in range(PAIRS):
            scale = jnp.concatenate([fstat[which, hp]] * tiles, 1)
            shift = jnp.concatenate([delt[hp]] * tiles, 1)
            p = wexp[hp, :, base : base + count] * scale
            pbv[hp, :, :count] = p.astype(BF16)
            dsv[hp, :, :count] = (p * (dpv[hp, :, :count] - shift)).astype(BF16)
        for hp in range(PAIRS):
            dt[D + hp * 128 : D + (hp + 1) * 128, base : base + count] = dot(
                g2t[hp], pbv[hp, :, :count]
            ).astype(BF16)
            dt[hp * 128 : (hp + 1) * 128, base : base + count] = dot(
                q2t[hp], dsv[hp, :, :count]
            ).astype(BF16)
            k = kv[base : base + count, hp * 128 : (hp + 1) * 128]
            dq[which, hp] = dot(dsv[hp, :, :count], k)

    attend_back(3 * ROWS, 4 * ROWS, 1)

    reclaim((c_up, c_dn))
    zero_block = jnp.zeros((D, ROWS), BF16)
    part[4] = zero_block
    psib[4] = zero_block
    c_ps = []
    da = pl.ds(0, DHALF)
    db = pl.ds(DHALF, DHALF)
    first4 = pl.ds(0, 4)
    for i, cols in enumerate((da, db)):
        every = dot(wkv[cols, :], dt[:, 3 * ROWS : 7 * ROWS]).astype(BF16)
        for e in range(4):
            part[e, cols, :] = every[:, e * ROWS : (e + 1) * ROWS]
        c_ps.append(
            push(part.at[first4, cols], psib.at[first4, cols], rrecv, i, twin)
        )

    attend_back(0, 3 * ROWS, 0)
    halves_t = dot(wkv[...], dt[:, 0 : 2 * ROWS]).astype(BF16)
    hsend[0] = halves_t[:, :ROWS]
    hsend[1] = halves_t[:, ROWS:]
    c_hd = push(hsend.at[0], hrecv.at[0], rrecv, 2, down)
    c_hu = push(hsend.at[1], hrecv.at[1], rrecv, 3, up)
    for copy in c_ps:
        copy.wait_recv()

    def slot_of(lists, target):
        slot = jnp.int32(4)
        for e in range(4):
            slot = jnp.where(lists[0, e] == target, jnp.int32(e), slot)
        return slot

    def summed(xx, rr, cols):
        target = block(xx, rows_of[rr])
        return (
            part[slot_of(listed, target), cols, :].astype(F32)
            + psib[slot_of(lsib, target), cols, :].astype(F32)
        )

    c_x = {}

    def opposite_step(rr):
        s0 = 5 + 6 * rr
        sbuf[rr, 0] = summed(x + 2, rr, da).astype(BF16)
        c_x[rr, 0] = push(sbuf.at[rr, 0], xo.at[rr, 0], rrecv, s0, right)
        sbuf[rr, 1] = summed(x + 2, rr, db).astype(BF16)
        c_x[rr, 1] = push(sbuf.at[rr, 1], xo.at[rr, 1], rrecv, s0 + 1, left)

    def direct_step(rr):
        s0 = 5 + 6 * rr
        sbuf[rr, 2] = summed(x + 1, rr, db).astype(BF16)
        c_x[rr, 2] = push(sbuf.at[rr, 2], yl.at[rr, db], rrecv, s0 + 2, right)
        sbuf[rr, 3] = summed(x + 3, rr, da).astype(BF16)
        c_x[rr, 3] = push(sbuf.at[rr, 3], yr.at[rr, da], rrecv, s0 + 3, left)

    def second_step(rr):
        s0 = 5 + 6 * rr
        c_x[rr, 0].wait_recv()
        sbuf[rr, 4] = (summed(x + 1, rr, da) + xo[rr, 0].astype(F32)).astype(BF16)
        c_x[rr, 4] = push(sbuf.at[rr, 4], yl.at[rr, da], rrecv, s0 + 4, right)
        c_x[rr, 1].wait_recv()
        sbuf[rr, 5] = (summed(x + 3, rr, db) + xo[rr, 1].astype(F32)).astype(BF16)
        c_x[rr, 5] = push(sbuf.at[rr, 5], yr.at[rr, db], rrecv, s0 + 5, left)

    opposite_step(1)
    own_t = dot(wkv[...], dt[:, 2 * ROWS : 3 * ROWS])
    grad_q = jnp.concatenate([head_join(dq[0, hp] + dq[1, hp]) for hp in range(PAIRS)], 1)
    grad_in = dot_t((grad_q * 0.125).astype(BF16), wq[...])
    both_out[:, 0:D] = residv[...] + dot(actv[...], wd[...])
    direct_step(1)
    second_step(1)
    opposite_step(0)
    direct_step(0)

    c_t = []
    for cols, slots, place in ((da, (3, 4), 4), (db, (2, 5), 17)):
        for slot in slots:
            c_x[1, slot].wait_recv()
        tbuf[cols] = (
            summed(x, 1, cols) + yl[1, cols, :].astype(F32) + yr[1, cols, :].astype(F32)
        ).astype(BF16)
        c_t.append(push(tbuf.at[cols], ybuf.at[cols], rrecv, place, across))
    second_step(0)
    c_hd.wait_recv()
    c_hu.wait_recv()
    own_t = own_t + hrecv[0].astype(F32) + hrecv[1].astype(F32)
    for slot in (2, 3, 4, 5):
        c_x[0, slot].wait_recv()
    own_t = own_t + yl[0].astype(F32) + yr[0].astype(F32)
    own_t = own_t + jnp.concatenate([summed(x, 0, da), summed(x, 0, db)], 0)
    grad_in = grad_in + jnp.transpose(own_t)
    unit_b, inv_b = normalize(xv[...].astype(F32))
    for copy in c_t:
        copy.wait_recv()
    grad_in = grad_in + jnp.transpose(ybuf[...].astype(F32))
    both_out[:, D : 2 * D] = grad_resid + normalize_back(unit_b, inv_b, grad_in)
    reclaim()


def on_device(nodes, experts_list, w_query, w_key, w_value, w_out, w_up, w_down, cotangent):
    rows, width = nodes.shape
    hbm = pl.BlockSpec(memory_space=pltpu.HBM)
    tile = lambda *shape, dtype=BF16: pltpu.VMEM(shape, dtype)
    out = jax.ShapeDtypeStruct((rows, width), BF16)
    vm = pl.BlockSpec(memory_space=pltpu.VMEM)
    both = pl.pallas_call(
        kernel,
        out_shape=jax.ShapeDtypeStruct((rows, 2 * width), F32),
        in_specs=[hbm] * 9,
        out_specs=vm,
        scratch_shapes=[
            tile(ROWS, D),
            tile(ROWS, D),
            tile(D, D),
            tile(D, 2 * D),
            tile(D, D),
            tile(D, FF),
            tile(FF, D),
            tile(16, ROWS, D),
            tile(2, ROWS, D),
            tile(7 * ROWS, 2 * D),
            tile(PAIRS, 2 * ROWS, 128),
            tile(PAIRS, 128, 2 * ROWS),
            tile(PAIRS, 2 * ROWS, 128),
            tile(PAIRS, 128, 2 * ROWS),
            tile(PAIRS, 2 * ROWS, 4 * ROWS, dtype=F32),
            tile(PAIRS, 2 * ROWS, 4 * ROWS),
            tile(PAIRS, 2 * ROWS, 4 * ROWS),
            tile(PAIRS, 2 * ROWS, 7 * ROWS, dtype=F32),
            tile(2, PAIRS, 2 * ROWS, 128, dtype=F32),
            tile(2, PAIRS, 2 * ROWS, 128, dtype=F32),
            tile(2, PAIRS, 2 * ROWS, 128, dtype=F32),
            tile(2, PAIRS, 2 * ROWS, 128, dtype=F32),
            tile(ROWS, D),
            tile(PAIRS, 2 * ROWS, 128, dtype=F32),
            tile(2, PAIRS, 2 * ROWS, 128, dtype=F32),
            tile(2 * D, 7 * ROWS),
            tile(5, D, ROWS),
            tile(5, D, ROWS),
            pltpu.SMEM((1, 4), jnp.int32),
            pltpu.SMEM((1, 4), jnp.int32),
            tile(2, D, ROWS),
            tile(2, D, ROWS),
            tile(2, 2, DHALF, ROWS),
            tile(2, D, ROWS),
            tile(2, D, ROWS),
            tile(2, 6, DHALF, ROWS),
            tile(D, ROWS),
            tile(D, ROWS),
            tile(D, D),
            tile(FF, D),
            tile(4 * ROWS, D),
            tile(ROWS, FF),
            tile(ROWS, D, dtype=F32),
            tile(ROWS, FF, dtype=F32),
            pltpu.SemaphoreType.DMA((10,)),
            pltpu.SemaphoreType.REGULAR((2,)),
            pltpu.SemaphoreType.DMA((20,)),
            pltpu.SemaphoreType.DMA((25,)),
            pltpu.SemaphoreType.DMA((18,)),
        ],
        compiler_params=pltpu.CompilerParams(
            collective_id=0, has_side_effects=True, vmem_limit_bytes=28 * 1024 * 1024
        ),
        name="exphormer",
    )(
        *(
            pltpu.with_memory_space_constraint(a, pltpu.HBM)
            for a in (nodes, experts_list, w_query, w_key, w_value, w_out, w_up, w_down, cotangent)
        ),
    )
    return (both[:, :width].astype(BF16), both[:, width:].astype(BF16))


def solution(mesh):
    return jax.shard_map(
        on_device,
        mesh=mesh,
        in_specs=(
            P(("blk", "dom"), None),
            P(("blk", "dom"), None),
            P(),
            P(),
            P(),
            P(),
            P(),
            P(),
            P(("blk", "dom"), None),
        ),
        out_specs=(P(("blk", "dom"), None), P(("blk", "dom"), None)),
        check_vma=False,
    )
```
